32 devices in a mesh: dp: 4 (over z), ctx: 4 (over y, x), tensor: 2 (over core).
Axes of the slice: x: 2, y: 2, z: 4, core: 2. Of those that a mesh axis runs over, the one named last changes fastest.
Arguments:
- tokens: bfloat16 [4096, 1024], P(('dp', 'ctx')), may hold values from -6 to 6
- doc_lengths: int32 [4, 8], P('dp'), may hold values from 1 to 512, 1024 in all within a row
- gain_attn: bfloat16 [1024], P('dp'), may hold values from 0.5 to 1.5
- w_qkv: bfloat16 [3, 1024, 1024], P(None, 'dp', 'tensor'), may hold values from -0.1875 to 0.1875
- w_attn_out: bfloat16 [1024, 1024], P('tensor', 'dp'), may hold values from -0.5 to 0.5
- gain_mlp: bfloat16 [1024], P('dp'), may hold values from 0.5 to 1.5
- w_in: bfloat16 [2, 1024, 2624], P(None, 'dp', 'tensor'), may hold values from -0.1875 to 0.1875
- w_mlp_out: bfloat16 [2624, 1024], P('tensor', 'dp'), may hold values from -0.125 to 0.125
- cotangent: bfloat16 [4096, 1024], P(('dp', 'ctx')), may hold values from -6 to 6
Outputs:
- out_tokens: bfloat16 [4096, 1024], P(('dp', 'ctx'))
- grad_tokens: float32 [4096, 1024], P(('dp', 'ctx'))
- grad_gain_attn: float32 [1024], P('dp')
- grad_w_qkv: float32 [3, 1024, 1024], P(None, 'dp', 'tensor')
- grad_w_attn_out: float32 [1024, 1024], P('tensor', 'dp')
- grad_gain_mlp: float32 [1024], P('dp')
- grad_w_in: float32 [2, 1024, 2624], P(None, 'dp', 'tensor')
- grad_w_mlp_out: float32 [2624, 1024], P('tensor', 'dp')
The draws below stay inside these ranges and needn't reach their ends.
Inputs may be any that keep to these rules, and one draw needn't show every extreme that they name: `doc_lengths`: each row sums to 1024, and the longest document of each row has exactly half of 1024 tokens.
All inputs are finite; a program needn't handle non-finite values.
Results may differ from the reference program's by a relative error of at most 0.013.
Values may be sent and summed in bfloat16 or wider, within the bound.
A program may use at most 128 MiB of HBM per device.

```python
import math
import jax
import jax.numpy as jnp
import numpy as np
from jax import lax

D = 1024
HD = 64
FF = 2624
DOCS = 8
TOK_DEV = 256
SPAN = 1024
SPANS = 4
TOKENS = 4096
N_CTX = 4


def draw_tokens(key, part):
    values = jnp.clip(jax.random.normal(jax.random.fold_in(key, 11), (TOKENS, D), jnp.float32), -6.0, 6.0)
    return values.astype(jnp.bfloat16)


def draw_w_qkv(key, part):
    spread = D ** (-0.5)
    values = jnp.clip(jax.random.normal(jax.random.fold_in(key, 21), (3, D, D), jnp.float32), -6.0, 6.0) * spread
    return values.astype(jnp.bfloat16)


def block_scale(key, extent, cuts, low, top_value):
    level = 1.0
    for dim, shards_of in cuts:
        draws = jax.random.uniform(jax.random.fold_in(jax.random.fold_in(key, 6), dim), (shards_of,), jnp.float32, low / len(cuts), top_value / len(cuts))
        level = level * jnp.repeat(jnp.exp(draws), extent[dim] // shards_of).reshape((-1,) + (1,) * (len(extent) - 1 - dim))
    return level


def split_up(count, total, most, lean):
    loads = [(1 << 20) // math.isqrt(grade ** lean) + 1 for grade in range(2, count + 1)]
    rest, counts = total - most - (count - 1), [1] * (count - 1)
    while rest > 0:
        candidates = [i for i in range(count - 1) if counts[i] < most]
        pool, left = sum([loads[i] for i in candidates]), rest
        for i in candidates:
            extra = min(most - counts[i], max(1, left * loads[i] // pool), rest)
            counts[i] = counts[i] + extra
            rest = rest - extra
    return np.array([most] + counts)


def uneven_parts(key, number_of, total, most, skew):
    if number_of == 2:
        one = jax.random.randint(key, (), max(1, total - most), min(most, total - 1) + 1)
        return jnp.stack([one, total - one])
    sizes = jnp.asarray(split_up(number_of, total, most, skew), jnp.int32)
    pairs = (number_of - 1) // 2
    source_of, sink = sizes[1:1 + 2 * pairs:2], sizes[2:2 + 2 * pairs:2]
    room = jnp.minimum(source_of - 1, most - sink)
    shifted = jax.random.randint(jax.random.fold_in(key, 1), (pairs,), 0, 1 << 20) % (room + 1)
    sizes = sizes.at[1:1 + 2 * pairs:2].set(source_of - shifted).at[2:2 + 2 * pairs:2].set(sink + shifted)
    return sizes[jax.random.permutation(jax.random.fold_in(key, 2), number_of)]


def centred(key, dims, scale, bound, cuts=(), kind=jnp.bfloat16):
    values = jax.random.normal(key, dims, jnp.float32) * scale
    if len(cuts) > 0:
        values = block_scale(key, dims, cuts, -0.22, 0.18) * values
    return jnp.clip(values, min=-bound, max=bound).astype(kind)


def setup_inputs(seed: int = 0) -> dict:
    splits = jax.random.split(jax.random.key(seed), 10)
    return {
        "tokens": draw_tokens(jax.random.fold_in(splits[9], 71), 0),
        "doc_lengths": jax.vmap(lambda own: uneven_parts(own, DOCS, SPAN, SPAN // 2, 2))(jax.random.split(splits[1], SPANS)).reshape((SPANS, DOCS)).astype(jnp.int32),
        "gain_attn": jnp.clip(1.0 + 0.1 * jax.random.normal(splits[2], (D,), jnp.float32), 0.5, 1.5).astype(jnp.bfloat16),
        "w_qkv": draw_w_qkv(jax.random.fold_in(splits[9], 71), 0),
        "w_attn_out": centred(splits[4], (D, D), (D // 8) ** -0.5, 0.5, ((0, 2), (1, 4))),
        "gain_mlp": jnp.clip(1.0 + 0.1 * jax.random.normal(splits[5], (D,), jnp.float32), 0.5, 1.5).astype(jnp.bfloat16),
        "w_in": centred(splits[6], (2, D, FF), D ** -0.5, 0.1875, ((1, 4), (2, 2))),
        "w_mlp_out": centred(splits[7], (FF, D), FF ** -0.5, 0.125, ((0, 2), (1, 4))),
        "cotangent": centred(splits[8], (TOKENS, D), 1.0, 6.0, ((0, 16),)),
    }


NORM_EPS = 1e-05
ROPE_BASE = 160000.0
MASK_FILL = -1e+30
INV_ROOT_TWO = 1.0 / math.sqrt(2.0)
INV_ROOT_TWO_PI = 1.0 / math.sqrt(2.0 * math.pi)

def norm_forward(x_float, gain_vec):
    row_mean = lax.optimization_barrier(jnp.mean(x_float, axis=-1, keepdims=True))
    centered = x_float - row_mean
    inv_std = lax.rsqrt(lax.optimization_barrier(jnp.mean(centered * centered, axis=-1, keepdims=True)) + NORM_EPS)
    x_hat = centered * inv_std
    normed = (x_hat * gain_vec.astype(jnp.float32)).astype(jnp.bfloat16)
    return (x_hat, inv_std, normed)

def norm_backward(grad_out, x_hat, inv_std, gain_vec):
    grad_hat = grad_out * gain_vec.astype(jnp.float32)
    grad_gain = lax.optimization_barrier(jnp.sum(grad_out * x_hat, axis=0))
    inner_term = grad_hat - lax.optimization_barrier(jnp.mean(grad_hat, axis=-1, keepdims=True)) - x_hat * lax.optimization_barrier(jnp.mean(grad_hat * x_hat, axis=-1, keepdims=True))
    return (inv_std * inner_term, grad_gain)

def rope_tables(doc_len, span_len, head_width):
    doc_len = doc_len.astype(jnp.int32)
    doc_end = jnp.cumsum(doc_len).astype(jnp.int32)
    doc_start = doc_end - doc_len
    places = jnp.arange(span_len, dtype=jnp.int32)
    inside = places[:, None] >= doc_start[None, :]
    begins = lax.optimization_barrier(jnp.max(jnp.where(inside, doc_start[None, :], 0), axis=1)).astype(jnp.int32)
    segment = lax.optimization_barrier(jnp.sum((places[:, None] >= doc_end[None, :]).astype(jnp.int32), axis=1)).astype(jnp.int32)
    offset = (places - begins).astype(jnp.float32)
    half_width = head_width // 2
    frequency = ROPE_BASE ** (-(jnp.arange(half_width, dtype=jnp.float32) * (2.0 / head_width)))
    angles = offset[:, None] * frequency[None, :]
    angles = jnp.concatenate([angles, angles], axis=1)
    return (jnp.cos(angles), jnp.sin(angles), segment)

def rotate(values_in, cosines, sines):
    half_width = values_in.shape[-1] // 2
    turned = jnp.concatenate([-values_in[..., half_width:], values_in[..., :half_width]], axis=-1)
    return values_in * cosines[:, None, :] + turned * sines[:, None, :]

def rotate_back(grads_in, cosines, sines):
    half_width = grads_in.shape[-1] // 2
    scaled = grads_in * sines[:, None, :]
    turned = jnp.concatenate([scaled[..., half_width:], -scaled[..., :half_width]], axis=-1)
    return grads_in * cosines[:, None, :] + turned

def masked_scores(query_blk, keys_all, same_doc):
    score_scale = query_blk.shape[-1] ** (-0.5)
    scores = jnp.einsum('bhe,che->hbc', query_blk.astype(jnp.float32), keys_all.astype(jnp.float32)) * score_scale
    return jnp.where(same_doc[None, :, :], scores, MASK_FILL)

def attend_rows(query_blk, keys_all, vals_all, same_doc):
    scores = masked_scores(query_blk, keys_all, same_doc)
    row_max = lax.optimization_barrier(jnp.max(scores, axis=-1, keepdims=True))
    expo_vals = jnp.exp(scores - row_max)
    row_total = lax.optimization_barrier(jnp.sum(expo_vals, axis=-1, keepdims=True))
    prob_b = (expo_vals / row_total).astype(jnp.bfloat16)
    out_rows = jnp.einsum('hbc,che->bhe', prob_b.astype(jnp.float32), vals_all.astype(jnp.float32))
    log_total = (row_max + jnp.log(row_total))[:, :, 0]
    return (out_rows.astype(jnp.bfloat16), log_total)

def attend_rows_back(query_blk, out_blk, grad_blk, log_blk, keys_all, vals_all, same_doc):
    score_scale = query_blk.shape[-1] ** (-0.5)
    scores = masked_scores(query_blk, keys_all, same_doc)
    probs = jnp.exp(scores - log_blk[:, :, None])
    prob_b = probs.astype(jnp.bfloat16)
    grad_f = grad_blk.astype(jnp.float32)
    grad_vals = jnp.einsum('hbc,bhe->che', prob_b.astype(jnp.float32), grad_f)
    grad_prob = jnp.einsum('bhe,che->hbc', grad_f, vals_all.astype(jnp.float32))
    delta_row = lax.optimization_barrier(jnp.sum(grad_f * out_blk.astype(jnp.float32), axis=-1)).T
    grad_score = (probs * (grad_prob - delta_row[:, :, None]) * score_scale).astype(jnp.bfloat16)
    grad_query = jnp.einsum('hbc,che->bhe', grad_score.astype(jnp.float32), keys_all.astype(jnp.float32))
    grad_keys = jnp.einsum('hbc,bhe->che', grad_score.astype(jnp.float32), query_blk.astype(jnp.float32))
    return (grad_query, grad_keys, grad_vals)

def attention_forward(query_rot, keys_all, vals_all, segment):
    row_count, head_count, head_width = query_rot.shape
    block_rows = min(512, row_count)
    block_count = row_count // block_rows
    query_blocks = query_rot.reshape(block_count, block_rows, head_count, head_width)
    seg_blocks = segment.reshape(block_count, block_rows)

    def one_block(block_args):
        query_blk, seg_blk = block_args
        same_doc = seg_blk[:, None] == segment[None, :]
        return attend_rows(query_blk, keys_all, vals_all, same_doc)
    out_blocks, log_blocks = lax.map(one_block, (query_blocks, seg_blocks))
    return (out_blocks.reshape(row_count, head_count, head_width), log_blocks)

def attention_backward(query_rot, keys_all, vals_all, attn_heads, grad_heads, log_blocks, segment):
    row_count, head_count, head_width = query_rot.shape
    block_rows = min(512, row_count)
    block_count = row_count // block_rows
    shaped = (block_count, block_rows, head_count, head_width)

    def one_block(carry, block_args):
        keys_acc, vals_acc = carry
        query_blk, out_blk, grad_blk, log_blk, seg_blk = block_args
        same_doc = seg_blk[:, None] == segment[None, :]
        grad_query, grad_keys, grad_vals = attend_rows_back(query_blk, out_blk, grad_blk, log_blk, keys_all, vals_all, same_doc)
        return ((keys_acc + grad_keys, vals_acc + grad_vals), grad_query)
    zeros_acc = jnp.zeros((row_count, head_count, head_width), jnp.float32)
    (grad_keys, grad_vals), grad_query = lax.scan(one_block, (zeros_acc, zeros_acc), (query_rot.reshape(shaped), attn_heads.reshape(shaped), grad_heads.reshape(shaped), log_blocks, segment.reshape(block_count, block_rows)))
    return (grad_query.reshape(row_count, head_count, head_width), grad_keys, grad_vals)

def layer_pass(span_tok, span_docs, span_cot, gain_attn, w_qkv, w_attn_out, gain_mlp, w_in, w_mlp_out):
    f32 = jnp.float32
    bf16 = jnp.bfloat16
    span_len, width = span_tok.shape
    head_count = width // HD
    cosines, sines, segment = rope_tables(span_docs, span_len, HD)
    x_float = span_tok.astype(f32)
    hat_one, inv_one, normed_one = norm_forward(x_float, gain_attn)
    projected = jnp.stack([jnp.dot(normed_one, w_qkv[part_idx], preferred_element_type=f32) for part_idx in range(3)]).astype(bf16)
    split_heads = projected.reshape(3, span_len, head_count, HD)
    query_rot = rotate(split_heads[0].astype(f32), cosines, sines).astype(bf16)
    keys_all = rotate(split_heads[1].astype(f32), cosines, sines).astype(bf16)
    vals_all = split_heads[2]
    attn_heads, log_blocks = attention_forward(query_rot, keys_all, vals_all, segment)
    attn_flat = attn_heads.reshape(span_len, width)
    mixed_one = x_float + jnp.dot(attn_flat, w_attn_out, preferred_element_type=f32)
    hat_two, inv_two, normed_two = norm_forward(mixed_one, gain_mlp)
    act_in = jnp.dot(normed_two, w_in[0], preferred_element_type=f32)
    gate_in = jnp.dot(normed_two, w_in[1], preferred_element_type=f32)
    cdf_val = 0.5 * (1.0 + jax.scipy.special.erf(act_in * INV_ROOT_TWO))
    gelu_val = act_in * cdf_val
    hidden = (gelu_val * gate_in).astype(bf16)
    result = (mixed_one + jnp.dot(hidden, w_mlp_out, preferred_element_type=f32)).astype(bf16)
    cot_float = span_cot.astype(f32)
    grad_mlp_out = jnp.dot(hidden.T, span_cot, preferred_element_type=f32)
    grad_hidden = jnp.dot(span_cot, w_mlp_out.T, preferred_element_type=f32)
    gelu_slope = cdf_val + act_in * jnp.exp(-0.5 * act_in * act_in) * INV_ROOT_TWO_PI
    grad_act = (grad_hidden * gate_in * gelu_slope).astype(bf16)
    grad_gate = (grad_hidden * gelu_val).astype(bf16)
    grad_in = jnp.stack([jnp.dot(normed_two.T, grad_act, preferred_element_type=f32), jnp.dot(normed_two.T, grad_gate, preferred_element_type=f32)])
    grad_normed_two = jnp.dot(grad_act, w_in[0].T, preferred_element_type=f32) + jnp.dot(grad_gate, w_in[1].T, preferred_element_type=f32)
    back_two, grad_gain_mlp = norm_backward(grad_normed_two, hat_two, inv_two, gain_mlp)
    grad_mixed = cot_float + back_two
    grad_mixed_b = grad_mixed.astype(bf16)
    grad_attn_out = jnp.dot(attn_flat.T, grad_mixed_b, preferred_element_type=f32)
    grad_heads = jnp.dot(grad_mixed_b, w_attn_out.T, preferred_element_type=f32).astype(bf16).reshape(span_len, head_count, HD)
    grad_query, grad_keys, grad_vals = attention_backward(query_rot, keys_all, vals_all, attn_heads, grad_heads, log_blocks, segment)
    grad_query = rotate_back(grad_query, cosines, sines).astype(bf16)
    grad_keys = rotate_back(grad_keys, cosines, sines).astype(bf16)
    grad_proj = jnp.stack([grad_query, grad_keys, grad_vals.astype(bf16)]).reshape(3, span_len, width)
    grad_qkv = jnp.stack([jnp.dot(normed_one.T, grad_proj[part_idx], preferred_element_type=f32) for part_idx in range(3)])
    grad_normed_one = jnp.dot(grad_proj[0], w_qkv[0].T, preferred_element_type=f32)
    grad_normed_one = grad_normed_one + jnp.dot(grad_proj[1], w_qkv[1].T, preferred_element_type=f32)
    grad_normed_one = grad_normed_one + jnp.dot(grad_proj[2], w_qkv[2].T, preferred_element_type=f32)
    back_one, grad_gain_attn = norm_backward(grad_normed_one, hat_one, inv_one, gain_attn)
    grad_tok = grad_mixed + back_one
    return (result, grad_tok, grad_gain_attn, grad_qkv, grad_attn_out, grad_gain_mlp, grad_in, grad_mlp_out)

def reference(tokens, doc_lengths, gain_attn, w_qkv, w_attn_out, gain_mlp, w_in, w_mlp_out, cotangent):
    span_len = TOK_DEV * N_CTX
    width = tokens.shape[1]

    def span_step(carry, inputs):
        span_tok, span_docs, span_cot = inputs
        outcome = layer_pass(span_tok, span_docs, span_cot, gain_attn, w_qkv, w_attn_out, gain_mlp, w_in, w_mlp_out)
        summed = tuple((held + term for held, term in zip(carry, outcome[2:])))
        return (summed, (outcome[0], outcome[1]))
    start_sums = (jnp.zeros(gain_attn.shape, jnp.float32), jnp.zeros(w_qkv.shape, jnp.float32), jnp.zeros(w_attn_out.shape, jnp.float32), jnp.zeros(gain_mlp.shape, jnp.float32), jnp.zeros(w_in.shape, jnp.float32), jnp.zeros(w_mlp_out.shape, jnp.float32))
    span_count = doc_lengths.shape[0]
    sums, (results, grad_toks) = lax.scan(span_step, start_sums, (tokens.reshape(span_count, span_len, width), doc_lengths, cotangent.reshape(span_count, span_len, width)))
    return (results.reshape(-1, width), grad_toks.reshape(-1, width), sums[0], sums[1], sums[2], sums[3], sums[4], sums[5])
```

```python
import functools
import math

import jax
import jax.numpy as jnp
from jax import lax
from jax.experimental import pallas as pl
from jax.experimental.pallas import tpu as pltpu
from jax.sharding import PartitionSpec as P

HD = 64
LANES = 128
NORM_EPS = 1e-05
ROPE_BASE = 160000.0
MASK_FILL = -1e30
INV_ROOT_TWO = 1.0 / math.sqrt(2.0)
INV_ROOT_TWO_PI = 1.0 / math.sqrt(2.0 * math.pi)
MESH = pl.DeviceIdType.MESH
F32 = jnp.float32
BF16 = jnp.bfloat16

AG_X, AG_COT, AG_N2, AG_GM = range(4)
RS_ATTN, RS_GN2, RS_OUT, RS_GN1 = range(4)
Z_GAIN, Z_WA, Z_WM, Z_GWM, Z_GWA, Z_GG = range(6)


def dot(a, b, ca=1, cb=0):
    return lax.dot_general(a, b, (((ca,), (cb,)), ((), ())), preferred_element_type=F32)


def partner(c, m):
    y = lax.rem(lax.div(c, 2) + m // 2, 2)
    x = lax.rem(lax.rem(c, 2) + m % 2, 2)
    return y * 2 + x


def swap_halves(u):
    lane = lax.broadcasted_iota(jnp.int32, u.shape, 1)
    first = lax.rem(lane, HD) < HD // 2
    return jnp.where(first, pltpu.roll(u, LANES - HD // 2, 1), pltpu.roll(u, HD // 2, 1))


def norm_stats(v):
    centered = v - jnp.mean(v, axis=-1, keepdims=True)
    inv = lax.rsqrt(jnp.mean(centered * centered, axis=-1, keepdims=True) + NORM_EPS)
    return centered * inv, inv


def norm_back(grad, hat, inv, gain):
    gh = grad * gain
    inner = (
        gh
        - jnp.mean(gh, axis=-1, keepdims=True)
        - hat * jnp.mean(gh * hat, axis=-1, keepdims=True)
    )
    return inv * inner, jnp.sum(grad * hat, axis=0, keepdims=True)


def layer_kernel(
    ways,
    x_h, cot_h, wa_h, wm_h, gain_h, cos_r, sin_r, segr_r, segc_r,
    out_o, gtok_o, ga_o, gmo_o, gain_o,
    xall, cotall, n1, n2, gm, gslots, wA, wM, q_s, k_s, v_s, kT, vT, attn, attnT, eT, inv_r,
    acc, sst, srv, pst, prv, hid, gpair, gMst, gMrv, gAst, gArv, gMf, gAf,
    mixed1, gmixed, gproj, gk, gv, gvec, ggst, ggrv,
    ag_ps, ag_pr, ag_ss, ag_sr, rs_ss, rs_sr, rs_ps, rs_pr, z_s, z_r, f_s, f_r, sw_s, sw_r,
    gg_s, gg_r, loc,
):
    Z, N = ways
    z, c, t = lax.axis_index("dp"), lax.axis_index("ctx"), lax.axis_index("tensor")
    o = 1 - t
    R, D = x_h.shape
    H = R // 2
    S = R * N
    Dz = wa_h.shape[0]
    PW = wa_h.shape[1] // 4
    UW = wm_h.shape[1] // 3
    heads = PW // HD

    def rows(cb, half):
        return pl.ds(pl.multiple_of(cb * R + half * H, H), H)

    def block(cb):
        return pl.ds(pl.multiple_of(cb * R, R), R)

    def rcopy(src, dst, ss, rs, dev):
        return pltpu.make_async_remote_copy(
            src_ref=src, dst_ref=dst, send_sem=ss, recv_sem=rs, device_id=dev, device_id_type=MESH
        )

    bar = pltpu.get_barrier_semaphore()
    for m in range(1, N):
        pl.semaphore_signal(bar, inc=1, device_id={"ctx": partner(c, m)}, device_id_type=MESH)
    pl.semaphore_signal(bar, inc=1, device_id={"tensor": o}, device_id_type=MESH)
    for d in range(1, Z):
        pl.semaphore_signal(bar, inc=1, device_id={"dp": lax.rem(z + d, Z)}, device_id_type=MESH)
    pl.semaphore_wait(bar, N - 1 + 1 + Z - 1)

    def ag_peer(kind, buf, m, src=None):
        own = rows(c, t)
        return rcopy(
            buf.at[own] if src is None else src, buf.at[own], ag_ps.at[kind, m], ag_pr.at[kind, m],
            {"ctx": partner(c, m)},
        )

    def ag_sib(kind, buf, m):
        own = rows(partner(c, m), t)
        return rcopy(
            buf.at[own], buf.at[own], ag_ss.at[kind, m], ag_sr.at[kind, m], {"tensor": o}
        )

    def ag_arrive(kind, buf, m):
        there = buf.at[rows(partner(c, m), t)]
        rcopy(there, there, ag_ps.at[kind, m], ag_pr.at[kind, m], {"ctx": partner(c, m)}).wait_recv()
        ag_sib(kind, buf, m).start()

    def ag_sibling_half(kind, buf, m):
        there = buf.at[rows(partner(c, m), o)]
        rcopy(there, there, ag_ss.at[kind, m], ag_sr.at[kind, m], {"tensor": o}).wait_recv()

    def rs_sib(kind, m):
        return rcopy(
            sst.at[kind, m], srv.at[kind, m], rs_ss.at[kind, m], rs_sr.at[kind, m], {"tensor": o}
        )

    def rs_peer(kind, m):
        return rcopy(
            pst.at[kind, m], prv.at[kind, m], rs_ps.at[kind, m], rs_pr.at[kind, m],
            {"ctx": partner(c, m)},
        )

    def rs_begin(kind, m, partial):
        cb = partner(c, m)
        sst[kind, m] = partial(cb, o).astype(BF16)
        rs_sib(kind, m).start()
        acc[m] = partial(cb, t)

    def rs_mid(kind, m):
        rs_sib(kind, m).wait_recv()
        total = acc[m] + srv[kind, m].astype(F32)
        if m == 0:
            acc[0] = total
        else:
            pst[kind, m] = total.astype(BF16)
            rs_peer(kind, m).start()

    def rs_end(kind):
        for m in (1, 2, 3):
            rs_peer(kind, m).wait_recv()
        return (
            acc[0]
            + prv[kind, 1].astype(F32)
            + prv[kind, 2].astype(F32)
            + prv[kind, 3].astype(F32)
        )

    def zrow(i):
        return pl.ds(pl.multiple_of(i * Dz, Dz), Dz)

    def z_copy(kind, d, src, dst):
        return rcopy(
            src, dst, z_s.at[kind, d], z_r.at[kind, d], {"dp": lax.rem(z + d, Z)}
        )

    def z_recv(kind, d, dst):
        rcopy(dst, dst, z_s.at[kind, d], z_r.at[kind, d], {"dp": lax.rem(z + d, Z)}).wait_recv()

    def z_gain(d):
        return z_copy(Z_GAIN, d, gain_h, gslots.at[z])

    def z_wa(d):
        return z_copy(Z_WA, d, wa_h, wA.at[zrow(z)])

    def z_wm(d):
        return z_copy(Z_WM, d, wm_h, wM.at[zrow(z)])

    def z_gwm(d):
        return z_copy(Z_GWM, d, gMst.at[zrow(lax.rem(z + d, Z))], gMrv.at[d])

    def z_gwa(d):
        return z_copy(Z_GWA, d, gAst.at[zrow(lax.rem(z + d, Z))], gArv.at[d])

    x_half = pl.ds(pl.multiple_of(t * H, H), H)
    for m in (1, 2, 3):
        ag_peer(AG_X, xall, m, x_h.at[x_half]).start()
    for d in range(1, Z):
        z_gain(d).start()
    for d in range(1, Z):
        z_wa(d).start()
    local = [
        pltpu.make_async_copy(x_h, xall.at[block(c)], loc.at[0]),
        pltpu.make_async_copy(gain_h, gslots.at[z], loc.at[1]),
        pltpu.make_async_copy(wa_h, wA.at[zrow(z)], loc.at[2]),
        pltpu.make_async_copy(cot_h, cotall.at[block(c)], loc.at[3]),
        pltpu.make_async_copy(wm_h, wM.at[zrow(z)], loc.at[4]),
    ]
    for one in local:
        one.start()
    for d in range(1, Z):
        z_wm(d).start()
    for m in (1, 2, 3):
        ag_peer(AG_COT, cotall, m, cot_h.at[x_half]).start()
    for one in local:
        one.wait()

    for d in range(1, Z):
        z_recv(Z_GAIN, d, gslots.at[lax.rem(z + Z - d, Z)])
    gains = gslots[0].astype(F32)
    for i in range(1, Z):
        gains = gains + gslots[i].astype(F32)
    gvec[...] = gains[0:8]

    def norm_one(cb):
        def body(i, carry):
            r = pl.ds(pl.multiple_of(cb * R + i * 64, 64), 64)
            hat, _ = norm_stats(xall[r, :].astype(F32))
            n1[r, :] = (hat * gvec[0:1, :]).astype(BF16)
            return carry

        lax.fori_loop(0, R // 64, body, 0)

    norm_one(c)
    for m in (1, 2, 3):
        ag_arrive(AG_X, xall, m)
    for m in (1, 2, 3):
        ag_sibling_half(AG_X, xall, m)
        norm_one(partner(c, m))

    for d in range(1, Z):
        z_recv(Z_WA, d, wA.at[zrow(lax.rem(z + Z - d, Z))])

    def project(cb, carry):
        b = block(cb)
        proj = dot(n1[b, :], wA[:, 0 : 3 * PW]).astype(BF16)
        cos, sin = cos_r[b, :], sin_r[b, :]
        qf = proj[:, 0:PW].astype(F32)
        kf = proj[:, PW : 2 * PW].astype(F32)
        q_rot = (qf * cos + swap_halves(qf) * sin).astype(BF16).astype(F32) * (HD**-0.5)
        k_rot = (kf * cos + swap_halves(kf) * sin).astype(BF16)
        val = proj[:, 2 * PW : 3 * PW]
        q_s[b, :] = q_rot.astype(BF16)
        k_s[b, :] = k_rot
        v_s[b, :] = val
        kT[:, b] = k_rot.astype(F32).T.astype(BF16)
        vT[:, b] = val.astype(F32).T.astype(BF16)
        return carry

    lax.fori_loop(0, N, project, 0)

    lane = lax.broadcasted_iota(jnp.int32, (R, PW), 1)

    def only(u, h):
        return jnp.where(lax.div(lane, HD) == h, u, jnp.zeros_like(u))

    def attend(cb):
        b = block(cb)
        same = segc_r[:, 0:1] == segr_r[0:1, b]
        for h in range(heads):
            s = dot(k_s[...], only(q_s[b, :], h), 1, 1)
            s = jnp.where(same, s, MASK_FILL)
            e = jnp.exp(s - jnp.max(s, axis=0, keepdims=True))
            inv = 1.0 / jnp.sum(e, axis=0, keepdims=True)
            eb = e.astype(BF16)
            eT[h, cb] = eb
            inv_r[h : h + 1, b] = inv
            hr = slice(h * HD, (h + 1) * HD)
            attnT[hr, b] = (dot(vT[hr, :], eb) * inv).astype(BF16)
        attn[b, :] = attnT[:, b].astype(F32).T.astype(BF16)

    def part_attn(cb, half):
        return dot(attn[rows(cb, half), :], wA[:, 3 * PW :], 1, 1)

    order = (3, 2, 1, 0)
    for i, m in enumerate(order):
        attend(partner(c, m))
        rs_begin(RS_ATTN, m, part_attn)
        if i:
            rs_mid(RS_ATTN, order[i - 1])
    rs_mid(RS_ATTN, 0)
    for m in (1, 2, 3):
        ag_arrive(AG_COT, cotall, m)
    mixed1[...] = xall[rows(c, t), :].astype(F32) + rs_end(RS_ATTN)

    hat2, inv2 = norm_stats(mixed1[...])
    n2[rows(c, t), :] = (hat2 * gvec[1:2, :]).astype(BF16)
    for m in (1, 2, 3):
        ag_peer(AG_N2, n2, m).start()
    ag_sib(AG_N2, n2, 0).start()
    for d in range(1, Z):
        z_recv(Z_WM, d, wM.at[zrow(lax.rem(z + Z - d, Z))])
    for m in (1, 2, 3):
        ag_sibling_half(AG_COT, cotall, m)

    def mlp(cb):
        b = block(cb)
        pair = dot(n2[b, :], wM[:, 0 : 2 * UW])
        grad_h = dot(cotall[b, :], wM[:, 2 * UW :])
        a, g = pair[:, :UW], pair[:, UW:]
        cdf = 0.5 * (1.0 + lax.erf(a * INV_ROOT_TWO))
        gelu = a * cdf
        hid[b, :] = (gelu * g).astype(BF16)
        slope = cdf + a * jnp.exp(-0.5 * a * a) * INV_ROOT_TWO_PI
        gpair[b, 0:UW] = (grad_h * g * slope).astype(BF16)
        gpair[b, UW:] = (grad_h * gelu).astype(BF16)

    def part_gn2(cb, half):
        return dot(gpair[rows(cb, half), :], wM[:, 0 : 2 * UW], 1, 1)

    def part_out(cb, half):
        return dot(hid[rows(cb, half), :], wM[:, 2 * UW :], 1, 1)

    for i, m in enumerate((0, 1, 2, 3)):
        if m:
            ag_arrive(AG_N2, n2, m)
        ag_sibling_half(AG_N2, n2, m)
        mlp(partner(c, m))
        rs_begin(RS_GN2, m, part_gn2)
        if i:
            rs_mid(RS_GN2, m - 1)
    rs_mid(RS_GN2, 3)

    hat2, inv2 = norm_stats(mixed1[...])
    back2, gg_mlp = norm_back(rs_end(RS_GN2), hat2, inv2, gvec[1:2, :])
    ggst[0, 1:2, :] = gg_mlp
    gmixed[...] = cotall[rows(c, t), :].astype(F32) + back2
    gm[rows(c, t), :] = gmixed[...].astype(BF16)
    for m in (1, 2, 3):
        ag_peer(AG_GM, gm, m).start()
    ag_sib(AG_GM, gm, 0).start()

    CH = 256

    def grads_mlp(i, carry):
        col = pl.ds(pl.multiple_of(i * CH, CH), CH)
        gMst[col, 0 : 2 * UW] = dot(n2[:, col], gpair[...], 0, 0).astype(BF16)
        gMst[col, 2 * UW :] = dot(cotall[:, col], hid[...], 0, 0).astype(BF16)
        return carry

    lax.fori_loop(0, D // CH, grads_mlp, 0)
    for d in range(1, Z):
        z_gwm(d).start()

    gk[...] = jnp.zeros_like(gk)
    gv[...] = jnp.zeros_like(gv)

    def rotate_back(g, b):
        return g * cos_r[b, :] + swap_halves(g * sin_r[b, :])

    def attend_back(cb):
        b = block(cb)
        g = dot(gm[b, :], wA[:, 3 * PW :]).astype(BF16)
        gT = g.astype(F32).T
        scaled = []
        grad_q = []
        for h in range(heads):
            hr = slice(h * HD, (h + 1) * HD)
            inv = inv_r[h : h + 1, b]
            delta = jnp.sum(gT[hr, :] * attnT[hr, b].astype(F32), axis=0, keepdims=True)
            gp = dot(v_s[...], only(g, h), 1, 1)
            ds = (eT[h, cb].astype(F32) * ((gp - delta) * inv)).astype(BF16)
            grad_q.append(dot(kT[hr, :], ds))
            gk[...] += dot(ds, only(q_s[b, :], h))
            scaled.append(gT[hr, :] * inv)
        gs = jnp.concatenate(scaled, axis=0).T.astype(BF16)
        for h in range(heads):
            gv[...] += dot(eT[h, cb], only(gs, h))
        gq = jnp.concatenate(grad_q, axis=0).T * (HD**-0.5)
        gproj[b, 0:PW] = rotate_back(gq, b).astype(BF16)

    for m in (0, 1, 2, 3):
        if m:
            ag_arrive(AG_GM, gm, m)
        ag_sibling_half(AG_GM, gm, m)
        attend_back(partner(c, m))

    def unrotate(cb, carry):
        b = block(cb)
        gproj[b, PW : 2 * PW] = rotate_back(gk[b, :], b).astype(BF16)
        gproj[b, 2 * PW :] = gv[b, :].astype(BF16)
        return carry

    lax.fori_loop(0, N, unrotate, 0)

    def grads_attn(i, carry):
        col = pl.ds(pl.multiple_of(i * CH, CH), CH)
        gAst[col, 0 : 3 * PW] = dot(n1[:, col], gproj[...], 0, 0).astype(BF16)
        gAst[col, 3 * PW :] = dot(gm[:, col], attn[...], 0, 0).astype(BF16)
        return carry

    lax.fori_loop(0, D // CH, grads_attn, 0)
    for d in range(1, Z):
        z_gwa(d).start()

    def part_gn1(cb, half):
        return dot(gproj[rows(cb, half), :], wA[:, 0 : 3 * PW], 1, 1)

    for i, m in enumerate(order):
        rs_begin(RS_GN1, m, part_gn1)
        if i:
            rs_mid(RS_GN1, order[i - 1])
    rs_mid(RS_GN1, 0)

    def fin(kind, m, own, out):
        return rcopy(own, out.at[c], f_s.at[kind, m], f_r.at[kind, m], {"ctx": partner(c, m)})

    total = gMst[zrow(z), :].astype(F32)
    for d in range(1, Z):
        z_recv(Z_GWM, d, gMrv.at[d])
        total = total + gMrv[d].astype(F32)
    gMf[...] = total.astype(BF16)
    for m in (1, 2, 3):
        fin(0, m, gMf, gmo_o).start()
    own_m = pltpu.make_async_copy(gMf, gmo_o.at[c], loc.at[0])
    own_m.start()

    hat1, inv1 = norm_stats(xall[rows(c, t), :].astype(F32))
    back1, gg_attn = norm_back(rs_end(RS_GN1), hat1, inv1, gvec[0:1, :])
    ggst[0, 0:1, :] = gg_attn
    gtok_o[x_half, :] = gmixed[...] + back1
    swap_tok = rcopy(
        gtok_o.at[x_half], gtok_o.at[x_half], sw_s.at[0], sw_r.at[0], {"tensor": o}
    )
    swap_tok.start()

    ggst[0, 2:8, :] = jnp.zeros_like(ggst[0, 2:8, :])
    gg0 = rcopy(ggst.at[0], ggrv.at[0], gg_s.at[0], gg_r.at[0], {"tensor": o})
    gg0.start()

    total = gAst[zrow(z), :].astype(F32)
    for d in range(1, Z):
        z_recv(Z_GWA, d, gArv.at[d])
        total = total + gArv[d].astype(F32)
    gAf[...] = total.astype(BF16)
    for m in (1, 2, 3):
        fin(1, m, gAf, ga_o).start()
    own_a = pltpu.make_async_copy(gAf, ga_o.at[c], loc.at[1])
    own_a.start()

    gg0.wait_recv()
    ggst[1] = ggst[0] + ggrv[0]

    def gg_ctx(m):
        return rcopy(ggst.at[1], ggrv.at[m], gg_s.at[m], gg_r.at[m], {"ctx": partner(c, m)})

    for m in (1, 2, 3):
        gg_ctx(m).start()

    for i, m in enumerate(order):
        rs_begin(RS_OUT, m, part_out)
        if i:
            rs_mid(RS_OUT, order[i - 1])
    rs_mid(RS_OUT, 0)
    for m in (1, 2, 3):
        gg_ctx(m).wait_recv()
    ggst[2] = (ggst[1] + ggrv[1]) + (ggrv[2] + ggrv[3])

    def gg_z(d):
        return z_copy(Z_GG, d, ggst.at[2], ggrv.at[3 + d])

    for d in range(1, Z):
        gg_z(d).start()
    out_o[x_half, :] = (mixed1[...] + rs_end(RS_OUT)).astype(BF16)
    swap_out = rcopy(
        out_o.at[x_half], out_o.at[x_half], sw_s.at[1], sw_r.at[1], {"tensor": o}
    )
    swap_out.start()
    total = ggst[2]
    for d in range(1, Z):
        z_recv(Z_GG, d, ggrv.at[3 + d])
        total = total + ggrv[3 + d]
    gain_o[...] = total

    other = pl.ds(pl.multiple_of(o * H, H), H)
    rcopy(gtok_o.at[other], gtok_o.at[other], sw_s.at[0], sw_r.at[0], {"tensor": o}).wait_recv()
    rcopy(out_o.at[other], out_o.at[other], sw_s.at[1], sw_r.at[1], {"tensor": o}).wait_recv()
    for m in (1, 2, 3):
        for kind, (own, out) in enumerate(((gMf, gmo_o), (gAf, ga_o))):
            there = out.at[partner(c, m)]
            rcopy(there, there, f_s.at[kind, m], f_r.at[kind, m], {"ctx": partner(c, m)}).wait_recv()
            fin(kind, m, own, out).wait_send()
        gg_ctx(m).wait_send()
    own_m.wait()
    own_a.wait()
    gg0.wait_send()
    swap_tok.wait_send()
    swap_out.wait_send()
    for m in (1, 2, 3):
        ag_peer(AG_X, xall, m, x_h.at[x_half]).wait_send()
        ag_peer(AG_COT, cotall, m, cot_h.at[x_half]).wait_send()
        ag_peer(AG_N2, n2, m).wait_send()
        ag_peer(AG_GM, gm, m).wait_send()
        for kind in range(4):
            rs_peer(kind, m).wait_send()
        ag_sib(AG_X, xall, m).wait_send()
        ag_sib(AG_COT, cotall, m).wait_send()
    for m in range(4):
        ag_sib(AG_N2, n2, m).wait_send()
        ag_sib(AG_GM, gm, m).wait_send()
        for kind in range(4):
            rs_sib(kind, m).wait_send()
    for d in range(1, Z):
        for make in (z_gain, z_wa, z_wm, z_gwm, z_gwa, gg_z):
            make(d).wait_send()


def tables(doc_len, span_len):
    count = doc_len.shape[0]
    upto = jnp.arange(count)[:, None] >= jnp.arange(count)[None, :]
    doc_end = jnp.sum(jnp.where(upto, doc_len[None, :], 0), axis=1)
    doc_start = doc_end - doc_len
    places = jnp.arange(span_len, dtype=jnp.int32)
    begins = jnp.max(
        jnp.where(places[:, None] >= doc_start[None, :], doc_start[None, :], 0), axis=1
    )
    segment = jnp.sum((places[:, None] >= doc_end[None, :]).astype(jnp.int32), axis=1)
    offset = (places - begins).astype(F32)
    half = HD // 2
    frequency = ROPE_BASE ** (-(jnp.arange(half, dtype=F32) * (2.0 / HD)))
    angles = offset[:, None] * frequency[None, :]
    cos, sin = jnp.cos(angles), jnp.sin(angles)
    return (
        jnp.concatenate([cos] * 4, axis=1),
        jnp.concatenate([-sin, sin, -sin, sin], axis=1),
        segment.astype(F32),
    )


def local(ways, tokens, doc_lengths, gain_attn, w_qkv, w_attn_out, gain_mlp, w_in, w_mlp_out, cotangent):
    Z, N = ways
    ci, zi = lax.axis_index("ctx"), lax.axis_index("dp")
    R, D = tokens.shape
    S = R * N
    H = R // 2
    Dz, width = w_qkv.shape[1:]
    units = w_in.shape[2]
    PW = width // N
    UW = -(-units // (N * LANES)) * LANES
    padded = UW * N

    qkv = lax.dynamic_slice_in_dim(w_qkv, ci * PW, PW, 2)
    w_out = lax.dynamic_slice_in_dim(w_attn_out, ci * PW, PW, 0).T
    wa = jnp.concatenate([qkv[0], qkv[1], qkv[2], w_out], axis=1)
    w_up = jnp.pad(w_in, ((0, 0), (0, 0), (0, padded - units)))
    w_up = lax.dynamic_slice_in_dim(w_up, ci * UW, UW, 2)
    w_down = jnp.pad(w_mlp_out, ((0, padded - units), (0, 0)))
    w_down = lax.dynamic_slice_in_dim(w_down, ci * UW, UW, 0).T
    wm = jnp.concatenate([w_up[0], w_up[1], w_down], axis=1)
    gains = lax.dynamic_update_slice(
        jnp.zeros((16, D), BF16), jnp.stack([gain_attn, gain_mlp]), (0, zi * Dz)
    )
    cos, sin, segment = tables(doc_lengths[0], S)
    segr = jnp.broadcast_to(segment[None, :], (8, S))
    segc = jnp.broadcast_to(segment[:, None], (S, LANES))

    anywhere = pl.BlockSpec(memory_space=pl.ANY)
    vmem = pl.BlockSpec(memory_space=pltpu.VMEM)
    V = pltpu.VMEM
    dma = pltpu.SemaphoreType.DMA
    scratch = [
        V((S, D), BF16), V((S, D), BF16), V((S, D), BF16), V((S, D), BF16), V((S, D), BF16),
        V((Z, 16, D), BF16), V((D, 4 * PW), BF16), V((D, 3 * UW), BF16),
        V((S, PW), BF16), V((S, PW), BF16), V((S, PW), BF16), V((PW, S), BF16), V((PW, S), BF16),
        V((S, PW), BF16), V((PW, S), BF16), V((PW // HD, N, S, R), BF16), V((8, S), F32),
        V((N, H, D), F32), V((4, N, H, D), BF16), V((4, N, H, D), BF16), V((4, N, H, D), BF16),
        V((4, N, H, D), BF16), V((S, UW), BF16), V((S, 2 * UW), BF16),
        V((D, 3 * UW), BF16), V((Z, Dz, 3 * UW), BF16), V((D, 4 * PW), BF16), V((Z, Dz, 4 * PW), BF16),
        V((Dz, 3 * UW), BF16), V((Dz, 4 * PW), BF16),
        V((H, D), F32), V((H, D), F32), V((S, 3 * PW), BF16), V((S, PW), F32), V((S, PW), F32),
        V((8, D), F32), V((3, 8, D), F32), V((3 + Z, 8, D), F32),
        dma((4, N)), dma((4, N)), dma((4, N)), dma((4, N)), dma((4, N)), dma((4, N)), dma((4, N)),
        dma((4, N)), dma((6, Z)), dma((6, Z)), dma((2, N)), dma((2, N)), dma((2,)), dma((2,)),
        dma((N,)), dma((N,)), dma((5,)),
    ]
    out, gtok, ga, gmm, gg = pl.pallas_call(
        functools.partial(layer_kernel, ways),
        out_shape=[
            jax.ShapeDtypeStruct((R, D), BF16),
            jax.ShapeDtypeStruct((R, D), F32),
            jax.ShapeDtypeStruct((N, Dz, 4 * PW), BF16),
            jax.ShapeDtypeStruct((N, Dz, 3 * UW), BF16),
            jax.ShapeDtypeStruct((8, D), F32),
        ],
        in_specs=[anywhere] * 5 + [vmem] * 4,
        out_specs=[vmem, vmem, anywhere, anywhere, vmem],
        scratch_shapes=scratch,
        compiler_params=pltpu.CompilerParams(
            collective_id=0, has_side_effects=True, vmem_limit_bytes=60 * 1024 * 1024
        ),
        cost_estimate=pl.CostEstimate(
            flops=12 * 10**9, bytes_accessed=12 * 2**20, transcendentals=4 * 10**6
        ),
        name="layer",
    )(tokens, cotangent, wa, wm, gains, cos, sin, segr, segc)

    gains_own = lax.dynamic_slice_in_dim(gg[0:2], zi * Dz, Dz, 1)
    ga_f = ga.astype(F32)
    g_qkv = jnp.stack(
        [
            ga_f[:, :, k * PW : (k + 1) * PW].transpose(1, 0, 2).reshape(Dz, N * PW)
            for k in range(3)
        ]
    )
    g_out = ga_f[:, :, 3 * PW :].transpose(0, 2, 1).reshape(N * PW, Dz)
    gm_f = gmm.astype(F32)
    g_in = jnp.stack(
        [
            gm_f[:, :, k * UW : (k + 1) * UW].transpose(1, 0, 2).reshape(Dz, padded)[:, :units]
            for k in range(2)
        ]
    )
    g_down = gm_f[:, :, 2 * UW :].transpose(0, 2, 1).reshape(padded, Dz)[:units]
    return (out, gtok, gains_own[0], g_qkv, g_out, gains_own[1], g_in, g_down)


def solution(mesh):
    in_specs = (
        P(("dp", "ctx"), None),
        P("dp", None),
        P("dp"),
        P(None, "dp", "tensor"),
        P("tensor", "dp"),
        P("dp"),
        P(None, "dp", "tensor"),
        P("tensor", "dp"),
        P(("dp", "ctx"), None),
    )
    out_specs = (
        P(("dp", "ctx"), None),
        P(("dp", "ctx"), None),
        P("dp"),
        P(None, "dp", "tensor"),
        P("tensor", "dp"),
        P("dp"),
        P(None, "dp", "tensor"),
        P("tensor", "dp"),
    )
    ways = (mesh.shape["dp"], mesh.shape["ctx"])
    return jax.shard_map(
        functools.partial(local, ways),
        mesh=mesh,
        in_specs=in_specs,
        out_specs=out_specs,
        check_vma=False,
    )
```

```python
import functools
import math

import jax
import jax.numpy as jnp
from jax import lax
from jax.experimental import pallas as pl
from jax.experimental.pallas import tpu as pltpu
from jax.sharding import PartitionSpec as P

HD = 64
LANES = 128
NORM_EPS = 1e-05
ROPE_BASE = 160000.0
MASK_FILL = -1e30
INV_ROOT_TWO = 1.0 / math.sqrt(2.0)
INV_ROOT_TWO_PI = 1.0 / math.sqrt(2.0 * math.pi)
MESH = pl.DeviceIdType.MESH
F32 = jnp.float32
BF16 = jnp.bfloat16

AG_X, AG_COT, AG_N2, AG_GM = range(4)
RS_ATTN, RS_GN2, RS_OUT, RS_GN1 = range(4)
Z_GAIN, Z_WA, Z_WM, Z_GIN, Z_GDOWN, Z_GWA, Z_GG = range(7)


def dot(a, b, ca=1, cb=0):
    return lax.dot_general(a, b, (((ca,), (cb,)), ((), ())), preferred_element_type=F32)


def partner(c, m):
    y = lax.rem(lax.div(c, 2) + m // 2, 2)
    x = lax.rem(lax.rem(c, 2) + m % 2, 2)
    return y * 2 + x


def swap_halves(u):
    lane = lax.broadcasted_iota(jnp.int32, u.shape, 1)
    first = lax.rem(lane, HD) < HD // 2
    return jnp.where(first, pltpu.roll(u, LANES - HD // 2, 1), pltpu.roll(u, HD // 2, 1))


def norm_stats(v):
    centered = v - jnp.mean(v, axis=-1, keepdims=True)
    inv = lax.rsqrt(jnp.mean(centered * centered, axis=-1, keepdims=True) + NORM_EPS)
    return centered * inv, inv


def norm_back(grad, hat, inv, gain):
    gh = grad * gain
    inner = (
        gh
        - jnp.mean(gh, axis=-1, keepdims=True)
        - hat * jnp.mean(gh * hat, axis=-1, keepdims=True)
    )
    return inv * inner, jnp.sum(grad * hat, axis=0, keepdims=True)


def layer_kernel(
    ways,
    x_h, cot_h, wa_h, wm_h, gain_h, tab_r,
    out_o, gtok_o, ga_o, gi_o, gd_o, gain_o,
    xall, cotall, n1, n2, gm, gslots, wA, wM, q_s, k_s, v_s, kT, vT, attn, attnT, eT, inv_r,
    acc, sst, srv, pst, prv, hid, gpair, gIst, gIrv, gDst, gDrv, gAst, gArv, gIf, gDf, gAf,
    mixed1, gmixed, gproj, gk, gv, gvec, ggst, ggrv,
    segr, ag_ps, ag_pr, ag_ss, ag_sr, rs_ss, rs_sr, rs_ps, rs_pr, z_s, z_r, f_s, f_r, sw_s, sw_r,
    gg_s, gg_r, loc,
):
    Z, N = ways
    z, c, t = lax.axis_index("dp"), lax.axis_index("ctx"), lax.axis_index("tensor")
    o = 1 - t
    R, D = x_h.shape
    H = R // 2
    S = R * N
    Dz = wa_h.shape[0]
    PW = wa_h.shape[1] // 4
    UW = wm_h.shape[1] // 3
    heads = PW // HD
    CH = 256
    cos_r, sin_r = tab_r.at[:, 0:LANES], tab_r.at[:, LANES : 2 * LANES]
    segc_r = tab_r.at[:, 2 * LANES :]

    def rows(cb, half):
        return pl.ds(pl.multiple_of(cb * R + half * H, H), H)

    def block(cb):
        return pl.ds(pl.multiple_of(cb * R, R), R)

    def rcopy(src, dst, ss, rs, dev):
        return pltpu.make_async_remote_copy(
            src_ref=src, dst_ref=dst, send_sem=ss, recv_sem=rs, device_id=dev, device_id_type=MESH
        )

    bar = pltpu.get_barrier_semaphore()
    for m in range(1, N):
        pl.semaphore_signal(bar, inc=1, device_id={"ctx": partner(c, m)}, device_id_type=MESH)
    pl.semaphore_signal(bar, inc=1, device_id={"tensor": o}, device_id_type=MESH)
    for d in range(1, Z):
        pl.semaphore_signal(bar, inc=1, device_id={"dp": lax.rem(z + d, Z)}, device_id_type=MESH)
    pl.semaphore_wait(bar, N - 1 + 1 + Z - 1)

    def ag_peer(kind, buf, m, src=None):
        own = rows(c, t)
        return rcopy(
            buf.at[own] if src is None else src, buf.at[own], ag_ps.at[kind, m], ag_pr.at[kind, m],
            {"ctx": partner(c, m)},
        )

    def ag_sib(kind, buf, m):
        own = rows(partner(c, m), t)
        return rcopy(
            buf.at[own], buf.at[own], ag_ss.at[kind, m], ag_sr.at[kind, m], {"tensor": o}
        )

    def ag_arrive(kind, buf, m):
        there = buf.at[rows(partner(c, m), t)]
        rcopy(there, there, ag_ps.at[kind, m], ag_pr.at[kind, m], {"ctx": partner(c, m)}).wait_recv()
        ag_sib(kind, buf, m).start()

    def ag_sibling_half(kind, buf, m):
        there = buf.at[rows(partner(c, m), o)]
        rcopy(there, there, ag_ss.at[kind, m], ag_sr.at[kind, m], {"tensor": o}).wait_recv()

    def rs_sib(kind, m):
        return rcopy(
            sst.at[kind, m], srv.at[kind, m], rs_ss.at[kind, m], rs_sr.at[kind, m], {"tensor": o}
        )

    def rs_peer(kind, m):
        return rcopy(
            pst.at[kind, m], prv.at[kind, m], rs_ps.at[kind, m], rs_pr.at[kind, m],
            {"ctx": partner(c, m)},
        )

    def rs_begin(kind, m, partial):
        cb = partner(c, m)
        sst[kind, m] = partial(cb, o).astype(BF16)
        rs_sib(kind, m).start()
        acc[kind % 2, m] = partial(cb, t)

    def rs_mid(kind, m):
        rs_sib(kind, m).wait_recv()
        total = acc[kind % 2, m] + srv[kind, m].astype(F32)
        if m == 0:
            acc[kind % 2, 0] = total
        else:
            pst[kind, m] = total.astype(BF16)
            rs_peer(kind, m).start()

    def rs_end(kind):
        for m in (1, 2, 3):
            rs_peer(kind, m).wait_recv()
        return (
            acc[kind % 2, 0]
            + prv[kind, 1].astype(F32)
            + prv[kind, 2].astype(F32)
            + prv[kind, 3].astype(F32)
        )

    def zrow(i):
        return pl.ds(pl.multiple_of(i * Dz, Dz), Dz)

    def z_copy(kind, d, src, dst):
        return rcopy(
            src, dst, z_s.at[kind, d], z_r.at[kind, d], {"dp": lax.rem(z + d, Z)}
        )

    def z_recv(kind, d, dst):
        rcopy(dst, dst, z_s.at[kind, d], z_r.at[kind, d], {"dp": lax.rem(z + d, Z)}).wait_recv()

    def z_gain(d):
        return z_copy(Z_GAIN, d, gain_h, gslots.at[z])

    def z_wa(d):
        return z_copy(Z_WA, d, wa_h, wA.at[zrow(z)])

    def z_wm(d):
        return z_copy(Z_WM, d, wm_h, wM.at[zrow(z)])

    def z_gin(d):
        return z_copy(Z_GIN, d, gIst.at[zrow(lax.rem(z + d, Z))], gIrv.at[d])

    def z_gdown(d):
        return z_copy(Z_GDOWN, d, gDst.at[zrow(lax.rem(z + d, Z))], gDrv.at[d])

    def z_gwa(d):
        return z_copy(Z_GWA, d, gAst.at[zrow(lax.rem(z + d, Z))], gArv.at[d])

    x_half = pl.ds(pl.multiple_of(t * H, H), H)
    for m in (1, 2, 3):
        ag_peer(AG_X, xall, m, x_h.at[x_half]).start()
    for d in range(1, Z):
        z_gain(d).start()
    for d in range(1, Z):
        z_wa(d).start()
    local = [
        pltpu.make_async_copy(x_h, xall.at[block(c)], loc.at[0]),
        pltpu.make_async_copy(gain_h, gslots.at[z], loc.at[1]),
        pltpu.make_async_copy(wa_h, wA.at[zrow(z)], loc.at[2]),
        pltpu.make_async_copy(cot_h, cotall.at[block(c)], loc.at[3]),
        pltpu.make_async_copy(wm_h, wM.at[zrow(z)], loc.at[4]),
    ]
    for one in local:
        one.start()
    for d in range(1, Z):
        z_wm(d).start()
    for m in (1, 2, 3):
        ag_peer(AG_COT, cotall, m, cot_h.at[x_half]).start()
    for one in local:
        one.wait()

    for d in range(1, Z):
        z_recv(Z_GAIN, d, gslots.at[lax.rem(z + Z - d, Z)])
    gains = gslots[0].astype(F32)
    for i in range(1, Z):
        gains = gains + gslots[i].astype(F32)
    gvec[...] = gains[0:8]

    def norm_one(cb):
        def body(i, carry):
            r = pl.ds(pl.multiple_of(cb * R + i * 64, 64), 64)
            hat, _ = norm_stats(xall[r, :].astype(F32))
            n1[r, :] = (hat * gvec[0:1, :]).astype(BF16)
            return carry

        lax.fori_loop(0, R // 64, body, 0)

    norm_one(c)
    for m in (1, 2, 3):
        ag_arrive(AG_X, xall, m)
    for m in (1, 2, 3):
        ag_sibling_half(AG_X, xall, m)
        norm_one(partner(c, m))

    segr[...] = segc_r[...].T[0:8, :]

    for d in range(1, Z):
        z_recv(Z_WA, d, wA.at[zrow(lax.rem(z + Z - d, Z))])

    def project(cb, carry):
        b = block(cb)
        proj = dot(n1[b, :], wA[:, 0 : 3 * PW]).astype(BF16)
        cos, sin = cos_r[b, :], sin_r[b, :]
        qf = proj[:, 0:PW].astype(F32)
        kf = proj[:, PW : 2 * PW].astype(F32)
        q_rot = (qf * cos + swap_halves(qf) * sin).astype(BF16).astype(F32) * (HD**-0.5)
        k_rot = (kf * cos + swap_halves(kf) * sin).astype(BF16)
        val = proj[:, 2 * PW : 3 * PW]
        q_s[b, :] = q_rot.astype(BF16)
        k_s[b, :] = k_rot
        v_s[b, :] = val
        kT[:, b] = k_rot.astype(F32).T.astype(BF16)
        vT[:, b] = val.astype(F32).T.astype(BF16)
        return carry

    lax.fori_loop(0, N, project, 0)

    lane = lax.broadcasted_iota(jnp.int32, (R, PW), 1)

    def only(u, h):
        return jnp.where(lax.div(lane, HD) == h, u, jnp.zeros_like(u))

    def attend(cb):
        b = block(cb)
        same = segc_r[:, 0:1] == segr[0:1, b]
        for h in range(heads):
            s = dot(k_s[...], only(q_s[b, :], h), 1, 1)
            s = jnp.where(same, s, MASK_FILL)
            e = jnp.exp(s - jnp.max(s, axis=0, keepdims=True))
            inv = 1.0 / jnp.sum(e, axis=0, keepdims=True)
            eb = e.astype(BF16)
            eT[h, cb] = eb
            inv_r[h : h + 1, b] = inv
            hr = slice(h * HD, (h + 1) * HD)
            attnT[hr, b] = (dot(vT[hr, :], eb) * inv).astype(BF16)
        attn[b, :] = attnT[:, b].astype(F32).T.astype(BF16)

    def part_attn(cb, half):
        return dot(attn[rows(cb, half), :], wA[:, 3 * PW :], 1, 1)

    order = (3, 2, 1, 0)
    for i, m in enumerate(order):
        attend(partner(c, m))
        rs_begin(RS_ATTN, m, part_attn)
        if i:
            rs_mid(RS_ATTN, order[i - 1])
    rs_mid(RS_ATTN, 0)
    for m in (1, 2, 3):
        ag_arrive(AG_COT, cotall, m)
    mixed1[...] = xall[rows(c, t), :].astype(F32) + rs_end(RS_ATTN)

    hat2, inv2 = norm_stats(mixed1[...])
    n2[rows(c, t), :] = (hat2 * gvec[1:2, :]).astype(BF16)
    for m in (1, 2, 3):
        ag_peer(AG_N2, n2, m).start()
    ag_sib(AG_N2, n2, 0).start()
    for d in range(1, Z):
        z_recv(Z_WM, d, wM.at[zrow(lax.rem(z + Z - d, Z))])
    for m in (1, 2, 3):
        ag_sibling_half(AG_COT, cotall, m)

    def mlp(cb):
        b = block(cb)
        pair = dot(n2[b, :], wM[:, 0 : 2 * UW])
        grad_h = dot(cotall[b, :], wM[:, 2 * UW :])
        a, g = pair[:, :UW], pair[:, UW:]
        cdf = 0.5 * (1.0 + lax.erf(a * INV_ROOT_TWO))
        gelu = a * cdf
        hid[b, :] = (gelu * g).astype(BF16)
        slope = cdf + a * jnp.exp(-0.5 * a * a) * INV_ROOT_TWO_PI
        gpair[b, 0:UW] = (grad_h * g * slope).astype(BF16)
        gpair[b, UW:] = (grad_h * gelu).astype(BF16)

    def part_gn2(cb, half):
        return dot(gpair[rows(cb, half), :], wM[:, 0 : 2 * UW], 1, 1)

    def part_out(cb, half):
        return dot(hid[rows(cb, half), :], wM[:, 2 * UW :], 1, 1)

    for i, m in enumerate((0, 1, 2, 3)):
        if m:
            ag_arrive(AG_N2, n2, m)
        ag_sibling_half(AG_N2, n2, m)
        mlp(partner(c, m))
        rs_begin(RS_GN2, m, part_gn2)
        if i:
            rs_mid(RS_GN2, m - 1)
    rs_mid(RS_GN2, 3)

    def grads_down(i, carry):
        col = pl.ds(pl.multiple_of(i * CH, CH), CH)
        gDst[col, :] = dot(cotall[:, col], hid[...], 0, 0).astype(BF16)
        return carry

    def grads_in(i, carry):
        col = pl.ds(pl.multiple_of(i * CH, CH), CH)
        gIst[col, :] = dot(n2[:, col], gpair[...], 0, 0).astype(BF16)
        return carry

    lax.fori_loop(0, D // CH, grads_down, 0)
    for d in range(1, Z):
        z_gdown(d).start()
    lax.fori_loop(0, D // CH, grads_in, 0)
    for d in range(1, Z):
        z_gin(d).start()

    hat2, inv2 = norm_stats(mixed1[...])
    back2, gg_mlp = norm_back(rs_end(RS_GN2), hat2, inv2, gvec[1:2, :])
    ggst[0, 1:2, :] = gg_mlp
    gmixed[...] = cotall[rows(c, t), :].astype(F32) + back2
    gm[rows(c, t), :] = gmixed[...].astype(BF16)
    for m in (1, 2, 3):
        ag_peer(AG_GM, gm, m).start()
    ag_sib(AG_GM, gm, 0).start()
    for m in order:
        rs_begin(RS_OUT, m, part_out)

    def fin(kind, m, own, out):
        return rcopy(own, out.at[c], f_s.at[kind, m], f_r.at[kind, m], {"ctx": partner(c, m)})

    def own_copy(kind, own, out):
        return pltpu.make_async_copy(own, out.at[c], loc.at[kind])

    def finish(kind, z_kind, stage, arrived, own, out):
        total = stage[zrow(z), :].astype(F32)
        for d in range(1, Z):
            z_recv(z_kind, d, arrived.at[d])
            total = total + arrived[d].astype(F32)
        own[...] = total.astype(BF16)
        for m in (1, 2, 3):
            fin(kind, m, own, out).start()
        own_copy(kind, own, out).start()

    finals = ((gIf, gi_o), (gDf, gd_o), (gAf, ga_o))

    gk[...] = jnp.zeros_like(gk)
    gv[...] = jnp.zeros_like(gv)

    def rotate_back(g, b):
        return g * cos_r[b, :] + swap_halves(g * sin_r[b, :])

    def attend_back(cb):
        b = block(cb)
        g = dot(gm[b, :], wA[:, 3 * PW :]).astype(BF16)
        gT = g.astype(F32).T
        scaled = []
        grad_q = []
        for h in range(heads):
            hr = slice(h * HD, (h + 1) * HD)
            inv = inv_r[h : h + 1, b]
            delta = jnp.sum(gT[hr, :] * attnT[hr, b].astype(F32), axis=0, keepdims=True)
            gp = dot(v_s[...], only(g, h), 1, 1)
            ds = (eT[h, cb].astype(F32) * ((gp - delta) * inv)).astype(BF16)
            grad_q.append(dot(kT[hr, :], ds))
            gk[...] += dot(ds, only(q_s[b, :], h))
            scaled.append(gT[hr, :] * inv)
        gs = jnp.concatenate(scaled, axis=0).T.astype(BF16)
        for h in range(heads):
            gv[...] += dot(eT[h, cb], only(gs, h))
        gq = jnp.concatenate(grad_q, axis=0).T * (HD**-0.5)
        gproj[b, 0:PW] = rotate_back(gq, b).astype(BF16)

    for m in (0, 1, 2, 3):
        if m:
            ag_arrive(AG_GM, gm, m)
        ag_sibling_half(AG_GM, gm, m)
        attend_back(partner(c, m))
        rs_mid(RS_OUT, 3 - m)
    finish(1, Z_GDOWN, gDst, gDrv, gDf, gd_o)

    def unrotate(cb, carry):
        b = block(cb)
        gproj[b, PW : 2 * PW] = rotate_back(gk[b, :], b).astype(BF16)
        gproj[b, 2 * PW :] = gv[b, :].astype(BF16)
        return carry

    lax.fori_loop(0, N, unrotate, 0)

    def grads_attn(i, carry):
        col = pl.ds(pl.multiple_of(i * CH, CH), CH)
        gAst[col, 0 : 3 * PW] = dot(n1[:, col], gproj[...], 0, 0).astype(BF16)
        gAst[col, 3 * PW :] = dot(gm[:, col], attn[...], 0, 0).astype(BF16)
        return carry

    lax.fori_loop(0, D // CH, grads_attn, 0)
    for d in range(1, Z):
        z_gwa(d).start()

    def part_gn1(cb, half):
        return dot(gproj[rows(cb, half), :], wA[:, 0 : 3 * PW], 1, 1)

    for i, m in enumerate(order):
        rs_begin(RS_GN1, m, part_gn1)
        if i:
            rs_mid(RS_GN1, order[i - 1])
    rs_mid(RS_GN1, 0)

    finish(0, Z_GIN, gIst, gIrv, gIf, gi_o)

    hat1, inv1 = norm_stats(xall[rows(c, t), :].astype(F32))
    back1, gg_attn = norm_back(rs_end(RS_GN1), hat1, inv1, gvec[0:1, :])
    ggst[0, 0:1, :] = gg_attn
    gtok_o[x_half, :] = gmixed[...] + back1
    swap_tok = rcopy(
        gtok_o.at[x_half], gtok_o.at[x_half], sw_s.at[0], sw_r.at[0], {"tensor": o}
    )
    swap_tok.start()

    ggst[0, 2:8, :] = jnp.zeros_like(ggst[0, 2:8, :])
    gg0 = rcopy(ggst.at[0], ggrv.at[0], gg_s.at[0], gg_r.at[0], {"tensor": o})
    gg0.start()

    out_o[x_half, :] = (mixed1[...] + rs_end(RS_OUT)).astype(BF16)
    swap_out = rcopy(
        out_o.at[x_half], out_o.at[x_half], sw_s.at[1], sw_r.at[1], {"tensor": o}
    )
    swap_out.start()
    gg0.wait_recv()
    ggst[1] = ggst[0] + ggrv[0]

    def gg_ctx(m):
        return rcopy(ggst.at[1], ggrv.at[m], gg_s.at[m], gg_r.at[m], {"ctx": partner(c, m)})

    for m in (1, 2, 3):
        gg_ctx(m).start()

    for m in (1, 2, 3):
        gg_ctx(m).wait_recv()
    ggst[2] = (ggst[1] + ggrv[1]) + (ggrv[2] + ggrv[3])

    def gg_z(d):
        return z_copy(Z_GG, d, ggst.at[2], ggrv.at[3 + d])

    for d in range(1, Z):
        gg_z(d).start()
    finish(2, Z_GWA, gAst, gArv, gAf, ga_o)
    total = ggst[2]
    for d in range(1, Z):
        z_recv(Z_GG, d, ggrv.at[3 + d])
        total = total + ggrv[3 + d]
    gain_o[...] = total

    other = pl.ds(pl.multiple_of(o * H, H), H)
    rcopy(gtok_o.at[other], gtok_o.at[other], sw_s.at[0], sw_r.at[0], {"tensor": o}).wait_recv()
    rcopy(out_o.at[other], out_o.at[other], sw_s.at[1], sw_r.at[1], {"tensor": o}).wait_recv()
    for m in (1, 2, 3):
        for kind, (own, out) in enumerate(finals):
            there = out.at[partner(c, m)]
            rcopy(there, there, f_s.at[kind, m], f_r.at[kind, m], {"ctx": partner(c, m)}).wait_recv()
            fin(kind, m, own, out).wait_send()
        gg_ctx(m).wait_send()
    for kind, (own, out) in enumerate(finals):
        own_copy(kind, own, out).wait()
    gg0.wait_send()
    swap_tok.wait_send()
    swap_out.wait_send()
    for m in (1, 2, 3):
        ag_peer(AG_X, xall, m, x_h.at[x_half]).wait_send()
        ag_peer(AG_COT, cotall, m, cot_h.at[x_half]).wait_send()
        ag_peer(AG_N2, n2, m).wait_send()
        ag_peer(AG_GM, gm, m).wait_send()
        for kind in range(4):
            rs_peer(kind, m).wait_send()
        ag_sib(AG_X, xall, m).wait_send()
        ag_sib(AG_COT, cotall, m).wait_send()
    for m in range(4):
        ag_sib(AG_N2, n2, m).wait_send()
        ag_sib(AG_GM, gm, m).wait_send()
        for kind in range(4):
            rs_sib(kind, m).wait_send()
    for d in range(1, Z):
        for make in (z_gain, z_wa, z_wm, z_gin, z_gdown, z_gwa, gg_z):
            make(d).wait_send()


def spread_kernel(ga, gi, gd, qkv_o, out_o, in_o, down_o):
    width, units = out_o.shape[0], down_o.shape[0]
    for k in range(3):
        qkv_o[k] = ga[:, k * width : (k + 1) * width].astype(F32)
    out_o[...] = ga[:, 3 * width :].astype(F32).T
    for k in range(2):
        in_o[k] = gi[:, k * units : (k + 1) * units].astype(F32)
    down_o[...] = gd[...].astype(F32).T


def tables(doc_len, span_len):
    count = doc_len.shape[0]
    upto = jnp.arange(count)[:, None] >= jnp.arange(count)[None, :]
    doc_end = jnp.sum(jnp.where(upto, doc_len[None, :], 0), axis=1)
    doc_start = doc_end - doc_len
    places = jnp.arange(span_len, dtype=jnp.int32)
    begins = jnp.max(
        jnp.where(places[:, None] >= doc_start[None, :], doc_start[None, :], 0), axis=1
    )
    segment = jnp.sum((places[:, None] >= doc_end[None, :]).astype(jnp.int32), axis=1)
    offset = (places - begins).astype(F32)
    half = HD // 2
    frequency = ROPE_BASE ** (-(jnp.arange(half, dtype=F32) * (2.0 / HD)))
    angles = offset[:, None] * frequency[None, :]
    cos, sin = jnp.cos(angles), jnp.sin(angles)
    seg = jnp.broadcast_to(segment.astype(F32)[:, None], (span_len, LANES))
    return jnp.concatenate([cos] * 4 + [-sin, sin, -sin, sin] + [seg], axis=1)


def local(ways, tokens, doc_lengths, gain_attn, w_qkv, w_attn_out, gain_mlp, w_in, w_mlp_out, cotangent):
    Z, N = ways
    ci, zi = lax.axis_index("ctx"), lax.axis_index("dp")
    R, D = tokens.shape
    S = R * N
    H = R // 2
    Dz, width = w_qkv.shape[1:]
    units = w_in.shape[2]
    PW = width // N
    UW = -(-units // (N * LANES)) * LANES
    padded = UW * N

    qkv = lax.dynamic_slice_in_dim(w_qkv, ci * PW, PW, 2)
    w_out = lax.dynamic_slice_in_dim(w_attn_out, ci * PW, PW, 0).T
    wa = jnp.concatenate([qkv[0], qkv[1], qkv[2], w_out], axis=1)
    w_up = jnp.pad(w_in, ((0, 0), (0, 0), (0, padded - units)))
    w_up = lax.dynamic_slice_in_dim(w_up, ci * UW, UW, 2)
    w_down = jnp.pad(w_mlp_out, ((0, padded - units), (0, 0)))
    w_down = lax.dynamic_slice_in_dim(w_down, ci * UW, UW, 0).T
    wm = jnp.concatenate([w_up[0], w_up[1], w_down], axis=1)
    gains = lax.dynamic_update_slice(
        jnp.zeros((16, D), BF16), jnp.stack([gain_attn, gain_mlp]), (0, zi * Dz)
    )
    tab = tables(doc_lengths[0], S)

    anywhere = pl.BlockSpec(memory_space=pl.ANY)
    vmem = pl.BlockSpec(memory_space=pltpu.VMEM)
    V = pltpu.VMEM
    dma = pltpu.SemaphoreType.DMA
    scratch = [
        V((S, D), BF16), V((S, D), BF16), V((S, D), BF16), V((S, D), BF16), V((S, D), BF16),
        V((Z, 16, D), BF16), V((D, 4 * PW), BF16), V((D, 3 * UW), BF16),
        V((S, PW), BF16), V((S, PW), BF16), V((S, PW), BF16), V((PW, S), BF16), V((PW, S), BF16),
        V((S, PW), BF16), V((PW, S), BF16), V((PW // HD, N, S, R), BF16), V((8, S), F32),
        V((2, N, H, D), F32), V((4, N, H, D), BF16), V((4, N, H, D), BF16), V((4, N, H, D), BF16),
        V((4, N, H, D), BF16), V((S, UW), BF16), V((S, 2 * UW), BF16),
        V((D, 2 * UW), BF16), V((Z, Dz, 2 * UW), BF16), V((D, UW), BF16), V((Z, Dz, UW), BF16),
        V((D, 4 * PW), BF16), V((Z, Dz, 4 * PW), BF16),
        V((Dz, 2 * UW), BF16), V((Dz, UW), BF16), V((Dz, 4 * PW), BF16),
        V((H, D), F32), V((H, D), F32), V((S, 3 * PW), BF16), V((S, PW), F32), V((S, PW), F32),
        V((8, D), F32), V((3, 8, D), F32), V((3 + Z, 8, D), F32), V((8, S), F32),
        dma((4, N)), dma((4, N)), dma((4, N)), dma((4, N)), dma((4, N)), dma((4, N)), dma((4, N)),
        dma((4, N)), dma((7, Z)), dma((7, Z)), dma((3, N)), dma((3, N)), dma((2,)), dma((2,)),
        dma((N,)), dma((N,)), dma((5,)),
    ]
    out, gtok, ga, gi, gd, gg = pl.pallas_call(
        functools.partial(layer_kernel, ways),
        out_shape=[
            jax.ShapeDtypeStruct((R, D), BF16),
            jax.ShapeDtypeStruct((R, D), F32),
            jax.ShapeDtypeStruct((N, Dz, 4 * PW), BF16),
            jax.ShapeDtypeStruct((N, Dz, 2 * UW), BF16),
            jax.ShapeDtypeStruct((N, Dz, UW), BF16),
            jax.ShapeDtypeStruct((8, D), F32),
        ],
        in_specs=[anywhere] * 5 + [vmem],
        out_specs=[vmem, vmem, anywhere, anywhere, anywhere, vmem],
        scratch_shapes=scratch,
        compiler_params=pltpu.CompilerParams(
            collective_id=0, has_side_effects=True, vmem_limit_bytes=60 * 1024 * 1024
        ),
        cost_estimate=pl.CostEstimate(
            flops=12 * 10**9, bytes_accessed=12 * 2**20, transcendentals=4 * 10**6
        ),
        name="layer",
    )(tokens, cotangent, wa, wm, gains, tab)

    gains_own = lax.dynamic_slice_in_dim(gg[0:2], zi * Dz, Dz, 1)
    g_qkv, g_out, g_in, g_down = pl.pallas_call(
        spread_kernel,
        grid=(N,),
        out_shape=[
            jax.ShapeDtypeStruct((3, Dz, N * PW), F32),
            jax.ShapeDtypeStruct((N * PW, Dz), F32),
            jax.ShapeDtypeStruct((2, Dz, units), F32),
            jax.ShapeDtypeStruct((units, Dz), F32),
        ],
        in_specs=[
            pl.BlockSpec((None, Dz, 4 * PW), lambda i: (i, 0, 0)),
            pl.BlockSpec((None, Dz, 2 * UW), lambda i: (i, 0, 0)),
            pl.BlockSpec((None, Dz, UW), lambda i: (i, 0, 0)),
        ],
        out_specs=[
            pl.BlockSpec((3, Dz, PW), lambda i: (0, 0, i)),
            pl.BlockSpec((PW, Dz), lambda i: (i, 0)),
            pl.BlockSpec((2, Dz, UW), lambda i: (0, 0, i)),
            pl.BlockSpec((UW, Dz), lambda i: (i, 0)),
        ],
        compiler_params=pltpu.CompilerParams(vmem_limit_bytes=32 * 1024 * 1024),
        name="spread",
    )(ga, gi, gd)
    return (out, gtok, gains_own[0], g_qkv, g_out, gains_own[1], g_in, g_down)


def solution(mesh):
    in_specs = (
        P(("dp", "ctx"), None),
        P("dp", None),
        P("dp"),
        P(None, "dp", "tensor"),
        P("tensor", "dp"),
        P("dp"),
        P(None, "dp", "tensor"),
        P("tensor", "dp"),
        P(("dp", "ctx"), None),
    )
    out_specs = (
        P(("dp", "ctx"), None),
        P(("dp", "ctx"), None),
        P("dp"),
        P(None, "dp", "tensor"),
        P("tensor", "dp"),
        P("dp"),
        P(None, "dp", "tensor"),
        P("tensor", "dp"),
    )
    ways = (mesh.shape["dp"], mesh.shape["ctx"])
    return jax.shard_map(
        functools.partial(local, ways),
        mesh=mesh,
        in_specs=in_specs,
        out_specs=out_specs,
        check_vma=False,
    )
```

```python
import functools
import math

import jax
import jax.numpy as jnp
from jax import lax
from jax.experimental import pallas as pl
from jax.experimental.pallas import tpu as pltpu
from jax.sharding import PartitionSpec as P

HD = 64
LANES = 128
NORM_EPS = 1e-05
ROPE_BASE = 160000.0
MASK_FILL = -1e30
INV_ROOT_TWO = 1.0 / math.sqrt(2.0)
INV_ROOT_TWO_PI = 1.0 / math.sqrt(2.0 * math.pi)
MESH = pl.DeviceIdType.MESH
F32 = jnp.float32
BF16 = jnp.bfloat16

AG_X, AG_COT, AG_N2, AG_GM = range(4)
RS_ATTN, RS_GN2, RS_OUT, RS_GN1 = range(4)
Z_GAIN, Z_GG = range(2)
L_GIN, L_GDOWN, L_GWA, L_WA, L_WM = range(5)


def dot(a, b, ca=1, cb=0):
    return lax.dot_general(a, b, (((ca,), (cb,)), ((), ())), preferred_element_type=F32)


def partner(c, m):
    y = lax.rem(lax.div(c, 2) + lax.div(m, 2), 2)
    x = lax.rem(lax.rem(c, 2) + lax.rem(m, 2), 2)
    return y * 2 + x


def swap_halves(u):
    lane = lax.broadcasted_iota(jnp.int32, u.shape, 1)
    first = lax.rem(lane, HD) < HD // 2
    return jnp.where(first, pltpu.roll(u, LANES - HD // 2, 1), pltpu.roll(u, HD // 2, 1))


def norm_stats(v):
    centered = v - jnp.mean(v, axis=-1, keepdims=True)
    inv = lax.rsqrt(jnp.mean(centered * centered, axis=-1, keepdims=True) + NORM_EPS)
    return centered * inv, inv


def norm_back(grad, hat, inv, gain):
    gh = grad * gain
    inner = (
        gh
        - jnp.mean(gh, axis=-1, keepdims=True)
        - hat * jnp.mean(gh * hat, axis=-1, keepdims=True)
    )
    return inv * inner, jnp.sum(grad * hat, axis=0, keepdims=True)


def layer_kernel(
    ways,
    x_h, cot_h, wa_h, wm_h, gain_h, cos_r, sin_r, segc_r,
    out_o, gtok_o, ga_o, gi_o, gd_o, gain_o,
    xall, cotall, n1, n2, gm, gslots, wA, wM, q_s, k_s, v_s, kT, vT, attn, attnT, eT, inv_r,
    acc, sst, srv, pst, prv, hid, gpair, gIst, gIrv, gDst, gDrv, gAst, gArv, gIf, gDf, gAf,
    mixed1, gmixed, gproj, gk, gv, gvec, ggst, ggrv,
    segr, ag_ps, ag_pr, ag_ss, ag_sr, rs_ss, rs_sr, rs_ps, rs_pr, z_s, z_r, l_s, l_r, f_s, f_r, sw_s, sw_r,
    gg_s, gg_r, loc,
):
    Z, N = ways
    z, c, t = lax.axis_index("dp"), lax.axis_index("ctx"), lax.axis_index("tensor")
    o = 1 - t
    via, onto = 1 + t, 2 - t
    R, D = x_h.shape
    H = R // 2
    S = R * N
    Dz = wa_h.shape[0]
    PW = wa_h.shape[1] // 4
    UW = wm_h.shape[0] // 3
    heads = PW // HD
    CH = 256
    gst, grv = (gIst, gDst, gAst), (gIrv, gDrv, gArv)

    def rows(cb, half):
        return pl.ds(pl.multiple_of(cb * R + half * H, H), H)

    def block(cb):
        return pl.ds(pl.multiple_of(cb * R, R), R)

    def rcopy(src, dst, ss, rs, dev):
        return pltpu.make_async_remote_copy(
            src_ref=src, dst_ref=dst, send_sem=ss, recv_sem=rs, device_id=dev, device_id_type=MESH
        )

    bar = pltpu.get_barrier_semaphore()
    for m in range(1, N):
        pl.semaphore_signal(bar, inc=1, device_id={"ctx": partner(c, m)}, device_id_type=MESH)
    pl.semaphore_signal(bar, inc=1, device_id={"tensor": o}, device_id_type=MESH)
    for d in range(1, Z):
        pl.semaphore_signal(bar, inc=1, device_id={"dp": lax.rem(z + d, Z)}, device_id_type=MESH)
    pl.semaphore_wait(bar, N - 1 + 1 + Z - 1)

    def ag_peer(kind, buf, m, src=None):
        own = rows(c, t)
        return rcopy(
            buf.at[own] if src is None else src, buf.at[own], ag_ps.at[kind, m], ag_pr.at[kind, m],
            {"ctx": partner(c, m)},
        )

    def ag_sib(kind, buf, m):
        own = rows(partner(c, m), t)
        return rcopy(
            buf.at[own], buf.at[own], ag_ss.at[kind, m], ag_sr.at[kind, m], {"tensor": o}
        )

    def ag_relay(kind, buf):
        there = buf.at[rows(partner(c, via), t)]
        return rcopy(
            there, there, ag_ps.at[kind, 3], ag_pr.at[kind, 3], {"ctx": partner(c, onto)}
        )

    def ag_arrive(kind, buf, m):
        there = buf.at[rows(partner(c, m), t)]
        rcopy(there, there, ag_ps.at[kind, m], ag_pr.at[kind, m], {"ctx": partner(c, onto)}).wait_recv()

    def ag_near(kind, buf):
        ag_arrive(kind, buf, via)
        ag_relay(kind, buf).start()
        ag_sib(kind, buf, via).start()
        ag_arrive(kind, buf, onto)
        ag_sib(kind, buf, onto).start()

    def ag_far(kind, buf):
        ag_arrive(kind, buf, 3)
        ag_sib(kind, buf, 3).start()

    def ag_sibling_half(kind, buf, m):
        there = buf.at[rows(partner(c, m), o)]
        rcopy(there, there, ag_ss.at[kind, m], ag_sr.at[kind, m], {"tensor": o}).wait_recv()

    def rs_sib(kind, m):
        return rcopy(
            sst.at[kind, m], srv.at[kind, m], rs_ss.at[kind, m], rs_sr.at[kind, m], {"tensor": o}
        )

    def rs_peer(kind, m, to):
        return rcopy(
            pst.at[kind, m - 1], prv.at[kind, m - 1], rs_ps.at[kind, m], rs_pr.at[kind, m],
            {"ctx": partner(c, to)},
        )

    def rs_begin(kind, m, partial):
        cb = partner(c, m)
        sst[kind, m] = partial(cb, o).astype(BF16)
        rs_sib(kind, m).start()
        acc[kind % 2, m] = partial(cb, t)

    def rs_total(kind, m):
        rs_sib(kind, m).wait_recv()
        return acc[kind % 2, m] + srv[kind, m].astype(F32)

    def rs_own(kind):
        acc[kind % 2, 0] = rs_total(kind, 0)

    def rs_far(kind):
        pst[kind, 2] = rs_total(kind, 3).astype(BF16)
        rs_peer(kind, 3, onto).start()

    def rs_near(kind):
        pst[kind, onto - 1] = rs_total(kind, onto).astype(BF16)
        rs_peer(kind, onto, onto).start()

    def rs_joined(kind):
        total = rs_total(kind, via)
        rs_peer(kind, 3, onto).wait_recv()
        pst[kind, via - 1] = (total + prv[kind, 2].astype(F32)).astype(BF16)
        rs_peer(kind, via, via).start()

    def rs_end(kind):
        for m in (1, 2):
            rs_peer(kind, m, m).wait_recv()
        return acc[kind % 2, 0] + prv[kind, 0].astype(F32) + prv[kind, 1].astype(F32)

    def zrow(i):
        return pl.ds(pl.multiple_of(i * Dz, Dz), Dz)

    def z_copy(kind, d, src, dst):
        return rcopy(
            src, dst, z_s.at[kind, d], z_r.at[kind, d], {"dp": lax.rem(z + d, Z)}
        )

    def z_recv(kind, d, dst):
        rcopy(dst, dst, z_s.at[kind, d], z_r.at[kind, d], {"dp": lax.rem(z + d, Z)}).wait_recv()

    def z_gain(d):
        return z_copy(Z_GAIN, d, gain_h, gslots.at[z])

    right, left = lax.rem(z + 1, Z), lax.rem(z + Z - 1, Z)

    def line_copy(kind, side, at, src, dst):
        return rcopy(
            src, dst, l_s.at[kind, side, at], l_r.at[kind, side, at],
            {"dp": left if side else right},
        )

    def gather_send(kind, buf, h, act):
        for side in (0, 1):
            src = z + (h - 1) if side else z - (h - 1)
            ok = (src < Z) & (z > 0) if side else (src >= 0) & (z < Z - 1)

            @pl.when(ok)
            def _():
                there = buf.at[zrow(src)]
                act(line_copy(kind, side, h, there, there))

    def gather_step(kind, buf, h):
        for side in (0, 1):
            src = z + h if side else z - h

            @pl.when((src < Z) if side else (src >= 0))
            def _():
                there = buf.at[zrow(src)]
                line_copy(kind, side, h, there, there).wait_recv()

        if h + 1 < Z:
            gather_send(kind, buf, h + 1, start)

    def scatter_copy(kind, side, j):
        stage, arrived = gst[kind], grv[kind]
        return line_copy(kind, side, j, stage.at[zrow(j)], arrived.at[side, zrow(j)])

    def scatter_each(k, side, use):
        j = k if side else Z - 1 - k
        pl.when((j < z) if side else (j > z))(lambda: use(j))

    def scatter_step(kind, k):
        stage, arrived = gst[kind], grv[kind]
        for side in (0, 1):

            def use(j, side=side):
                @pl.when((z < Z - 1) if side else (z > 0))
                def _():
                    scatter_copy(kind, side, j).wait_recv()
                    stage[zrow(j), :] = (
                        stage[zrow(j), :].astype(F32) + arrived[side, zrow(j), :].astype(F32)
                    ).astype(BF16)
                    scatter_copy(kind, side, j).start()

            scatter_each(k, side, use)

    def scatter_total(kind):
        stage, arrived = gst[kind], grv[kind]
        own = zrow(z)
        for side in (0, 1):

            @pl.when((z < Z - 1) if side else (z > 0))
            def _():
                scatter_copy(kind, side, z).wait_recv()

        has_left = jnp.where(z > 0, 1.0, 0.0)
        has_right = jnp.where(z < Z - 1, 1.0, 0.0)
        return (
            stage[own, :].astype(F32)
            + jnp.where(has_left > 0.5, arrived[0, own, :].astype(F32), 0.0)
            + jnp.where(has_right > 0.5, arrived[1, own, :].astype(F32), 0.0)
        )

    def start(copy):
        copy.start()

    def sent(copy):
        copy.wait_send()

    x_half = pl.ds(pl.multiple_of(t * H, H), H)
    for m in (1, 2):
        ag_peer(AG_X, xall, m, x_h.at[x_half]).start()
    for d in range(1, Z):
        z_gain(d).start()
    local = [
        pltpu.make_async_copy(x_h, xall.at[block(c)], loc.at[0]),
        pltpu.make_async_copy(gain_h, gslots.at[z], loc.at[1]),
        pltpu.make_async_copy(wa_h, wA.at[zrow(z)], loc.at[2]),
        pltpu.make_async_copy(cot_h, cotall.at[block(c)], loc.at[3]),
    ]
    for one in local:
        one.start()
    local[2].wait()
    gather_send(L_WA, wA, 1, start)
    for i in (0, 1, 3):
        local[i].wait()

    for d in range(1, Z):
        z_recv(Z_GAIN, d, gslots.at[lax.rem(z + Z - d, Z)])
    gains = gslots[0].astype(F32)
    for i in range(1, Z):
        gains = gains + gslots[i].astype(F32)
    gvec[...] = gains[0:8]

    def norm_one(cb):
        def body(i, carry):
            r = pl.ds(pl.multiple_of(cb * R + i * 64, 64), 64)
            hat, _ = norm_stats(xall[r, :].astype(F32))
            n1[r, :] = (hat * gvec[0:1, :]).astype(BF16)
            return carry

        lax.fori_loop(0, R // 64, body, 0)

    norm_one(c)
    for k in range(3):
        part = wm_h[k * UW : (k + 1) * UW, :].astype(F32).T
        wM[zrow(z), k * UW : (k + 1) * UW] = part.astype(BF16)
    gather_step(L_WA, wA, 1)
    ag_near(AG_X, xall)
    for m in (1, 2):
        ag_peer(AG_COT, cotall, m, cot_h.at[x_half]).start()
    for m in (1, 2):
        ag_sibling_half(AG_X, xall, m)
        norm_one(partner(c, m))
    for h in range(2, Z - 1):
        gather_step(L_WA, wA, h)
    gather_send(L_WM, wM, 1, start)
    ag_far(AG_X, xall)
    ag_sibling_half(AG_X, xall, 3)
    norm_one(partner(c, 3))

    segr[...] = segc_r[...].T[0:8, :]

    ag_near(AG_COT, cotall)
    gather_step(L_WA, wA, Z - 1)

    def project(cb, carry):
        b = block(cb)
        proj = dot(n1[b, :], wA[:, 0 : 3 * PW]).astype(BF16)
        cos, sin = cos_r[b, :], sin_r[b, :]
        qf = proj[:, 0:PW].astype(F32)
        kf = proj[:, PW : 2 * PW].astype(F32)
        q_rot = (qf * cos + swap_halves(qf) * sin).astype(BF16).astype(F32) * (HD**-0.5)
        k_rot = (kf * cos + swap_halves(kf) * sin).astype(BF16)
        val = proj[:, 2 * PW : 3 * PW]
        q_s[b, :] = q_rot.astype(BF16)
        k_s[b, :] = k_rot
        v_s[b, :] = val
        kT[:, b] = k_rot.astype(F32).T.astype(BF16)
        vT[:, b] = val.astype(F32).T.astype(BF16)
        return carry

    lax.fori_loop(0, N, project, 0)

    lane = lax.broadcasted_iota(jnp.int32, (R, PW), 1)

    def only(u, h):
        return jnp.where(lax.div(lane, HD) == h, u, jnp.zeros_like(u))

    def attend(cb):
        b = block(cb)
        same = segc_r[:, 0:1] == segr[0:1, b]
        for h in range(heads):
            s = dot(k_s[...], only(q_s[b, :], h), 1, 1)
            s = jnp.where(same, s, MASK_FILL)
            e = jnp.exp(s - jnp.max(s, axis=0, keepdims=True))
            inv = 1.0 / jnp.sum(e, axis=0, keepdims=True)
            eb = e.astype(BF16)
            eT[h, cb] = eb
            inv_r[h : h + 1, b] = inv
            hr = slice(h * HD, (h + 1) * HD)
            attnT[hr, b] = (dot(vT[hr, :], eb) * inv).astype(BF16)
        attn[b, :] = attnT[:, b].astype(F32).T.astype(BF16)

    def part_attn(cb, half):
        return dot(attn[rows(cb, half), :], wA[:, 3 * PW :], 1, 1)

    def attend_begin(m):
        attend(partner(c, m))
        rs_begin(RS_ATTN, m, part_attn)

    attend_begin(3)
    attend_begin(2)
    rs_far(RS_ATTN)
    attend_begin(1)
    gather_step(L_WM, wM, 1)
    rs_near(RS_ATTN)
    attend_begin(0)
    rs_joined(RS_ATTN)
    rs_own(RS_ATTN)
    ag_far(AG_COT, cotall)
    mixed1[...] = xall[rows(c, t), :].astype(F32) + rs_end(RS_ATTN)

    hat2, inv2 = norm_stats(mixed1[...])
    n2[rows(c, t), :] = (hat2 * gvec[1:2, :]).astype(BF16)
    for m in (1, 2):
        ag_peer(AG_N2, n2, m).start()
    ag_sib(AG_N2, n2, 0).start()
    for h in range(2, Z):
        gather_step(L_WM, wM, h)
    for m in (1, 2, 3):
        ag_sibling_half(AG_COT, cotall, m)

    def mlp(cb):
        b = block(cb)
        pair = dot(n2[b, :], wM[:, 0 : 2 * UW])
        grad_h = dot(cotall[b, :], wM[:, 2 * UW :])
        a, g = pair[:, :UW], pair[:, UW:]
        cdf = 0.5 * (1.0 + lax.erf(a * INV_ROOT_TWO))
        gelu = a * cdf
        hid[b, :] = (gelu * g).astype(BF16)
        slope = cdf + a * jnp.exp(-0.5 * a * a) * INV_ROOT_TWO_PI
        gpair[b, 0:UW] = (grad_h * g * slope).astype(BF16)
        gpair[b, UW:] = (grad_h * gelu).astype(BF16)

    def part_gn2(cb, half):
        return dot(gpair[rows(cb, half), :], wM[:, 0 : 2 * UW], 1, 1)

    def part_out(cb, half):
        return dot(hid[rows(cb, half), :], wM[:, 2 * UW :], 1, 1)

    def mlp_at(m):
        ag_sibling_half(AG_N2, n2, m)
        mlp(partner(c, m))

    mlp_at(0)
    rs_begin(RS_GN2, 0, part_gn2)
    ag_near(AG_N2, n2)
    mlp_at(1)
    rs_begin(RS_GN2, 1, part_gn2)
    rs_own(RS_GN2)
    ag_far(AG_N2, n2)
    mlp_at(3)
    rs_begin(RS_GN2, 3, part_gn2)
    mlp_at(2)
    rs_far(RS_GN2)
    rs_begin(RS_GN2, 2, part_gn2)
    rs_near(RS_GN2)
    rs_joined(RS_GN2)

    def grads_down(i, carry):
        col = pl.ds(pl.multiple_of(i * CH, CH), CH)
        gDst[col, :] = dot(cotall[:, col], hid[...], 0, 0).astype(BF16)
        return carry

    def grads_in(i, carry):
        col = pl.ds(pl.multiple_of(i * CH, CH), CH)
        gIst[col, :] = dot(n2[:, col], gpair[...], 0, 0).astype(BF16)
        return carry

    lax.fori_loop(0, D // CH, grads_down, 0)
    def scatter_ends(kind):
        for k in range(Z - 1):
            for side in (0, 1):

                def use(j, side=side):
                    @pl.when((z == Z - 1) if side else (z == 0))
                    def _():
                        scatter_copy(kind, side, j).start()

                scatter_each(k, side, use)

    scatter_ends(L_GDOWN)
    lax.fori_loop(0, D // CH, grads_in, 0)
    scatter_ends(L_GIN)

    hat2, inv2 = norm_stats(mixed1[...])
    back2, gg_mlp = norm_back(rs_end(RS_GN2), hat2, inv2, gvec[1:2, :])
    ggst[0, 1:2, :] = gg_mlp
    gmixed[...] = cotall[rows(c, t), :].astype(F32) + back2
    gm[rows(c, t), :] = gmixed[...].astype(BF16)
    for m in (1, 2):
        ag_peer(AG_GM, gm, m).start()
    ag_sib(AG_GM, gm, 0).start()
    scatter_step(L_GDOWN, 0)
    rs_begin(RS_OUT, 3, part_out)
    rs_begin(RS_OUT, 2, part_out)
    for k in range(1, Z - 1):
        scatter_step(L_GDOWN, k)
    rs_begin(RS_OUT, 1, part_out)
    rs_begin(RS_OUT, 0, part_out)

    def fin(kind, m, own, out):
        return rcopy(own, out.at[c], f_s.at[kind, m], f_r.at[kind, m], {"ctx": partner(c, m)})

    def own_copy(kind, own, out):
        return pltpu.make_async_copy(own, out.at[c], loc.at[kind])

    def finish(kind):
        own, out = finals[kind]
        own[...] = scatter_total(kind).astype(BF16)
        for m in (1, 2):
            fin(kind, m, own, out).start()
        own_copy(kind, own, out).start()

    def fin_relay(kind):
        there = finals[kind][1].at[partner(c, via)]
        return rcopy(
            there, there, f_s.at[kind, 3], f_r.at[kind, 3], {"ctx": partner(c, onto)}
        )

    def fin_arrive(kind, m):
        there = finals[kind][1].at[partner(c, m)]
        rcopy(there, there, f_s.at[kind, m], f_r.at[kind, m], {"ctx": partner(c, onto)}).wait_recv()

    def pass_on(kind):
        fin_arrive(kind, via)
        fin_relay(kind).start()

    finals = ((gIf, gi_o), (gDf, gd_o), (gAf, ga_o))

    gk[...] = jnp.zeros_like(gk)
    gv[...] = jnp.zeros_like(gv)

    def rotate_back(g, b):
        return g * cos_r[b, :] + swap_halves(g * sin_r[b, :])

    def attend_back(cb):
        b = block(cb)
        g = dot(gm[b, :], wA[:, 3 * PW :]).astype(BF16)
        gT = g.astype(F32).T
        scaled = []
        grad_q = []
        for h in range(heads):
            hr = slice(h * HD, (h + 1) * HD)
            inv = inv_r[h : h + 1, b]
            delta = jnp.sum(gT[hr, :] * attnT[hr, b].astype(F32), axis=0, keepdims=True)
            gp = dot(v_s[...], only(g, h), 1, 1)
            ds = (eT[h, cb].astype(F32) * ((gp - delta) * inv)).astype(BF16)
            grad_q.append(dot(kT[hr, :], ds))
            gk[...] += dot(ds, only(q_s[b, :], h))
            scaled.append(gT[hr, :] * inv)
        gs = jnp.concatenate(scaled, axis=0).T.astype(BF16)
        for h in range(heads):
            gv[...] += dot(eT[h, cb], only(gs, h))
        gq = jnp.concatenate(grad_q, axis=0).T * (HD**-0.5)
        gproj[b, 0:PW] = rotate_back(gq, b).astype(BF16)

    for m in (0, 1, 2, 3):
        if m == 0:
            ag_near(AG_GM, gm)
        if m == 2:
            ag_far(AG_GM, gm)
        ag_sibling_half(AG_GM, gm, m)
        attend_back(partner(c, m))
        if m == 1:
            finish(L_GDOWN)
            rs_far(RS_OUT)
            rs_near(RS_OUT)
        if m == 2:
            scatter_step(L_GIN, 0)
    rs_joined(RS_OUT)
    rs_own(RS_OUT)

    def unrotate(cb, carry):
        b = block(cb)
        gproj[b, PW : 2 * PW] = rotate_back(gk[b, :], b).astype(BF16)
        gproj[b, 2 * PW :] = gv[b, :].astype(BF16)
        return carry

    lax.fori_loop(0, N, unrotate, 0)

    def grads_attn(i, carry):
        col = pl.ds(pl.multiple_of(i * CH, CH), CH)
        gAst[col, 0 : 3 * PW] = dot(n1[:, col], gproj[...], 0, 0).astype(BF16)
        gAst[col, 3 * PW :] = dot(gm[:, col], attn[...], 0, 0).astype(BF16)
        return carry

    lax.fori_loop(0, D // CH, grads_attn, 0)
    scatter_ends(L_GWA)
    for k in range(1, Z - 1):
        scatter_step(L_GIN, k)

    def part_gn1(cb, half):
        return dot(gproj[rows(cb, half), :], wA[:, 0 : 3 * PW], 1, 1)

    rs_begin(RS_GN1, 3, part_gn1)
    rs_begin(RS_GN1, 2, part_gn1)
    rs_far(RS_GN1)
    pass_on(L_GDOWN)
    rs_begin(RS_GN1, 1, part_gn1)
    rs_near(RS_GN1)
    rs_begin(RS_GN1, 0, part_gn1)
    rs_joined(RS_GN1)
    rs_own(RS_GN1)

    finish(L_GIN)
    scatter_step(L_GWA, 0)

    hat1, inv1 = norm_stats(xall[rows(c, t), :].astype(F32))
    back1, gg_attn = norm_back(rs_end(RS_GN1), hat1, inv1, gvec[0:1, :])
    ggst[0, 0:1, :] = gg_attn
    gtok_o[x_half, :] = gmixed[...] + back1
    swap_tok = rcopy(
        gtok_o.at[x_half], gtok_o.at[x_half], sw_s.at[0], sw_r.at[0], {"tensor": o}
    )
    swap_tok.start()

    ggst[0, 2:8, :] = jnp.zeros_like(ggst[0, 2:8, :])
    gg0 = rcopy(ggst.at[0], ggrv.at[0], gg_s.at[0], gg_r.at[0], {"tensor": o})
    gg0.start()

    for k in range(1, Z - 1):
        scatter_step(L_GWA, k)
    out_o[x_half, :] = (mixed1[...] + rs_end(RS_OUT)).astype(BF16)
    swap_out = rcopy(
        out_o.at[x_half], out_o.at[x_half], sw_s.at[1], sw_r.at[1], {"tensor": o}
    )
    swap_out.start()
    gg0.wait_recv()
    ggst[1] = ggst[0] + ggrv[0]

    def gg_ctx(m):
        return rcopy(ggst.at[1], ggrv.at[m], gg_s.at[m], gg_r.at[m], {"ctx": partner(c, m)})

    for m in (1, 2, 3):
        gg_ctx(m).start()

    for m in (1, 2, 3):
        gg_ctx(m).wait_recv()
    ggst[2] = (ggst[1] + ggrv[1]) + (ggrv[2] + ggrv[3])

    def gg_z(d):
        return z_copy(Z_GG, d, ggst.at[2], ggrv.at[3 + d])

    for d in range(1, Z):
        gg_z(d).start()
    pass_on(L_GIN)
    finish(L_GWA)
    total = ggst[2]
    for d in range(1, Z):
        z_recv(Z_GG, d, ggrv.at[3 + d])
        total = total + ggrv[3 + d]
    gain_o[...] = total
    pass_on(L_GWA)

    other = pl.ds(pl.multiple_of(o * H, H), H)
    rcopy(gtok_o.at[other], gtok_o.at[other], sw_s.at[0], sw_r.at[0], {"tensor": o}).wait_recv()
    rcopy(out_o.at[other], out_o.at[other], sw_s.at[1], sw_r.at[1], {"tensor": o}).wait_recv()
    for kind, (own, out) in enumerate(finals):
        fin_arrive(kind, onto)
        fin_arrive(kind, 3)
        fin_relay(kind).wait_send()
        for m in (1, 2):
            fin(kind, m, own, out).wait_send()
    for m in (1, 2, 3):
        gg_ctx(m).wait_send()
    for kind, (own, out) in enumerate(finals):
        own_copy(kind, own, out).wait()
    gg0.wait_send()
    swap_tok.wait_send()
    swap_out.wait_send()
    for m in (1, 2):
        ag_peer(AG_X, xall, m, x_h.at[x_half]).wait_send()
        ag_peer(AG_COT, cotall, m, cot_h.at[x_half]).wait_send()
        ag_peer(AG_N2, n2, m).wait_send()
        ag_peer(AG_GM, gm, m).wait_send()
    for kind, buf in ((AG_X, xall), (AG_COT, cotall), (AG_N2, n2), (AG_GM, gm)):
        ag_relay(kind, buf).wait_send()
    for m in (1, 2, 3):
        for kind in range(4):
            rs_peer(kind, m, onto).wait_send()
        ag_sib(AG_X, xall, m).wait_send()
        ag_sib(AG_COT, cotall, m).wait_send()
    for m in range(4):
        ag_sib(AG_N2, n2, m).wait_send()
        ag_sib(AG_GM, gm, m).wait_send()
        for kind in range(4):
            rs_sib(kind, m).wait_send()
    for d in range(1, Z):
        z_gain(d).wait_send()
        gg_z(d).wait_send()
        gather_send(L_WA, wA, d, sent)
        gather_send(L_WM, wM, d, sent)
    for kind in (L_GIN, L_GDOWN, L_GWA):
        for k in range(Z - 1):
            for side in (0, 1):
                scatter_each(k, side, lambda j, side=side: sent(scatter_copy(kind, side, j)))


def spread_kernel(ga, gi, gd, tok_i, gtok_i, qkv_o, out_o, in_o, down_o, tok_o, gtok_o):
    width, units = out_o.shape[0], down_o.shape[0]
    for k in range(3):
        qkv_o[k] = ga[:, k * width : (k + 1) * width].astype(F32)
    out_o[...] = ga[:, 3 * width :].astype(F32).T
    for k in range(2):
        in_o[k] = gi[:, k * units : (k + 1) * units].astype(F32).T
    down_o[...] = gd[...].astype(F32).T
    tok_o[...] = tok_i[...]
    gtok_o[...] = gtok_i[...]


def tables(doc_len, span_len):
    count = doc_len.shape[0]
    upto = jnp.arange(count)[:, None] >= jnp.arange(count)[None, :]
    doc_end = jnp.sum(jnp.where(upto, doc_len[None, :], 0), axis=1)
    doc_start = doc_end - doc_len
    places = jnp.arange(span_len, dtype=jnp.int32)
    begins = jnp.max(
        jnp.where(places[:, None] >= doc_start[None, :], doc_start[None, :], 0), axis=1
    )
    segment = jnp.sum((places[:, None] >= doc_end[None, :]).astype(jnp.int32), axis=1)
    offset = (places - begins).astype(F32)
    half = HD // 2
    place = jnp.arange(LANES, dtype=jnp.int32)
    frequency = ROPE_BASE ** (-((place % half).astype(F32) * (2.0 / HD)))
    turn = jnp.where(place % HD < half, -1.0, 1.0)
    angles = offset[:, None] * frequency[None, :]
    seg = jnp.broadcast_to(segment.astype(F32)[:, None], (span_len, LANES))
    return jnp.cos(angles), jnp.sin(angles) * turn[None, :], seg


def local(ways, tokens, doc_lengths, gain_attn, w_qkv, w_attn_out, gain_mlp, w_in, w_mlp_out, cotangent):
    Z, N = ways
    ci, zi = lax.axis_index("ctx"), lax.axis_index("dp")
    R, D = tokens.shape
    S = R * N
    H = R // 2
    Dz, width = w_qkv.shape[1:]
    units = w_in.shape[2]
    PW = width // N
    UW = -(-units // (N * LANES)) * LANES
    padded = UW * N

    qkv = lax.dynamic_slice_in_dim(w_qkv, ci * PW, PW, 2)
    w_out = lax.dynamic_slice_in_dim(w_attn_out, ci * PW, PW, 0).T
    wa = jnp.concatenate([qkv[0], qkv[1], qkv[2], w_out], axis=1)
    w_up = jnp.pad(w_in.transpose(0, 2, 1), ((0, 0), (0, padded - units), (0, 0)))
    w_up = lax.dynamic_slice_in_dim(w_up, ci * UW, UW, 1)
    w_down = jnp.pad(w_mlp_out, ((0, padded - units), (0, 0)))
    w_down = lax.dynamic_slice_in_dim(w_down, ci * UW, UW, 0)
    wm = jnp.concatenate([w_up[0], w_up[1], w_down], axis=0)
    gains = lax.dynamic_update_slice(
        jnp.zeros((16, D), BF16), jnp.stack([gain_attn, gain_mlp]), (0, zi * Dz)
    )
    cos, sin, seg = tables(doc_lengths[0], S)

    anywhere = pl.BlockSpec(memory_space=pl.ANY)
    vmem = pl.BlockSpec(memory_space=pltpu.VMEM)
    V = pltpu.VMEM
    dma = pltpu.SemaphoreType.DMA
    scratch = [
        V((S, D), BF16), V((S, D), BF16), V((S, D), BF16), V((S, D), BF16), V((S, D), BF16),
        V((Z, 16, D), BF16), V((D, 4 * PW), BF16), V((D, 3 * UW), BF16),
        V((S, PW), BF16), V((S, PW), BF16), V((S, PW), BF16), V((PW, S), BF16), V((PW, S), BF16),
        V((S, PW), BF16), V((PW, S), BF16), V((PW // HD, N, S, R), BF16), V((8, S), F32),
        V((2, N, H, D), F32), V((4, N, H, D), BF16), V((4, N, H, D), BF16), V((4, N - 1, H, D), BF16),
        V((4, N - 1, H, D), BF16), V((S, UW), BF16), V((S, 2 * UW), BF16),
        V((D, 2 * UW), BF16), V((2, D, 2 * UW), BF16), V((D, UW), BF16), V((2, D, UW), BF16),
        V((D, 4 * PW), BF16), V((2, D, 4 * PW), BF16),
        V((Dz, 2 * UW), BF16), V((Dz, UW), BF16), V((Dz, 4 * PW), BF16),
        V((H, D), F32), V((H, D), F32), V((S, 3 * PW), BF16), V((S, PW), F32), V((S, PW), F32),
        V((8, D), F32), V((3, 8, D), F32), V((3 + Z, 8, D), F32), V((8, S), F32),
        dma((4, N)), dma((4, N)), dma((4, N)), dma((4, N)), dma((4, N)), dma((4, N)), dma((4, N)),
        dma((4, N)), dma((2, Z)), dma((2, Z)), dma((5, 2, Z)), dma((5, 2, Z)), dma((3, N)), dma((3, N)), dma((2,)), dma((2,)),
        dma((N,)), dma((N,)), dma((5,)),
    ]
    out, gtok, ga, gi, gd, gg = pl.pallas_call(
        functools.partial(layer_kernel, ways),
        out_shape=[
            jax.ShapeDtypeStruct((R, D), BF16),
            jax.ShapeDtypeStruct((R, D), F32),
            jax.ShapeDtypeStruct((N, Dz, 4 * PW), BF16),
            jax.ShapeDtypeStruct((N, Dz, 2 * UW), BF16),
            jax.ShapeDtypeStruct((N, Dz, UW), BF16),
            jax.ShapeDtypeStruct((8, D), F32),
        ],
        in_specs=[anywhere] * 3 + [vmem, anywhere] + [vmem] * 3,
        out_specs=[vmem, vmem, anywhere, anywhere, anywhere, vmem],
        scratch_shapes=scratch,
        compiler_params=pltpu.CompilerParams(
            collective_id=0, has_side_effects=True, vmem_limit_bytes=60 * 1024 * 1024
        ),
        cost_estimate=pl.CostEstimate(
            flops=12 * 10**9, bytes_accessed=12 * 2**20, transcendentals=4 * 10**6
        ),
        name="layer",
    )(tokens, cotangent, wa, wm, gains, cos, sin, seg)

    gains_own = lax.dynamic_slice_in_dim(gg[0:2], zi * Dz, Dz, 1)
    g_qkv, g_out, g_in, g_down, out, gtok = pl.pallas_call(
        spread_kernel,
        grid=(N,),
        out_shape=[
            jax.ShapeDtypeStruct((3, Dz, N * PW), F32),
            jax.ShapeDtypeStruct((N * PW, Dz), F32),
            jax.ShapeDtypeStruct((2, units, Dz), F32),
            jax.ShapeDtypeStruct((units, Dz), F32),
            jax.ShapeDtypeStruct((R, D), BF16),
            jax.ShapeDtypeStruct((R, D), F32),
        ],
        in_specs=[
            pl.BlockSpec((None, Dz, 4 * PW), lambda i: (i, 0, 0)),
            pl.BlockSpec((None, Dz, 2 * UW), lambda i: (i, 0, 0)),
            pl.BlockSpec((None, Dz, UW), lambda i: (i, 0, 0)),
            pl.BlockSpec((R // N, D), lambda i: (i, 0)),
            pl.BlockSpec((R // N, D), lambda i: (i, 0)),
        ],
        out_specs=[
            pl.BlockSpec((3, Dz, PW), lambda i: (0, 0, i)),
            pl.BlockSpec((PW, Dz), lambda i: (i, 0)),
            pl.BlockSpec((2, UW, Dz), lambda i: (0, i, 0)),
            pl.BlockSpec((UW, Dz), lambda i: (i, 0)),
            pl.BlockSpec((R // N, D), lambda i: (i, 0)),
            pl.BlockSpec((R // N, D), lambda i: (i, 0)),
        ],
        compiler_params=pltpu.CompilerParams(vmem_limit_bytes=60 * 1024 * 1024),
        name="spread",
    )(ga, gi, gd, out, gtok)
    g_in = g_in.transpose(0, 2, 1)
    return (out, gtok, gains_own[0], g_qkv, g_out, gains_own[1], g_in, g_down)


def solution(mesh):
    in_specs = (
        P(("dp", "ctx"), None),
        P("dp", None),
        P("dp"),
        P(None, "dp", "tensor"),
        P("tensor", "dp"),
        P("dp"),
        P(None, "dp", "tensor"),
        P("tensor", "dp"),
        P(("dp", "ctx"), None),
    )
    out_specs = (
        P(("dp", "ctx"), None),
        P(("dp", "ctx"), None),
        P("dp"),
        P(None, "dp", "tensor"),
        P("tensor", "dp"),
        P("dp"),
        P(None, "dp", "tensor"),
        P("tensor", "dp"),
    )
    ways = (mesh.shape["dp"], mesh.shape["ctx"])
    return jax.shard_map(
        functools.partial(local, ways),
        mesh=mesh,
        in_specs=in_specs,
        out_specs=out_specs,
        check_vma=False,
    )
```

```python
import functools
import math

import jax
import jax.numpy as jnp
from jax import lax
from jax.experimental import pallas as pl
from jax.experimental.pallas import tpu as pltpu
from jax.sharding import PartitionSpec as P

HD = 64
LANES = 128
NORM_EPS = 1e-05
ROPE_BASE = 160000.0
MASK_FILL = -1e30
INV_ROOT_TWO = 1.0 / math.sqrt(2.0)
INV_ROOT_TWO_PI = 1.0 / math.sqrt(2.0 * math.pi)
MESH = pl.DeviceIdType.MESH
F32 = jnp.float32
BF16 = jnp.bfloat16

AG_X, AG_COT, AG_N2, AG_GM = range(4)
RS_ATTN, RS_GN2, RS_OUT, RS_GN1 = range(4)
Z_GAIN, Z_GG = range(2)
L_GIN, L_GDOWN, L_GWA, L_WA, L_WM = range(5)


def dot(a, b, ca=1, cb=0):
    return lax.dot_general(a, b, (((ca,), (cb,)), ((), ())), preferred_element_type=F32)


def partner(c, m):
    y = lax.rem(lax.div(c, 2) + lax.div(m, 2), 2)
    x = lax.rem(lax.rem(c, 2) + lax.rem(m, 2), 2)
    return y * 2 + x


def swap_halves(u):
    lane = lax.broadcasted_iota(jnp.int32, u.shape, 1)
    first = lax.rem(lane, HD) < HD // 2
    return jnp.where(first, pltpu.roll(u, LANES - HD // 2, 1), pltpu.roll(u, HD // 2, 1))


def norm_stats(v):
    centered = v - jnp.mean(v, axis=-1, keepdims=True)
    inv = lax.rsqrt(jnp.mean(centered * centered, axis=-1, keepdims=True) + NORM_EPS)
    return centered * inv, inv


def norm_back(grad, hat, inv, gain):
    gh = grad * gain
    inner = (
        gh
        - jnp.mean(gh, axis=-1, keepdims=True)
        - hat * jnp.mean(gh * hat, axis=-1, keepdims=True)
    )
    return inv * inner, jnp.sum(grad * hat, axis=0, keepdims=True)


def layer_kernel(
    ways,
    x_h, cot_h, wa_h, wm_h, gain_h, cos_r, sin_r, segc_r,
    out_o, gtok_o, ga_o, gi_o, gd_o, gain_o,
    xall, cotall, n1, n2, gm, gslots, wA, wM, q_s, k_s, v_s, kT, vT, attn, attnT, eT, inv_r,
    acc, sst, srv, pst, prv, hid, gpair, gIst, gIrv, gDst, gDrv, gAst, gArv, gIf, gDf, gAf,
    mixed1, gmixed, gproj, gk, gv, gvec, ggst, ggrv,
    segr, ag_ps, ag_pr, ag_ss, ag_sr, rs_ss, rs_sr, rs_ps, rs_pr, z_s, z_r, l_s, l_r, f_s, f_r, sw_s, sw_r,
    gg_s, gg_r, loc,
):
    Z, N = ways
    z, c, t = lax.axis_index("dp"), lax.axis_index("ctx"), lax.axis_index("tensor")
    o = 1 - t
    via, onto = 1 + t, 2 - t
    R, D = x_h.shape
    H = R // 2
    S = R * N
    Dz = wa_h.shape[0]
    PW = wa_h.shape[1] // 4
    UW = wm_h.shape[0] // 3
    heads = PW // HD
    CH = 256
    gst, grv = (gIst, gDst, gAst), (gIrv, gDrv, gArv)

    def rows(cb, half):
        return pl.ds(pl.multiple_of(cb * R + half * H, H), H)

    def block(cb):
        return pl.ds(pl.multiple_of(cb * R, R), R)

    def rcopy(src, dst, ss, rs, dev):
        return pltpu.make_async_remote_copy(
            src_ref=src, dst_ref=dst, send_sem=ss, recv_sem=rs, device_id=dev, device_id_type=MESH
        )

    bar = pltpu.get_barrier_semaphore()
    for m in range(1, N):
        pl.semaphore_signal(bar, inc=1, device_id={"ctx": partner(c, m)}, device_id_type=MESH)
    pl.semaphore_signal(bar, inc=1, device_id={"tensor": o}, device_id_type=MESH)
    for d in range(1, Z):
        pl.semaphore_signal(bar, inc=1, device_id={"dp": lax.rem(z + d, Z)}, device_id_type=MESH)
    pl.semaphore_wait(bar, N - 1 + 1 + Z - 1)

    def ag_peer(kind, buf, m, src=None):
        own = rows(c, t)
        return rcopy(
            buf.at[own] if src is None else src, buf.at[own], ag_ps.at[kind, m], ag_pr.at[kind, m],
            {"ctx": partner(c, m)},
        )

    def ag_sib(kind, buf, m):
        own = rows(partner(c, m), t)
        return rcopy(
            buf.at[own], buf.at[own], ag_ss.at[kind, m], ag_sr.at[kind, m], {"tensor": o}
        )

    def ag_relay(kind, buf):
        there = buf.at[rows(partner(c, via), t)]
        return rcopy(
            there, there, ag_ps.at[kind, 3], ag_pr.at[kind, 3], {"ctx": partner(c, onto)}
        )

    def ag_arrive(kind, buf, m):
        there = buf.at[rows(partner(c, m), t)]
        rcopy(there, there, ag_ps.at[kind, m], ag_pr.at[kind, m], {"ctx": partner(c, onto)}).wait_recv()

    def ag_near(kind, buf):
        ag_arrive(kind, buf, via)
        ag_relay(kind, buf).start()
        ag_sib(kind, buf, via).start()
        ag_arrive(kind, buf, onto)
        ag_sib(kind, buf, onto).start()

    def ag_far(kind, buf):
        ag_arrive(kind, buf, 3)
        ag_sib(kind, buf, 3).start()

    def ag_sibling_half(kind, buf, m):
        there = buf.at[rows(partner(c, m), o)]
        rcopy(there, there, ag_ss.at[kind, m], ag_sr.at[kind, m], {"tensor": o}).wait_recv()

    def rs_sib(kind, m):
        return rcopy(
            sst.at[kind, m], srv.at[kind, m], rs_ss.at[kind, m], rs_sr.at[kind, m], {"tensor": o}
        )

    def rs_peer(kind, m, to):
        return rcopy(
            pst.at[kind, m - 1], prv.at[kind, m - 1], rs_ps.at[kind, m], rs_pr.at[kind, m],
            {"ctx": partner(c, to)},
        )

    def rs_begin(kind, m, partial):
        cb = partner(c, m)
        sst[kind, m] = partial(cb, o).astype(BF16)
        rs_sib(kind, m).start()
        acc[kind % 2, m] = partial(cb, t)

    def rs_total(kind, m):
        rs_sib(kind, m).wait_recv()
        return acc[kind % 2, m] + srv[kind, m].astype(F32)

    def rs_own(kind):
        acc[kind % 2, 0] = rs_total(kind, 0)

    def rs_far(kind):
        pst[kind, 2] = rs_total(kind, 3).astype(BF16)
        rs_peer(kind, 3, onto).start()

    def rs_near(kind):
        pst[kind, onto - 1] = rs_total(kind, onto).astype(BF16)
        rs_peer(kind, onto, onto).start()

    def rs_joined(kind):
        total = rs_total(kind, via)
        rs_peer(kind, 3, onto).wait_recv()
        pst[kind, via - 1] = (total + prv[kind, 2].astype(F32)).astype(BF16)
        rs_peer(kind, via, via).start()

    def rs_end(kind):
        for m in (1, 2):
            rs_peer(kind, m, m).wait_recv()
        return acc[kind % 2, 0] + prv[kind, 0].astype(F32) + prv[kind, 1].astype(F32)

    def zrow(i):
        return pl.ds(pl.multiple_of(i * Dz, Dz), Dz)

    def z_copy(kind, d, src, dst):
        return rcopy(
            src, dst, z_s.at[kind, d], z_r.at[kind, d], {"dp": lax.rem(z + d, Z)}
        )

    def z_recv(kind, d, dst):
        rcopy(dst, dst, z_s.at[kind, d], z_r.at[kind, d], {"dp": lax.rem(z + d, Z)}).wait_recv()

    def z_gain(d):
        return z_copy(Z_GAIN, d, gain_h, gslots.at[z])

    right, left = lax.rem(z + 1, Z), lax.rem(z + Z - 1, Z)

    def line_copy(kind, side, at, src, dst):
        return rcopy(
            src, dst, l_s.at[kind, side, at], l_r.at[kind, side, at],
            {"dp": left if side else right},
        )

    def gather_send(kind, buf, h, act):
        for side in (0, 1):
            src = z + (h - 1) if side else z - (h - 1)
            ok = (src < Z) & (z > 0) if side else (src >= 0) & (z < Z - 1)

            @pl.when(ok)
            def _():
                there = buf.at[zrow(src)]
                act(line_copy(kind, side, h, there, there))

    def gather_step(kind, buf, h):
        for side in (0, 1):
            src = z + h if side else z - h

            @pl.when((src < Z) if side else (src >= 0))
            def _():
                there = buf.at[zrow(src)]
                line_copy(kind, side, h, there, there).wait_recv()

        if h + 1 < Z:
            gather_send(kind, buf, h + 1, start)

    def scatter_copy(kind, d):
        to = lax.rem(z + d, Z)
        return rcopy(
            gst[kind].at[zrow(to)], grv[kind].at[d], l_s.at[kind, 0, d], l_r.at[kind, 0, d],
            {"dp": to},
        )

    def scatter_start(kind):
        for d in range(1, Z):
            scatter_copy(kind, d).start()

    def scatter_total(kind):
        total = gst[kind][zrow(z), :].astype(F32)
        for d in range(1, Z):
            scatter_copy(kind, d).wait_recv()
            total = total + grv[kind][d].astype(F32)
        return total

    def start(copy):
        copy.start()

    def sent(copy):
        copy.wait_send()

    x_half = pl.ds(pl.multiple_of(t * H, H), H)
    for m in (1, 2):
        ag_peer(AG_X, xall, m, x_h.at[x_half]).start()
    for d in range(1, Z):
        z_gain(d).start()
    local = [
        pltpu.make_async_copy(x_h, xall.at[block(c)], loc.at[0]),
        pltpu.make_async_copy(gain_h, gslots.at[z], loc.at[1]),
        pltpu.make_async_copy(wa_h, wA.at[zrow(z)], loc.at[2]),
        pltpu.make_async_copy(cot_h, cotall.at[block(c)], loc.at[3]),
    ]
    for one in local:
        one.start()
    local[2].wait()
    gather_send(L_WA, wA, 1, start)
    for i in (0, 1, 3):
        local[i].wait()

    for d in range(1, Z):
        z_recv(Z_GAIN, d, gslots.at[lax.rem(z + Z - d, Z)])
    gains = gslots[0].astype(F32)
    for i in range(1, Z):
        gains = gains + gslots[i].astype(F32)
    gvec[...] = gains[0:8]

    def norm_one(cb):
        def body(i, carry):
            r = pl.ds(pl.multiple_of(cb * R + i * 64, 64), 64)
            hat, _ = norm_stats(xall[r, :].astype(F32))
            n1[r, :] = (hat * gvec[0:1, :]).astype(BF16)
            return carry

        lax.fori_loop(0, R // 64, body, 0)

    norm_one(c)
    for k in range(3):
        part = wm_h[k * UW : (k + 1) * UW, :].astype(F32).T
        wM[zrow(z), k * UW : (k + 1) * UW] = part.astype(BF16)
    gather_step(L_WA, wA, 1)
    ag_near(AG_X, xall)
    for m in (1, 2):
        ag_peer(AG_COT, cotall, m, cot_h.at[x_half]).start()
    for m in (1, 2):
        ag_sibling_half(AG_X, xall, m)
        norm_one(partner(c, m))
    for h in range(2, Z - 1):
        gather_step(L_WA, wA, h)
    gather_send(L_WM, wM, 1, start)
    ag_far(AG_X, xall)
    ag_sibling_half(AG_X, xall, 3)
    norm_one(partner(c, 3))

    segr[...] = segc_r[...].T[0:8, :]

    ag_near(AG_COT, cotall)
    gather_step(L_WA, wA, Z - 1)

    def project(cb, carry):
        b = block(cb)
        proj = dot(n1[b, :], wA[:, 0 : 3 * PW]).astype(BF16)
        cos, sin = cos_r[b, :], sin_r[b, :]
        qf = proj[:, 0:PW].astype(F32)
        kf = proj[:, PW : 2 * PW].astype(F32)
        q_rot = (qf * cos + swap_halves(qf) * sin).astype(BF16).astype(F32) * (HD**-0.5)
        k_rot = (kf * cos + swap_halves(kf) * sin).astype(BF16)
        val = proj[:, 2 * PW : 3 * PW]
        q_s[b, :] = q_rot.astype(BF16)
        k_s[b, :] = k_rot
        v_s[b, :] = val
        kT[:, b] = k_rot.astype(F32).T.astype(BF16)
        vT[:, b] = val.astype(F32).T.astype(BF16)
        return carry

    lax.fori_loop(0, N, project, 0)

    lane = lax.broadcasted_iota(jnp.int32, (R, PW), 1)

    def only(u, h):
        return jnp.where(lax.div(lane, HD) == h, u, jnp.zeros_like(u))

    def attend(cb):
        b = block(cb)
        same = segc_r[:, 0:1] == segr[0:1, b]
        for h in range(heads):
            s = dot(k_s[...], only(q_s[b, :], h), 1, 1)
            s = jnp.where(same, s, MASK_FILL)
            e = jnp.exp(s - jnp.max(s, axis=0, keepdims=True))
            inv = 1.0 / jnp.sum(e, axis=0, keepdims=True)
            eb = e.astype(BF16)
            eT[h, cb] = eb
            inv_r[h : h + 1, b] = inv
            hr = slice(h * HD, (h + 1) * HD)
            attnT[hr, b] = (dot(vT[hr, :], eb) * inv).astype(BF16)
        attn[b, :] = attnT[:, b].astype(F32).T.astype(BF16)

    def part_attn(cb, half):
        return dot(attn[rows(cb, half), :], wA[:, 3 * PW :], 1, 1)

    def attend_begin(m):
        attend(partner(c, m))
        rs_begin(RS_ATTN, m, part_attn)

    attend_begin(3)
    attend_begin(2)
    rs_far(RS_ATTN)
    attend_begin(1)
    gather_step(L_WM, wM, 1)
    rs_near(RS_ATTN)
    attend_begin(0)
    rs_joined(RS_ATTN)
    rs_own(RS_ATTN)
    ag_far(AG_COT, cotall)
    mixed1[...] = xall[rows(c, t), :].astype(F32) + rs_end(RS_ATTN)

    hat2, inv2 = norm_stats(mixed1[...])
    n2[rows(c, t), :] = (hat2 * gvec[1:2, :]).astype(BF16)
    for m in (1, 2):
        ag_peer(AG_N2, n2, m).start()
    ag_sib(AG_N2, n2, 0).start()
    for h in range(2, Z):
        gather_step(L_WM, wM, h)
    for m in (1, 2, 3):
        ag_sibling_half(AG_COT, cotall, m)

    def mlp(cb):
        b = block(cb)
        pair = dot(n2[b, :], wM[:, 0 : 2 * UW])
        grad_h = dot(cotall[b, :], wM[:, 2 * UW :])
        a, g = pair[:, :UW], pair[:, UW:]
        cdf = 0.5 * (1.0 + lax.erf(a * INV_ROOT_TWO))
        gelu = a * cdf
        hid[b, :] = (gelu * g).astype(BF16)
        slope = cdf + a * jnp.exp(-0.5 * a * a) * INV_ROOT_TWO_PI
        gpair[b, 0:UW] = (grad_h * g * slope).astype(BF16)
        gpair[b, UW:] = (grad_h * gelu).astype(BF16)

    def part_gn2(cb, half):
        return dot(gpair[rows(cb, half), :], wM[:, 0 : 2 * UW], 1, 1)

    def part_out(cb, half):
        return dot(hid[rows(cb, half), :], wM[:, 2 * UW :], 1, 1)

    def mlp_at(m):
        ag_sibling_half(AG_N2, n2, m)
        mlp(partner(c, m))

    mlp_at(0)
    rs_begin(RS_GN2, 0, part_gn2)
    ag_near(AG_N2, n2)
    mlp_at(1)
    rs_begin(RS_GN2, 1, part_gn2)
    rs_own(RS_GN2)
    ag_far(AG_N2, n2)
    mlp_at(3)
    rs_begin(RS_GN2, 3, part_gn2)
    mlp_at(2)
    rs_far(RS_GN2)
    rs_begin(RS_GN2, 2, part_gn2)

    def grads_down(i, carry):
        col = pl.ds(pl.multiple_of(i * CH, CH), CH)
        gDst[col, :] = dot(cotall[:, col], hid[...], 0, 0).astype(BF16)
        return carry

    lax.fori_loop(0, D // CH, grads_down, 0)
    scatter_start(L_GDOWN)
    rs_near(RS_GN2)
    rs_joined(RS_GN2)

    def grads_in(i, carry):
        col = pl.ds(pl.multiple_of(i * CH, CH), CH)
        gIst[col, :] = dot(n2[:, col], gpair[...], 0, 0).astype(BF16)
        return carry

    lax.fori_loop(0, D // CH, grads_in, 0)
    scatter_start(L_GIN)

    hat2, inv2 = norm_stats(mixed1[...])
    back2, gg_mlp = norm_back(rs_end(RS_GN2), hat2, inv2, gvec[1:2, :])
    ggst[0, 1:2, :] = gg_mlp
    gmixed[...] = cotall[rows(c, t), :].astype(F32) + back2
    gm[rows(c, t), :] = gmixed[...].astype(BF16)
    for m in (1, 2):
        ag_peer(AG_GM, gm, m).start()
    ag_sib(AG_GM, gm, 0).start()
    rs_begin(RS_OUT, 3, part_out)
    rs_begin(RS_OUT, 2, part_out)
    rs_begin(RS_OUT, 1, part_out)
    rs_begin(RS_OUT, 0, part_out)

    def fin(kind, m, own, out):
        return rcopy(own, out.at[c], f_s.at[kind, m], f_r.at[kind, m], {"ctx": partner(c, m)})

    def own_copy(kind, own, out):
        return pltpu.make_async_copy(own, out.at[c], loc.at[kind])

    def finish(kind):
        own, out = finals[kind]
        own[...] = scatter_total(kind).astype(BF16)
        for m in (1, 2):
            fin(kind, m, own, out).start()
        own_copy(kind, own, out).start()

    def fin_relay(kind):
        there = finals[kind][1].at[partner(c, via)]
        return rcopy(
            there, there, f_s.at[kind, 3], f_r.at[kind, 3], {"ctx": partner(c, onto)}
        )

    def fin_arrive(kind, m):
        there = finals[kind][1].at[partner(c, m)]
        rcopy(there, there, f_s.at[kind, m], f_r.at[kind, m], {"ctx": partner(c, onto)}).wait_recv()

    def pass_on(kind):
        fin_arrive(kind, via)
        fin_relay(kind).start()

    finals = ((gIf, gi_o), (gDf, gd_o), (gAf, ga_o))

    gk[...] = jnp.zeros_like(gk)
    gv[...] = jnp.zeros_like(gv)

    def rotate_back(g, b):
        return g * cos_r[b, :] + swap_halves(g * sin_r[b, :])

    def attend_back(cb):
        b = block(cb)
        g = dot(gm[b, :], wA[:, 3 * PW :]).astype(BF16)
        gT = g.astype(F32).T
        scaled = []
        grad_q = []
        for h in range(heads):
            hr = slice(h * HD, (h + 1) * HD)
            inv = inv_r[h : h + 1, b]
            delta = jnp.sum(gT[hr, :] * attnT[hr, b].astype(F32), axis=0, keepdims=True)
            gp = dot(v_s[...], only(g, h), 1, 1)
            ds = (eT[h, cb].astype(F32) * ((gp - delta) * inv)).astype(BF16)
            grad_q.append(dot(kT[hr, :], ds))
            gk[...] += dot(ds, only(q_s[b, :], h))
            scaled.append(gT[hr, :] * inv)
        gs = jnp.concatenate(scaled, axis=0).T.astype(BF16)
        for h in range(heads):
            gv[...] += dot(eT[h, cb], only(gs, h))
        gq = jnp.concatenate(grad_q, axis=0).T * (HD**-0.5)
        gproj[b, 0:PW] = rotate_back(gq, b).astype(BF16)

    for m in (0, 1, 2, 3):
        if m == 0:
            ag_near(AG_GM, gm)
        if m == 2:
            ag_far(AG_GM, gm)
        ag_sibling_half(AG_GM, gm, m)
        attend_back(partner(c, m))
        if m == 1:
            rs_far(RS_OUT)
            rs_near(RS_OUT)
    rs_joined(RS_OUT)
    rs_own(RS_OUT)

    def unrotate(cb, carry):
        b = block(cb)
        gproj[b, PW : 2 * PW] = rotate_back(gk[b, :], b).astype(BF16)
        gproj[b, 2 * PW :] = gv[b, :].astype(BF16)
        return carry

    lax.fori_loop(0, N, unrotate, 0)

    def grads_attn(i, carry):
        col = pl.ds(pl.multiple_of(i * CH, CH), CH)
        gAst[col, 0 : 3 * PW] = dot(n1[:, col], gproj[...], 0, 0).astype(BF16)
        gAst[col, 3 * PW :] = dot(gm[:, col], attn[...], 0, 0).astype(BF16)
        return carry

    lax.fori_loop(0, D // CH, grads_attn, 0)
    scatter_start(L_GWA)
    finish(L_GDOWN)

    def part_gn1(cb, half):
        return dot(gproj[rows(cb, half), :], wA[:, 0 : 3 * PW], 1, 1)

    rs_begin(RS_GN1, 3, part_gn1)
    rs_begin(RS_GN1, 2, part_gn1)
    rs_far(RS_GN1)
    pass_on(L_GDOWN)
    rs_begin(RS_GN1, 1, part_gn1)
    rs_near(RS_GN1)
    rs_begin(RS_GN1, 0, part_gn1)
    rs_joined(RS_GN1)
    rs_own(RS_GN1)

    finish(L_GIN)

    hat1, inv1 = norm_stats(xall[rows(c, t), :].astype(F32))
    back1, gg_attn = norm_back(rs_end(RS_GN1), hat1, inv1, gvec[0:1, :])
    ggst[0, 0:1, :] = gg_attn
    gtok_o[x_half, :] = gmixed[...] + back1
    swap_tok = rcopy(
        gtok_o.at[x_half], gtok_o.at[x_half], sw_s.at[0], sw_r.at[0], {"tensor": o}
    )
    swap_tok.start()

    ggst[0, 2:8, :] = jnp.zeros_like(ggst[0, 2:8, :])
    gg0 = rcopy(ggst.at[0], ggrv.at[0], gg_s.at[0], gg_r.at[0], {"tensor": o})
    gg0.start()

    out_o[x_half, :] = (mixed1[...] + rs_end(RS_OUT)).astype(BF16)
    swap_out = rcopy(
        out_o.at[x_half], out_o.at[x_half], sw_s.at[1], sw_r.at[1], {"tensor": o}
    )
    swap_out.start()
    gg0.wait_recv()
    ggst[1] = ggst[0] + ggrv[0]

    def gg_ctx(m):
        return rcopy(ggst.at[1], ggrv.at[m], gg_s.at[m], gg_r.at[m], {"ctx": partner(c, m)})

    for m in (1, 2, 3):
        gg_ctx(m).start()

    for m in (1, 2, 3):
        gg_ctx(m).wait_recv()
    ggst[2] = (ggst[1] + ggrv[1]) + (ggrv[2] + ggrv[3])

    def gg_z(d):
        return z_copy(Z_GG, d, ggst.at[2], ggrv.at[3 + d])

    for d in range(1, Z):
        gg_z(d).start()
    pass_on(L_GIN)
    finish(L_GWA)
    total = ggst[2]
    for d in range(1, Z):
        z_recv(Z_GG, d, ggrv.at[3 + d])
        total = total + ggrv[3 + d]
    gain_o[...] = total
    pass_on(L_GWA)

    other = pl.ds(pl.multiple_of(o * H, H), H)
    rcopy(gtok_o.at[other], gtok_o.at[other], sw_s.at[0], sw_r.at[0], {"tensor": o}).wait_recv()
    rcopy(out_o.at[other], out_o.at[other], sw_s.at[1], sw_r.at[1], {"tensor": o}).wait_recv()
    for kind, (own, out) in enumerate(finals):
        fin_arrive(kind, onto)
        fin_arrive(kind, 3)
        fin_relay(kind).wait_send()
        for m in (1, 2):
            fin(kind, m, own, out).wait_send()
    for m in (1, 2, 3):
        gg_ctx(m).wait_send()
    for kind, (own, out) in enumerate(finals):
        own_copy(kind, own, out).wait()
    gg0.wait_send()
    swap_tok.wait_send()
    swap_out.wait_send()
    for m in (1, 2):
        ag_peer(AG_X, xall, m, x_h.at[x_half]).wait_send()
        ag_peer(AG_COT, cotall, m, cot_h.at[x_half]).wait_send()
        ag_peer(AG_N2, n2, m).wait_send()
        ag_peer(AG_GM, gm, m).wait_send()
    for kind, buf in ((AG_X, xall), (AG_COT, cotall), (AG_N2, n2), (AG_GM, gm)):
        ag_relay(kind, buf).wait_send()
    for m in (1, 2, 3):
        for kind in range(4):
            rs_peer(kind, m, onto).wait_send()
        ag_sib(AG_X, xall, m).wait_send()
        ag_sib(AG_COT, cotall, m).wait_send()
    for m in range(4):
        ag_sib(AG_N2, n2, m).wait_send()
        ag_sib(AG_GM, gm, m).wait_send()
        for kind in range(4):
            rs_sib(kind, m).wait_send()
    for d in range(1, Z):
        z_gain(d).wait_send()
        gg_z(d).wait_send()
        gather_send(L_WA, wA, d, sent)
        gather_send(L_WM, wM, d, sent)
        for kind in (L_GIN, L_GDOWN, L_GWA):
            scatter_copy(kind, d).wait_send()


def spread_kernel(ga, gi, gd, tok_i, gtok_i, qkv_o, out_o, in_o, down_o, tok_o, gtok_o):
    width, units = out_o.shape[0], down_o.shape[0]
    for k in range(3):
        qkv_o[k] = ga[:, k * width : (k + 1) * width].astype(F32)
    out_o[...] = ga[:, 3 * width :].astype(F32).T
    for k in range(2):
        in_o[k] = gi[:, k * units : (k + 1) * units].astype(F32).T
    down_o[...] = gd[...].astype(F32).T
    tok_o[...] = tok_i[...]
    gtok_o[...] = gtok_i[...]


def tables(doc_len, span_len):
    count = doc_len.shape[0]
    upto = jnp.arange(count)[:, None] >= jnp.arange(count)[None, :]
    doc_end = jnp.sum(jnp.where(upto, doc_len[None, :], 0), axis=1)
    doc_start = doc_end - doc_len
    places = jnp.arange(span_len, dtype=jnp.int32)
    begins = jnp.max(
        jnp.where(places[:, None] >= doc_start[None, :], doc_start[None, :], 0), axis=1
    )
    segment = jnp.sum((places[:, None] >= doc_end[None, :]).astype(jnp.int32), axis=1)
    offset = (places - begins).astype(F32)
    half = HD // 2
    place = jnp.arange(LANES, dtype=jnp.int32)
    frequency = ROPE_BASE ** (-((place % half).astype(F32) * (2.0 / HD)))
    turn = jnp.where(place % HD < half, -1.0, 1.0)
    angles = offset[:, None] * frequency[None, :]
    seg = jnp.broadcast_to(segment.astype(F32)[:, None], (span_len, LANES))
    return jnp.cos(angles), jnp.sin(angles) * turn[None, :], seg


def local(ways, tokens, doc_lengths, gain_attn, w_qkv, w_attn_out, gain_mlp, w_in, w_mlp_out, cotangent):
    Z, N = ways
    ci, zi = lax.axis_index("ctx"), lax.axis_index("dp")
    R, D = tokens.shape
    S = R * N
    H = R // 2
    Dz, width = w_qkv.shape[1:]
    units = w_in.shape[2]
    PW = width // N
    UW = -(-units // (N * LANES)) * LANES
    padded = UW * N

    qkv = lax.dynamic_slice_in_dim(w_qkv, ci * PW, PW, 2)
    w_out = lax.dynamic_slice_in_dim(w_attn_out, ci * PW, PW, 0).T
    wa = jnp.concatenate([qkv[0], qkv[1], qkv[2], w_out], axis=1)
    w_up = jnp.pad(w_in.transpose(0, 2, 1), ((0, 0), (0, padded - units), (0, 0)))
    w_up = lax.dynamic_slice_in_dim(w_up, ci * UW, UW, 1)
    w_down = jnp.pad(w_mlp_out, ((0, padded - units), (0, 0)))
    w_down = lax.dynamic_slice_in_dim(w_down, ci * UW, UW, 0)
    wm = jnp.concatenate([w_up[0], w_up[1], w_down], axis=0)
    gains = lax.dynamic_update_slice(
        jnp.zeros((16, D), BF16), jnp.stack([gain_attn, gain_mlp]), (0, zi * Dz)
    )
    cos, sin, seg = tables(doc_lengths[0], S)

    anywhere = pl.BlockSpec(memory_space=pl.ANY)
    vmem = pl.BlockSpec(memory_space=pltpu.VMEM)
    V = pltpu.VMEM
    dma = pltpu.SemaphoreType.DMA
    scratch = [
        V((S, D), BF16), V((S, D), BF16), V((S, D), BF16), V((S, D), BF16), V((S, D), BF16),
        V((Z, 16, D), BF16), V((D, 4 * PW), BF16), V((D, 3 * UW), BF16),
        V((S, PW), BF16), V((S, PW), BF16), V((S, PW), BF16), V((PW, S), BF16), V((PW, S), BF16),
        V((S, PW), BF16), V((PW, S), BF16), V((PW // HD, N, S, R), BF16), V((8, S), F32),
        V((2, N, H, D), F32), V((4, N, H, D), BF16), V((4, N, H, D), BF16), V((4, N - 1, H, D), BF16),
        V((4, N - 1, H, D), BF16), V((S, UW), BF16), V((S, 2 * UW), BF16),
        V((D, 2 * UW), BF16), V((Z, Dz, 2 * UW), BF16), V((D, UW), BF16), V((Z, Dz, UW), BF16),
        V((D, 4 * PW), BF16), V((Z, Dz, 4 * PW), BF16),
        V((Dz, 2 * UW), BF16), V((Dz, UW), BF16), V((Dz, 4 * PW), BF16),
        V((H, D), F32), V((H, D), F32), V((S, 3 * PW), BF16), V((S, PW), F32), V((S, PW), F32),
        V((8, D), F32), V((3, 8, D), F32), V((3 + Z, 8, D), F32), V((8, S), F32),
        dma((4, N)), dma((4, N)), dma((4, N)), dma((4, N)), dma((4, N)), dma((4, N)), dma((4, N)),
        dma((4, N)), dma((2, Z)), dma((2, Z)), dma((5, 2, Z)), dma((5, 2, Z)), dma((3, N)), dma((3, N)), dma((2,)), dma((2,)),
        dma((N,)), dma((N,)), dma((5,)),
    ]
    out, gtok, ga, gi, gd, gg = pl.pallas_call(
        functools.partial(layer_kernel, ways),
        out_shape=[
            jax.ShapeDtypeStruct((R, D), BF16),
            jax.ShapeDtypeStruct((R, D), F32),
            jax.ShapeDtypeStruct((N, Dz, 4 * PW), BF16),
            jax.ShapeDtypeStruct((N, Dz, 2 * UW), BF16),
            jax.ShapeDtypeStruct((N, Dz, UW), BF16),
            jax.ShapeDtypeStruct((8, D), F32),
        ],
        in_specs=[anywhere] * 3 + [vmem, anywhere] + [vmem] * 3,
        out_specs=[vmem, vmem, anywhere, anywhere, anywhere, vmem],
        scratch_shapes=scratch,
        compiler_params=pltpu.CompilerParams(
            collective_id=0, has_side_effects=True, vmem_limit_bytes=60 * 1024 * 1024
        ),
        cost_estimate=pl.CostEstimate(
            flops=12 * 10**9, bytes_accessed=12 * 2**20, transcendentals=4 * 10**6
        ),
        name="layer",
    )(tokens, cotangent, wa, wm, gains, cos, sin, seg)

    gains_own = lax.dynamic_slice_in_dim(gg[0:2], zi * Dz, Dz, 1)
    g_qkv, g_out, g_in, g_down, out, gtok = pl.pallas_call(
        spread_kernel,
        grid=(N,),
        out_shape=[
            jax.ShapeDtypeStruct((3, Dz, N * PW), F32),
            jax.ShapeDtypeStruct((N * PW, Dz), F32),
            jax.ShapeDtypeStruct((2, units, Dz), F32),
            jax.ShapeDtypeStruct((units, Dz), F32),
            jax.ShapeDtypeStruct((R, D), BF16),
            jax.ShapeDtypeStruct((R, D), F32),
        ],
        in_specs=[
            pl.BlockSpec((None, Dz, 4 * PW), lambda i: (i, 0, 0)),
            pl.BlockSpec((None, Dz, 2 * UW), lambda i: (i, 0, 0)),
            pl.BlockSpec((None, Dz, UW), lambda i: (i, 0, 0)),
            pl.BlockSpec((R // N, D), lambda i: (i, 0)),
            pl.BlockSpec((R // N, D), lambda i: (i, 0)),
        ],
        out_specs=[
            pl.BlockSpec((3, Dz, PW), lambda i: (0, 0, i)),
            pl.BlockSpec((PW, Dz), lambda i: (i, 0)),
            pl.BlockSpec((2, UW, Dz), lambda i: (0, i, 0)),
            pl.BlockSpec((UW, Dz), lambda i: (i, 0)),
            pl.BlockSpec((R // N, D), lambda i: (i, 0)),
            pl.BlockSpec((R // N, D), lambda i: (i, 0)),
        ],
        compiler_params=pltpu.CompilerParams(vmem_limit_bytes=60 * 1024 * 1024),
        name="spread",
    )(ga, gi, gd, out, gtok)
    g_in = g_in.transpose(0, 2, 1)
    return (out, gtok, gains_own[0], g_qkv, g_out, gains_own[1], g_in, g_down)


def solution(mesh):
    in_specs = (
        P(("dp", "ctx"), None),
        P("dp", None),
        P("dp"),
        P(None, "dp", "tensor"),
        P("tensor", "dp"),
        P("dp"),
        P(None, "dp", "tensor"),
        P("tensor", "dp"),
        P(("dp", "ctx"), None),
    )
    out_specs = (
        P(("dp", "ctx"), None),
        P(("dp", "ctx"), None),
        P("dp"),
        P(None, "dp", "tensor"),
        P("tensor", "dp"),
        P("dp"),
        P(None, "dp", "tensor"),
        P("tensor", "dp"),
    )
    ways = (mesh.shape["dp"], mesh.shape["ctx"])
    return jax.shard_map(
        functools.partial(local, ways),
        mesh=mesh,
        in_specs=in_specs,
        out_specs=out_specs,
        check_vma=False,
    )
```

```python
import functools
import math

import jax
import jax.numpy as jnp
from jax import lax
from jax.experimental import pallas as pl
from jax.experimental.pallas import tpu as pltpu
from jax.sharding import PartitionSpec as P

HD = 64
LANES = 128
NORM_EPS = 1e-05
ROPE_BASE = 160000.0
MASK_FILL = -1e30
INV_ROOT_TWO = 1.0 / math.sqrt(2.0)
INV_ROOT_TWO_PI = 1.0 / math.sqrt(2.0 * math.pi)
MESH = pl.DeviceIdType.MESH
F32 = jnp.float32
BF16 = jnp.bfloat16

AG_X, AG_COT, AG_N2, AG_GM = range(4)
RS_ATTN, RS_GN2, RS_OUT, RS_GN1 = range(4)
Z_GAIN, Z_GG = range(2)
L_GIN, L_GDOWN, L_GWA, L_WA, L_WM = range(5)


def dot(a, b, ca=1, cb=0):
    return lax.dot_general(a, b, (((ca,), (cb,)), ((), ())), preferred_element_type=F32)


def partner(c, m):
    y = lax.rem(lax.div(c, 2) + lax.div(m, 2), 2)
    x = lax.rem(lax.rem(c, 2) + lax.rem(m, 2), 2)
    return y * 2 + x


def swap_halves(u):
    lane = lax.broadcasted_iota(jnp.int32, u.shape, 1)
    first = lax.rem(lane, HD) < HD // 2
    return jnp.where(first, pltpu.roll(u, LANES - HD // 2, 1), pltpu.roll(u, HD // 2, 1))


def norm_stats(v):
    centered = v - jnp.mean(v, axis=-1, keepdims=True)
    inv = lax.rsqrt(jnp.mean(centered * centered, axis=-1, keepdims=True) + NORM_EPS)
    return centered * inv, inv


def norm_back(grad, hat, inv, gain):
    gh = grad * gain
    inner = (
        gh
        - jnp.mean(gh, axis=-1, keepdims=True)
        - hat * jnp.mean(gh * hat, axis=-1, keepdims=True)
    )
    return inv * inner, jnp.sum(grad * hat, axis=0, keepdims=True)


def layer_kernel(
    ways,
    x_h, cot_h, wa_h, wm_h, gain_h, cos_r, sin_r, segc_r,
    out_o, gtok_o, ga_o, gi_o, gd_o, gain_o,
    xall, cotall, n1, n2, gm, gslots, wA, wM, q_s, k_s, v_s, kT, vT, attn, attnT, eT, inv_r,
    acc, sst, srv, pst, prv, hid, gpair, gIst, gIrv, gDst, gDrv, gAst, gArv, gIf, gDf, gAf,
    mixed1, gmixed, gproj, gk, gv, gvec, ggst, ggrv,
    segr, ag_ps, ag_pr, ag_ss, ag_sr, rs_ss, rs_sr, rs_ps, rs_pr, z_s, z_r, l_s, l_r, f_s, f_r, sw_s, sw_r,
    gg_s, gg_r, loc,
):
    Z, N = ways
    z, c, t = lax.axis_index("dp"), lax.axis_index("ctx"), lax.axis_index("tensor")
    o = 1 - t
    via, onto = 1 + t, 2 - t
    R, D = x_h.shape
    H = R // 2
    S = R * N
    Dz = wa_h.shape[0]
    PW = wa_h.shape[1] // 4
    UW = wm_h.shape[0] // 3
    heads = PW // HD
    CH = 256
    gst, grv = (gIst, gDst, gAst), (gIrv, gDrv, gArv)

    def rows(cb, half):
        return pl.ds(pl.multiple_of(cb * R + half * H, H), H)

    def block(cb):
        return pl.ds(pl.multiple_of(cb * R, R), R)

    def rcopy(src, dst, ss, rs, dev):
        return pltpu.make_async_remote_copy(
            src_ref=src, dst_ref=dst, send_sem=ss, recv_sem=rs, device_id=dev, device_id_type=MESH
        )

    bar = pltpu.get_barrier_semaphore()
    for m in range(1, N):
        pl.semaphore_signal(bar, inc=1, device_id={"ctx": partner(c, m)}, device_id_type=MESH)
    pl.semaphore_signal(bar, inc=1, device_id={"tensor": o}, device_id_type=MESH)
    for d in range(1, Z):
        pl.semaphore_signal(bar, inc=1, device_id={"dp": lax.rem(z + d, Z)}, device_id_type=MESH)
    pl.semaphore_wait(bar, N - 1 + 1 + Z - 1)

    def ag_peer(kind, buf, m, src=None):
        own = rows(c, t)
        return rcopy(
            buf.at[own] if src is None else src, buf.at[own], ag_ps.at[kind, m], ag_pr.at[kind, m],
            {"ctx": partner(c, m)},
        )

    def ag_sib(kind, buf, m):
        own = rows(partner(c, m), t)
        return rcopy(
            buf.at[own], buf.at[own], ag_ss.at[kind, m], ag_sr.at[kind, m], {"tensor": o}
        )

    def ag_relay(kind, buf):
        there = buf.at[rows(partner(c, via), t)]
        return rcopy(
            there, there, ag_ps.at[kind, 3], ag_pr.at[kind, 3], {"ctx": partner(c, onto)}
        )

    def ag_arrive(kind, buf, m):
        there = buf.at[rows(partner(c, m), t)]
        rcopy(there, there, ag_ps.at[kind, m], ag_pr.at[kind, m], {"ctx": partner(c, onto)}).wait_recv()

    def ag_near(kind, buf):
        ag_arrive(kind, buf, via)
        ag_relay(kind, buf).start()
        ag_sib(kind, buf, via).start()
        ag_arrive(kind, buf, onto)
        ag_sib(kind, buf, onto).start()

    def ag_far(kind, buf):
        ag_arrive(kind, buf, 3)
        ag_sib(kind, buf, 3).start()

    def ag_sibling_half(kind, buf, m):
        there = buf.at[rows(partner(c, m), o)]
        rcopy(there, there, ag_ss.at[kind, m], ag_sr.at[kind, m], {"tensor": o}).wait_recv()

    def rs_sib(kind, m):
        return rcopy(
            sst.at[kind, m], srv.at[kind, m], rs_ss.at[kind, m], rs_sr.at[kind, m], {"tensor": o}
        )

    def rs_peer(kind, m, to):
        return rcopy(
            pst.at[kind, m - 1], prv.at[kind, m - 1], rs_ps.at[kind, m], rs_pr.at[kind, m],
            {"ctx": partner(c, to)},
        )

    def rs_begin(kind, m, partial):
        cb = partner(c, m)
        sst[kind, m] = partial(cb, o).astype(BF16)
        rs_sib(kind, m).start()
        acc[kind % 2, m] = partial(cb, t)

    def rs_total(kind, m):
        rs_sib(kind, m).wait_recv()
        return acc[kind % 2, m] + srv[kind, m].astype(F32)

    def rs_own(kind):
        acc[kind % 2, 0] = rs_total(kind, 0)

    def rs_far(kind):
        pst[kind, 2] = rs_total(kind, 3).astype(BF16)
        rs_peer(kind, 3, onto).start()

    def rs_near(kind):
        pst[kind, onto - 1] = rs_total(kind, onto).astype(BF16)
        rs_peer(kind, onto, onto).start()

    def rs_joined(kind):
        total = rs_total(kind, via)
        rs_peer(kind, 3, onto).wait_recv()
        pst[kind, via - 1] = (total + prv[kind, 2].astype(F32)).astype(BF16)
        rs_peer(kind, via, via).start()

    def rs_end(kind):
        for m in (1, 2):
            rs_peer(kind, m, m).wait_recv()
        return acc[kind % 2, 0] + prv[kind, 0].astype(F32) + prv[kind, 1].astype(F32)

    def zrow(i):
        return pl.ds(pl.multiple_of(i * Dz, Dz), Dz)

    def z_copy(kind, d, src, dst):
        return rcopy(
            src, dst, z_s.at[kind, d], z_r.at[kind, d], {"dp": lax.rem(z + d, Z)}
        )

    def z_recv(kind, d, dst):
        rcopy(dst, dst, z_s.at[kind, d], z_r.at[kind, d], {"dp": lax.rem(z + d, Z)}).wait_recv()

    def z_gain(d):
        return z_copy(Z_GAIN, d, gain_h, gslots.at[z])

    right, left = lax.rem(z + 1, Z), lax.rem(z + Z - 1, Z)

    def line_copy(kind, side, at, src, dst):
        return rcopy(
            src, dst, l_s.at[kind, side, at], l_r.at[kind, side, at],
            {"dp": left if side else right},
        )

    def gather_send(kind, buf, h, act):
        for side in (0, 1):
            src = z + (h - 1) if side else z - (h - 1)
            ok = (src < Z) & (z > 0) if side else (src >= 0) & (z < Z - 1)

            @pl.when(ok)
            def _():
                there = buf.at[zrow(src)]
                act(line_copy(kind, side, h, there, there))

    def gather_step(kind, buf, h):
        for side in (0, 1):
            src = z + h if side else z - h

            @pl.when((src < Z) if side else (src >= 0))
            def _():
                there = buf.at[zrow(src)]
                line_copy(kind, side, h, there, there).wait_recv()

        if h + 1 < Z:
            gather_send(kind, buf, h + 1, start)

    def scatter_copy(kind, d):
        to = lax.rem(z + d, Z)
        return rcopy(
            gst[kind].at[zrow(to)], grv[kind].at[d], l_s.at[kind, 0, d], l_r.at[kind, 0, d],
            {"dp": to},
        )

    def scatter_start(kind):
        for d in range(1, Z):
            scatter_copy(kind, d).start()

    def scatter_total(kind):
        total = gst[kind][zrow(z), :].astype(F32)
        for d in range(1, Z):
            scatter_copy(kind, d).wait_recv()
            total = total + grv[kind][d].astype(F32)
        return total

    def start(copy):
        copy.start()

    def sent(copy):
        copy.wait_send()

    x_half = pl.ds(pl.multiple_of(t * H, H), H)
    for m in (1, 2):
        ag_peer(AG_X, xall, m, x_h.at[x_half]).start()
    for d in range(1, Z):
        z_gain(d).start()
    local = [
        pltpu.make_async_copy(x_h, xall.at[block(c)], loc.at[0]),
        pltpu.make_async_copy(gain_h, gslots.at[z], loc.at[1]),
        pltpu.make_async_copy(wa_h, wA.at[zrow(z)], loc.at[2]),
        pltpu.make_async_copy(cot_h, cotall.at[block(c)], loc.at[3]),
    ]
    for one in local:
        one.start()
    local[2].wait()
    gather_send(L_WA, wA, 1, start)
    for i in (0, 1, 3):
        local[i].wait()

    for d in range(1, Z):
        z_recv(Z_GAIN, d, gslots.at[lax.rem(z + Z - d, Z)])
    gains = gslots[0].astype(F32)
    for i in range(1, Z):
        gains = gains + gslots[i].astype(F32)
    gvec[...] = gains[0:8]

    def norm_one(cb):
        def body(i, carry):
            r = pl.ds(pl.multiple_of(cb * R + i * 64, 64), 64)
            hat, _ = norm_stats(xall[r, :].astype(F32))
            n1[r, :] = (hat * gvec[0:1, :]).astype(BF16)
            return carry

        lax.fori_loop(0, R // 64, body, 0)

    norm_one(c)
    for k in range(3):
        part = wm_h[k * UW : (k + 1) * UW, :].astype(F32).T
        wM[zrow(z), k * UW : (k + 1) * UW] = part.astype(BF16)
    gather_step(L_WA, wA, 1)
    gather_send(L_WM, wM, 1, start)
    ag_near(AG_X, xall)
    for m in (1, 2):
        ag_peer(AG_COT, cotall, m, cot_h.at[x_half]).start()
    for m in (1, 2):
        ag_sibling_half(AG_X, xall, m)
        norm_one(partner(c, m))
    for h in range(2, Z - 1):
        gather_step(L_WA, wA, h)
    ag_far(AG_X, xall)
    ag_sibling_half(AG_X, xall, 3)
    norm_one(partner(c, 3))

    segr[...] = segc_r[...].T[0:8, :]

    ag_near(AG_COT, cotall)
    gather_step(L_WA, wA, Z - 1)

    def project(cb, carry):
        b = block(cb)
        proj = dot(n1[b, :], wA[:, 0 : 3 * PW]).astype(BF16)
        cos, sin = cos_r[b, :], sin_r[b, :]
        qf = proj[:, 0:PW].astype(F32)
        kf = proj[:, PW : 2 * PW].astype(F32)
        q_rot = (qf * cos + swap_halves(qf) * sin).astype(BF16).astype(F32) * (HD**-0.5)
        k_rot = (kf * cos + swap_halves(kf) * sin).astype(BF16)
        val = proj[:, 2 * PW : 3 * PW]
        q_s[b, :] = q_rot.astype(BF16)
        k_s[b, :] = k_rot
        v_s[b, :] = val
        kT[:, b] = k_rot.astype(F32).T.astype(BF16)
        vT[:, b] = val.astype(F32).T.astype(BF16)
        return carry

    lax.fori_loop(0, N, project, 0)

    lane = lax.broadcasted_iota(jnp.int32, (R, PW), 1)

    def only(u, h):
        return jnp.where(lax.div(lane, HD) == h, u, jnp.zeros_like(u))

    def attend(cb):
        b = block(cb)
        same = segc_r[:, 0:1] == segr[0:1, b]
        for h in range(heads):
            s = dot(k_s[...], only(q_s[b, :], h), 1, 1)
            s = jnp.where(same, s, MASK_FILL)
            e = jnp.exp(s - jnp.max(s, axis=0, keepdims=True))
            inv = 1.0 / jnp.sum(e, axis=0, keepdims=True)
            eb = e.astype(BF16)
            eT[h, cb] = eb
            inv_r[h : h + 1, b] = inv
            hr = slice(h * HD, (h + 1) * HD)
            attnT[hr, b] = (dot(vT[hr, :], eb) * inv).astype(BF16)
        attn[b, :] = attnT[:, b].astype(F32).T.astype(BF16)

    def part_attn(cb, half):
        return dot(attn[rows(cb, half), :], wA[:, 3 * PW :], 1, 1)

    def attend_begin(m):
        attend(partner(c, m))
        rs_begin(RS_ATTN, m, part_attn)

    attend_begin(3)
    attend_begin(2)
    rs_far(RS_ATTN)
    attend_begin(1)
    gather_step(L_WM, wM, 1)
    rs_near(RS_ATTN)
    attend_begin(0)
    rs_joined(RS_ATTN)
    rs_own(RS_ATTN)
    ag_far(AG_COT, cotall)
    mixed1[...] = xall[rows(c, t), :].astype(F32) + rs_end(RS_ATTN)

    hat2, inv2 = norm_stats(mixed1[...])
    n2[rows(c, t), :] = (hat2 * gvec[1:2, :]).astype(BF16)
    for m in (1, 2):
        ag_peer(AG_N2, n2, m).start()
    ag_sib(AG_N2, n2, 0).start()
    for h in range(2, Z):
        gather_step(L_WM, wM, h)
    for m in (1, 2, 3):
        ag_sibling_half(AG_COT, cotall, m)

    def mlp(cb):
        b = block(cb)
        pair = dot(n2[b, :], wM[:, 0 : 2 * UW])
        grad_h = dot(cotall[b, :], wM[:, 2 * UW :])
        a, g = pair[:, :UW], pair[:, UW:]
        cdf = 0.5 * (1.0 + lax.erf(a * INV_ROOT_TWO))
        gelu = a * cdf
        hid[b, :] = (gelu * g).astype(BF16)
        slope = cdf + a * jnp.exp(-0.5 * a * a) * INV_ROOT_TWO_PI
        gpair[b, 0:UW] = (grad_h * g * slope).astype(BF16)
        gpair[b, UW:] = (grad_h * gelu).astype(BF16)

    def part_gn2(cb, half):
        return dot(gpair[rows(cb, half), :], wM[:, 0 : 2 * UW], 1, 1)

    def part_out(cb, half):
        return dot(hid[rows(cb, half), :], wM[:, 2 * UW :], 1, 1)

    def mlp_at(m):
        ag_sibling_half(AG_N2, n2, m)
        mlp(partner(c, m))

    mlp_at(0)
    rs_begin(RS_GN2, 0, part_gn2)
    ag_near(AG_N2, n2)
    mlp_at(1)
    rs_begin(RS_GN2, 1, part_gn2)
    rs_own(RS_GN2)
    ag_far(AG_N2, n2)
    mlp_at(3)
    rs_begin(RS_GN2, 3, part_gn2)
    mlp_at(2)
    rs_far(RS_GN2)
    rs_begin(RS_GN2, 2, part_gn2)

    def grads_down(i, carry):
        col = pl.ds(pl.multiple_of(i * CH, CH), CH)
        gDst[col, :] = dot(cotall[:, col], hid[...], 0, 0).astype(BF16)
        return carry

    lax.fori_loop(0, D // CH, grads_down, 0)
    scatter_start(L_GDOWN)
    rs_near(RS_GN2)
    rs_joined(RS_GN2)

    def grads_in(i, carry):
        col = pl.ds(pl.multiple_of(i * CH, CH), CH)
        gIst[col, :] = dot(n2[:, col], gpair[...], 0, 0).astype(BF16)
        return carry

    lax.fori_loop(0, D // CH, grads_in, 0)
    scatter_start(L_GIN)

    hat2, inv2 = norm_stats(mixed1[...])
    back2, gg_mlp = norm_back(rs_end(RS_GN2), hat2, inv2, gvec[1:2, :])
    ggst[0, 1:2, :] = gg_mlp
    gmixed[...] = cotall[rows(c, t), :].astype(F32) + back2
    gm[rows(c, t), :] = gmixed[...].astype(BF16)
    for m in (1, 2):
        ag_peer(AG_GM, gm, m).start()
    ag_sib(AG_GM, gm, 0).start()
    rs_begin(RS_OUT, 3, part_out)
    rs_begin(RS_OUT, 2, part_out)
    rs_begin(RS_OUT, 1, part_out)
    rs_begin(RS_OUT, 0, part_out)

    def fin(kind, m, own, out):
        return rcopy(own, out.at[c], f_s.at[kind, m], f_r.at[kind, m], {"ctx": partner(c, m)})

    def own_copy(kind, own, out):
        return pltpu.make_async_copy(own, out.at[c], loc.at[kind])

    def finish(kind):
        own, out = finals[kind]
        own[...] = scatter_total(kind).astype(BF16)
        for m in (1, 2):
            fin(kind, m, own, out).start()
        own_copy(kind, own, out).start()

    def fin_relay(kind):
        there = finals[kind][1].at[partner(c, via)]
        return rcopy(
            there, there, f_s.at[kind, 3], f_r.at[kind, 3], {"ctx": partner(c, onto)}
        )

    def fin_arrive(kind, m):
        there = finals[kind][1].at[partner(c, m)]
        rcopy(there, there, f_s.at[kind, m], f_r.at[kind, m], {"ctx": partner(c, onto)}).wait_recv()

    def pass_on(kind):
        fin_arrive(kind, via)
        fin_relay(kind).start()

    finals = ((gIf, gi_o), (gDf, gd_o), (gAf, ga_o))

    gk[...] = jnp.zeros_like(gk)
    gv[...] = jnp.zeros_like(gv)

    def rotate_back(g, b):
        return g * cos_r[b, :] + swap_halves(g * sin_r[b, :])

    def attend_back(cb):
        b = block(cb)
        g = dot(gm[b, :], wA[:, 3 * PW :]).astype(BF16)
        gT = g.astype(F32).T
        scaled = []
        grad_q = []
        for h in range(heads):
            hr = slice(h * HD, (h + 1) * HD)
            inv = inv_r[h : h + 1, b]
            delta = jnp.sum(gT[hr, :] * attnT[hr, b].astype(F32), axis=0, keepdims=True)
            gp = dot(v_s[...], only(g, h), 1, 1)
            ds = (eT[h, cb].astype(F32) * ((gp - delta) * inv)).astype(BF16)
            grad_q.append(dot(kT[hr, :], ds))
            gk[...] += dot(ds, only(q_s[b, :], h))
            scaled.append(gT[hr, :] * inv)
        gs = jnp.concatenate(scaled, axis=0).T.astype(BF16)
        for h in range(heads):
            gv[...] += dot(eT[h, cb], only(gs, h))
        gq = jnp.concatenate(grad_q, axis=0).T * (HD**-0.5)
        gproj[b, 0:PW] = rotate_back(gq, b).astype(BF16)

    for m in (0, 1, 2, 3):
        if m == 0:
            ag_near(AG_GM, gm)
        if m == 2:
            ag_far(AG_GM, gm)
        ag_sibling_half(AG_GM, gm, m)
        attend_back(partner(c, m))
        if m == 1:
            rs_far(RS_OUT)
            rs_near(RS_OUT)
    rs_joined(RS_OUT)
    rs_own(RS_OUT)
    finish(L_GDOWN)

    def unrotate(cb, carry):
        b = block(cb)
        gproj[b, PW : 2 * PW] = rotate_back(gk[b, :], b).astype(BF16)
        gproj[b, 2 * PW :] = gv[b, :].astype(BF16)
        return carry

    lax.fori_loop(0, N, unrotate, 0)

    def grads_attn(i, carry):
        col = pl.ds(pl.multiple_of(i * CH, CH), CH)
        gAst[col, 0 : 3 * PW] = dot(n1[:, col], gproj[...], 0, 0).astype(BF16)
        gAst[col, 3 * PW :] = dot(gm[:, col], attn[...], 0, 0).astype(BF16)
        return carry

    lax.fori_loop(0, D // CH, grads_attn, 0)
    scatter_start(L_GWA)

    def part_gn1(cb, half):
        return dot(gproj[rows(cb, half), :], wA[:, 0 : 3 * PW], 1, 1)

    rs_begin(RS_GN1, 3, part_gn1)
    rs_begin(RS_GN1, 2, part_gn1)
    rs_far(RS_GN1)
    pass_on(L_GDOWN)
    rs_begin(RS_GN1, 1, part_gn1)
    rs_near(RS_GN1)
    rs_begin(RS_GN1, 0, part_gn1)
    rs_joined(RS_GN1)
    rs_own(RS_GN1)

    finish(L_GIN)

    hat1, inv1 = norm_stats(xall[rows(c, t), :].astype(F32))
    back1, gg_attn = norm_back(rs_end(RS_GN1), hat1, inv1, gvec[0:1, :])
    ggst[0, 0:1, :] = gg_attn
    gtok_o[x_half, :] = gmixed[...] + back1
    swap_tok = rcopy(
        gtok_o.at[x_half], gtok_o.at[x_half], sw_s.at[0], sw_r.at[0], {"tensor": o}
    )
    swap_tok.start()

    ggst[0, 2:8, :] = jnp.zeros_like(ggst[0, 2:8, :])
    gg0 = rcopy(ggst.at[0], ggrv.at[0], gg_s.at[0], gg_r.at[0], {"tensor": o})
    gg0.start()

    out_o[x_half, :] = (mixed1[...] + rs_end(RS_OUT)).astype(BF16)
    swap_out = rcopy(
        out_o.at[x_half], out_o.at[x_half], sw_s.at[1], sw_r.at[1], {"tensor": o}
    )
    swap_out.start()
    gg0.wait_recv()
    ggst[1] = ggst[0] + ggrv[0]

    def gg_ctx(m):
        return rcopy(ggst.at[1], ggrv.at[m], gg_s.at[m], gg_r.at[m], {"ctx": partner(c, m)})

    for m in (1, 2, 3):
        gg_ctx(m).start()

    for m in (1, 2, 3):
        gg_ctx(m).wait_recv()
    ggst[2] = (ggst[1] + ggrv[1]) + (ggrv[2] + ggrv[3])

    def gg_z(d):
        return z_copy(Z_GG, d, ggst.at[2], ggrv.at[3 + d])

    for d in range(1, Z):
        gg_z(d).start()
    pass_on(L_GIN)
    finish(L_GWA)
    total = ggst[2]
    for d in range(1, Z):
        z_recv(Z_GG, d, ggrv.at[3 + d])
        total = total + ggrv[3 + d]
    gain_o[...] = total
    pass_on(L_GWA)

    other = pl.ds(pl.multiple_of(o * H, H), H)
    rcopy(gtok_o.at[other], gtok_o.at[other], sw_s.at[0], sw_r.at[0], {"tensor": o}).wait_recv()
    rcopy(out_o.at[other], out_o.at[other], sw_s.at[1], sw_r.at[1], {"tensor": o}).wait_recv()
    for kind, (own, out) in enumerate(finals):
        fin_arrive(kind, onto)
        fin_arrive(kind, 3)
        fin_relay(kind).wait_send()
        for m in (1, 2):
            fin(kind, m, own, out).wait_send()
    for m in (1, 2, 3):
        gg_ctx(m).wait_send()
    for kind, (own, out) in enumerate(finals):
        own_copy(kind, own, out).wait()
    gg0.wait_send()
    swap_tok.wait_send()
    swap_out.wait_send()
    for m in (1, 2):
        ag_peer(AG_X, xall, m, x_h.at[x_half]).wait_send()
        ag_peer(AG_COT, cotall, m, cot_h.at[x_half]).wait_send()
        ag_peer(AG_N2, n2, m).wait_send()
        ag_peer(AG_GM, gm, m).wait_send()
    for kind, buf in ((AG_X, xall), (AG_COT, cotall), (AG_N2, n2), (AG_GM, gm)):
        ag_relay(kind, buf).wait_send()
    for m in (1, 2, 3):
        for kind in range(4):
            rs_peer(kind, m, onto).wait_send()
        ag_sib(AG_X, xall, m).wait_send()
        ag_sib(AG_COT, cotall, m).wait_send()
    for m in range(4):
        ag_sib(AG_N2, n2, m).wait_send()
        ag_sib(AG_GM, gm, m).wait_send()
        for kind in range(4):
            rs_sib(kind, m).wait_send()
    for d in range(1, Z):
        z_gain(d).wait_send()
        gg_z(d).wait_send()
        gather_send(L_WA, wA, d, sent)
        gather_send(L_WM, wM, d, sent)
        for kind in (L_GIN, L_GDOWN, L_GWA):
            scatter_copy(kind, d).wait_send()


def spread_kernel(ga, gi, gd, tok_i, gtok_i, qkv_o, out_o, in_o, down_o, tok_o, gtok_o):
    width, units = out_o.shape[0], down_o.shape[0]
    for k in range(3):
        qkv_o[k] = ga[:, k * width : (k + 1) * width].astype(F32)
    out_o[...] = ga[:, 3 * width :].astype(F32).T
    for k in range(2):
        in_o[k] = gi[:, k * units : (k + 1) * units].astype(F32).T
    down_o[...] = gd[...].astype(F32).T
    tok_o[...] = tok_i[...]
    gtok_o[...] = gtok_i[...]


def tables(doc_len, span_len):
    count = doc_len.shape[0]
    upto = jnp.arange(count)[:, None] >= jnp.arange(count)[None, :]
    doc_end = jnp.sum(jnp.where(upto, doc_len[None, :], 0), axis=1)
    doc_start = doc_end - doc_len
    places = jnp.arange(span_len, dtype=jnp.int32)
    begins = jnp.max(
        jnp.where(places[:, None] >= doc_start[None, :], doc_start[None, :], 0), axis=1
    )
    segment = jnp.sum((places[:, None] >= doc_end[None, :]).astype(jnp.int32), axis=1)
    offset = (places - begins).astype(F32)
    half = HD // 2
    place = jnp.arange(LANES, dtype=jnp.int32)
    frequency = ROPE_BASE ** (-((place % half).astype(F32) * (2.0 / HD)))
    turn = jnp.where(place % HD < half, -1.0, 1.0)
    angles = offset[:, None] * frequency[None, :]
    seg = jnp.broadcast_to(segment.astype(F32)[:, None], (span_len, LANES))
    return jnp.cos(angles), jnp.sin(angles) * turn[None, :], seg


def local(ways, tokens, doc_lengths, gain_attn, w_qkv, w_attn_out, gain_mlp, w_in, w_mlp_out, cotangent):
    Z, N = ways
    ci, zi = lax.axis_index("ctx"), lax.axis_index("dp")
    R, D = tokens.shape
    S = R * N
    H = R // 2
    Dz, width = w_qkv.shape[1:]
    units = w_in.shape[2]
    PW = width // N
    UW = -(-units // (N * LANES)) * LANES
    padded = UW * N

    qkv = lax.dynamic_slice_in_dim(w_qkv, ci * PW, PW, 2)
    w_out = lax.dynamic_slice_in_dim(w_attn_out, ci * PW, PW, 0).T
    wa = jnp.concatenate([qkv[0], qkv[1], qkv[2], w_out], axis=1)
    w_up = jnp.pad(w_in.transpose(0, 2, 1), ((0, 0), (0, padded - units), (0, 0)))
    w_up = lax.dynamic_slice_in_dim(w_up, ci * UW, UW, 1)
    w_down = jnp.pad(w_mlp_out, ((0, padded - units), (0, 0)))
    w_down = lax.dynamic_slice_in_dim(w_down, ci * UW, UW, 0)
    wm = jnp.concatenate([w_up[0], w_up[1], w_down], axis=0)
    gains = lax.dynamic_update_slice(
        jnp.zeros((16, D), BF16), jnp.stack([gain_attn, gain_mlp]), (0, zi * Dz)
    )
    cos, sin, seg = tables(doc_lengths[0], S)

    anywhere = pl.BlockSpec(memory_space=pl.ANY)
    vmem = pl.BlockSpec(memory_space=pltpu.VMEM)
    V = pltpu.VMEM
    dma = pltpu.SemaphoreType.DMA
    scratch = [
        V((S, D), BF16), V((S, D), BF16), V((S, D), BF16), V((S, D), BF16), V((S, D), BF16),
        V((Z, 16, D), BF16), V((D, 4 * PW), BF16), V((D, 3 * UW), BF16),
        V((S, PW), BF16), V((S, PW), BF16), V((S, PW), BF16), V((PW, S), BF16), V((PW, S), BF16),
        V((S, PW), BF16), V((PW, S), BF16), V((PW // HD, N, S, R), BF16), V((8, S), F32),
        V((2, N, H, D), F32), V((4, N, H, D), BF16), V((4, N, H, D), BF16), V((4, N - 1, H, D), BF16),
        V((4, N - 1, H, D), BF16), V((S, UW), BF16), V((S, 2 * UW), BF16),
        V((D, 2 * UW), BF16), V((Z, Dz, 2 * UW), BF16), V((D, UW), BF16), V((Z, Dz, UW), BF16),
        V((D, 4 * PW), BF16), V((Z, Dz, 4 * PW), BF16),
        V((Dz, 2 * UW), BF16), V((Dz, UW), BF16), V((Dz, 4 * PW), BF16),
        V((H, D), F32), V((H, D), F32), V((S, 3 * PW), BF16), V((S, PW), F32), V((S, PW), F32),
        V((8, D), F32), V((3, 8, D), F32), V((3 + Z, 8, D), F32), V((8, S), F32),
        dma((4, N)), dma((4, N)), dma((4, N)), dma((4, N)), dma((4, N)), dma((4, N)), dma((4, N)),
        dma((4, N)), dma((2, Z)), dma((2, Z)), dma((5, 2, Z)), dma((5, 2, Z)), dma((3, N)), dma((3, N)), dma((2,)), dma((2,)),
        dma((N,)), dma((N,)), dma((5,)),
    ]
    out, gtok, ga, gi, gd, gg = pl.pallas_call(
        functools.partial(layer_kernel, ways),
        out_shape=[
            jax.ShapeDtypeStruct((R, D), BF16),
            jax.ShapeDtypeStruct((R, D), F32),
            jax.ShapeDtypeStruct((N, Dz, 4 * PW), BF16),
            jax.ShapeDtypeStruct((N, Dz, 2 * UW), BF16),
            jax.ShapeDtypeStruct((N, Dz, UW), BF16),
            jax.ShapeDtypeStruct((8, D), F32),
        ],
        in_specs=[anywhere] * 3 + [vmem, anywhere] + [vmem] * 3,
        out_specs=[vmem, vmem, anywhere, anywhere, anywhere, vmem],
        scratch_shapes=scratch,
        compiler_params=pltpu.CompilerParams(
            collective_id=0, has_side_effects=True, vmem_limit_bytes=60 * 1024 * 1024
        ),
        cost_estimate=pl.CostEstimate(
            flops=12 * 10**9, bytes_accessed=12 * 2**20, transcendentals=4 * 10**6
        ),
        name="layer",
    )(tokens, cotangent, wa, wm, gains, cos, sin, seg)

    gains_own = lax.dynamic_slice_in_dim(gg[0:2], zi * Dz, Dz, 1)
    g_qkv, g_out, g_in, g_down, out, gtok = pl.pallas_call(
        spread_kernel,
        grid=(N,),
        out_shape=[
            jax.ShapeDtypeStruct((3, Dz, N * PW), F32),
            jax.ShapeDtypeStruct((N * PW, Dz), F32),
            jax.ShapeDtypeStruct((2, units, Dz), F32),
            jax.ShapeDtypeStruct((units, Dz), F32),
            jax.ShapeDtypeStruct((R, D), BF16),
            jax.ShapeDtypeStruct((R, D), F32),
        ],
        in_specs=[
            pl.BlockSpec((None, Dz, 4 * PW), lambda i: (i, 0, 0)),
            pl.BlockSpec((None, Dz, 2 * UW), lambda i: (i, 0, 0)),
            pl.BlockSpec((None, Dz, UW), lambda i: (i, 0, 0)),
            pl.BlockSpec((R // N, D), lambda i: (i, 0)),
            pl.BlockSpec((R // N, D), lambda i: (i, 0)),
        ],
        out_specs=[
            pl.BlockSpec((3, Dz, PW), lambda i: (0, 0, i)),
            pl.BlockSpec((PW, Dz), lambda i: (i, 0)),
            pl.BlockSpec((2, UW, Dz), lambda i: (0, i, 0)),
            pl.BlockSpec((UW, Dz), lambda i: (i, 0)),
            pl.BlockSpec((R // N, D), lambda i: (i, 0)),
            pl.BlockSpec((R // N, D), lambda i: (i, 0)),
        ],
        compiler_params=pltpu.CompilerParams(vmem_limit_bytes=60 * 1024 * 1024),
        name="spread",
    )(ga, gi, gd, out, gtok)
    g_in = g_in.transpose(0, 2, 1)
    return (out, gtok, gains_own[0], g_qkv, g_out, gains_own[1], g_in, g_down)


def solution(mesh):
    in_specs = (
        P(("dp", "ctx"), None),
        P("dp", None),
        P("dp"),
        P(None, "dp", "tensor"),
        P("tensor", "dp"),
        P("dp"),
        P(None, "dp", "tensor"),
        P("tensor", "dp"),
        P(("dp", "ctx"), None),
    )
    out_specs = (
        P(("dp", "ctx"), None),
        P(("dp", "ctx"), None),
        P("dp"),
        P(None, "dp", "tensor"),
        P("tensor", "dp"),
        P("dp"),
        P(None, "dp", "tensor"),
        P("tensor", "dp"),
    )
    ways = (mesh.shape["dp"], mesh.shape["ctx"])
    return jax.shard_map(
        functools.partial(local, ways),
        mesh=mesh,
        in_specs=in_specs,
        out_specs=out_specs,
        check_vma=False,
    )
```

```python
import functools
import math

import jax
import jax.numpy as jnp
from jax import lax
from jax.experimental import pallas as pl
from jax.experimental.pallas import tpu as pltpu
from jax.sharding import PartitionSpec as P

HD = 64
LANES = 128
NORM_EPS = 1e-05
ROPE_BASE = 160000.0
MASK_FILL = -1e30
INV_ROOT_TWO = 1.0 / math.sqrt(2.0)
INV_ROOT_TWO_PI = 1.0 / math.sqrt(2.0 * math.pi)
MESH = pl.DeviceIdType.MESH
F32 = jnp.float32
BF16 = jnp.bfloat16

AG_X, AG_COT, AG_N2, AG_GM = range(4)
RS_ATTN, RS_GN2, RS_OUT, RS_GN1 = range(4)
Z_GAIN, Z_GG = range(2)
L_GIN, L_GDOWN, L_GWA, L_WA, L_WM = range(5)


def dot(a, b, ca=1, cb=0):
    return lax.dot_general(a, b, (((ca,), (cb,)), ((), ())), preferred_element_type=F32)


def partner(c, m):
    y = lax.rem(lax.div(c, 2) + lax.div(m, 2), 2)
    x = lax.rem(lax.rem(c, 2) + lax.rem(m, 2), 2)
    return y * 2 + x


def swap_halves(u):
    lane = lax.broadcasted_iota(jnp.int32, u.shape, 1)
    first = lax.rem(lane, HD) < HD // 2
    return jnp.where(first, pltpu.roll(u, LANES - HD // 2, 1), pltpu.roll(u, HD // 2, 1))


def norm_stats(v):
    centered = v - jnp.mean(v, axis=-1, keepdims=True)
    inv = lax.rsqrt(jnp.mean(centered * centered, axis=-1, keepdims=True) + NORM_EPS)
    return centered * inv, inv


def norm_back(grad, hat, inv, gain):
    gh = grad * gain
    inner = (
        gh
        - jnp.mean(gh, axis=-1, keepdims=True)
        - hat * jnp.mean(gh * hat, axis=-1, keepdims=True)
    )
    return inv * inner, jnp.sum(grad * hat, axis=0, keepdims=True)


def layer_kernel(
    ways,
    x_h, cot_h, wa_h, wm_h, gain_h, cos_r, sin_r, segc_r,
    out_o, gtok_o, ga_o, gi_o, gd_o, gain_o,
    xall, cotall, n1, n2, gm, gslots, wA, wM, q_s, k_s, v_s, kT, vT, attn, attnT, eT, inv_r,
    acc, sst, srv, pst, prv, hid, gpair, gIst, gIrv, gDst, gDrv, gAst, gArv, gIf, gDf, gAf,
    mixed1, gmixed, gproj, gk, gv, gvec, ggst, ggrv,
    segr, ag_ps, ag_pr, ag_ss, ag_sr, rs_ss, rs_sr, rs_ps, rs_pr, z_s, z_r, l_s, l_r, f_s, f_r, sw_s, sw_r,
    gg_s, gg_r, loc,
):
    Z, N = ways
    z, c, t = lax.axis_index("dp"), lax.axis_index("ctx"), lax.axis_index("tensor")
    o = 1 - t
    via, onto = 1 + t, 2 - t
    R, D = x_h.shape
    H = R // 2
    S = R * N
    Dz = wa_h.shape[0]
    PW = wa_h.shape[1] // 4
    UW = wm_h.shape[0] // 3
    heads = PW // HD
    CH = 256
    gst, grv = (gIst, gDst, gAst), (gIrv, gDrv, gArv)

    def rows(cb, half):
        return pl.ds(pl.multiple_of(cb * R + half * H, H), H)

    def block(cb):
        return pl.ds(pl.multiple_of(cb * R, R), R)

    def rcopy(src, dst, ss, rs, dev):
        return pltpu.make_async_remote_copy(
            src_ref=src, dst_ref=dst, send_sem=ss, recv_sem=rs, device_id=dev, device_id_type=MESH
        )

    bar = pltpu.get_barrier_semaphore()
    for m in range(1, N):
        pl.semaphore_signal(bar, inc=1, device_id={"ctx": partner(c, m)}, device_id_type=MESH)
    pl.semaphore_signal(bar, inc=1, device_id={"tensor": o}, device_id_type=MESH)
    for d in range(1, Z):
        pl.semaphore_signal(bar, inc=1, device_id={"dp": lax.rem(z + d, Z)}, device_id_type=MESH)
    pl.semaphore_wait(bar, N - 1 + 1 + Z - 1)

    def ag_peer(kind, buf, m, src=None):
        own = rows(c, t)
        return rcopy(
            buf.at[own] if src is None else src, buf.at[own], ag_ps.at[kind, m], ag_pr.at[kind, m],
            {"ctx": partner(c, m)},
        )

    def ag_sib(kind, buf, m):
        own = rows(partner(c, m), t)
        return rcopy(
            buf.at[own], buf.at[own], ag_ss.at[kind, m], ag_sr.at[kind, m], {"tensor": o}
        )

    def ag_relay(kind, buf):
        there = buf.at[rows(partner(c, via), t)]
        return rcopy(
            there, there, ag_ps.at[kind, 3], ag_pr.at[kind, 3], {"ctx": partner(c, onto)}
        )

    def ag_arrive(kind, buf, m):
        there = buf.at[rows(partner(c, m), t)]
        rcopy(there, there, ag_ps.at[kind, m], ag_pr.at[kind, m], {"ctx": partner(c, onto)}).wait_recv()

    def ag_near(kind, buf):
        ag_arrive(kind, buf, via)
        ag_relay(kind, buf).start()
        ag_sib(kind, buf, via).start()
        ag_arrive(kind, buf, onto)
        ag_sib(kind, buf, onto).start()

    def ag_far(kind, buf):
        ag_arrive(kind, buf, 3)
        ag_sib(kind, buf, 3).start()

    def ag_sibling_half(kind, buf, m):
        there = buf.at[rows(partner(c, m), o)]
        rcopy(there, there, ag_ss.at[kind, m], ag_sr.at[kind, m], {"tensor": o}).wait_recv()

    def rs_sib(kind, m):
        return rcopy(
            sst.at[kind, m], srv.at[kind, m], rs_ss.at[kind, m], rs_sr.at[kind, m], {"tensor": o}
        )

    def rs_peer(kind, m, to):
        return rcopy(
            pst.at[kind, m - 1], prv.at[kind, m - 1], rs_ps.at[kind, m], rs_pr.at[kind, m],
            {"ctx": partner(c, to)},
        )

    def rs_begin(kind, m, partial):
        cb = partner(c, m)
        sst[kind, m] = partial(cb, o).astype(BF16)
        rs_sib(kind, m).start()
        acc[kind % 2, m] = partial(cb, t)

    def rs_total(kind, m):
        rs_sib(kind, m).wait_recv()
        return acc[kind % 2, m] + srv[kind, m].astype(F32)

    def rs_own(kind):
        acc[kind % 2, 0] = rs_total(kind, 0)

    def rs_far(kind):
        pst[kind, 2] = rs_total(kind, 3).astype(BF16)
        rs_peer(kind, 3, onto).start()

    def rs_near(kind):
        pst[kind, onto - 1] = rs_total(kind, onto).astype(BF16)
        rs_peer(kind, onto, onto).start()

    def rs_joined(kind):
        total = rs_total(kind, via)
        rs_peer(kind, 3, onto).wait_recv()
        pst[kind, via - 1] = (total + prv[kind, 2].astype(F32)).astype(BF16)
        rs_peer(kind, via, via).start()

    def rs_end(kind):
        for m in (1, 2):
            rs_peer(kind, m, m).wait_recv()
        return acc[kind % 2, 0] + prv[kind, 0].astype(F32) + prv[kind, 1].astype(F32)

    def zrow(i):
        return pl.ds(pl.multiple_of(i * Dz, Dz), Dz)

    def z_copy(kind, d, src, dst):
        return rcopy(
            src, dst, z_s.at[kind, d], z_r.at[kind, d], {"dp": lax.rem(z + d, Z)}
        )

    def z_recv(kind, d, dst):
        rcopy(dst, dst, z_s.at[kind, d], z_r.at[kind, d], {"dp": lax.rem(z + d, Z)}).wait_recv()

    def z_gain(d):
        return z_copy(Z_GAIN, d, gain_h, gslots.at[z])

    right, left = lax.rem(z + 1, Z), lax.rem(z + Z - 1, Z)

    def line_copy(kind, side, at, src, dst):
        return rcopy(
            src, dst, l_s.at[kind, side, at], l_r.at[kind, side, at],
            {"dp": left if side else right},
        )

    def gather_send(kind, buf, h, act):
        for side in (0, 1):
            src = z + (h - 1) if side else z - (h - 1)
            ok = (src < Z) & (z > 0) if side else (src >= 0) & (z < Z - 1)

            @pl.when(ok)
            def _():
                there = buf.at[zrow(src)]
                act(line_copy(kind, side, h, there, there))

    def gather_step(kind, buf, h):
        for side in (0, 1):
            src = z + h if side else z - h

            @pl.when((src < Z) if side else (src >= 0))
            def _():
                there = buf.at[zrow(src)]
                line_copy(kind, side, h, there, there).wait_recv()

        if h + 1 < Z:
            gather_send(kind, buf, h + 1, start)

    def scatter_copy(kind, d):
        to = lax.rem(z + d, Z)
        return rcopy(
            gst[kind].at[zrow(to)], grv[kind].at[d], l_s.at[kind, 0, d], l_r.at[kind, 0, d],
            {"dp": to},
        )

    def scatter_start(kind):
        for d in range(1, Z):
            scatter_copy(kind, d).start()

    def scatter_total(kind):
        total = gst[kind][zrow(z), :].astype(F32)
        for d in range(1, Z):
            scatter_copy(kind, d).wait_recv()
            total = total + grv[kind][d].astype(F32)
        return total

    def start(copy):
        copy.start()

    def sent(copy):
        copy.wait_send()

    x_half = pl.ds(pl.multiple_of(t * H, H), H)
    for m in (1, 2):
        ag_peer(AG_X, xall, m, x_h.at[x_half]).start()
    for d in range(1, Z):
        z_gain(d).start()
    local = [
        pltpu.make_async_copy(x_h, xall.at[block(c)], loc.at[0]),
        pltpu.make_async_copy(gain_h, gslots.at[z], loc.at[1]),
        pltpu.make_async_copy(wa_h, wA.at[zrow(z)], loc.at[2]),
        pltpu.make_async_copy(cot_h, cotall.at[block(c)], loc.at[3]),
    ]
    for one in local:
        one.start()
    local[2].wait()
    gather_send(L_WA, wA, 1, start)
    for i in (0, 1, 3):
        local[i].wait()

    for d in range(1, Z):
        z_recv(Z_GAIN, d, gslots.at[lax.rem(z + Z - d, Z)])
    gains = gslots[0].astype(F32)
    for i in range(1, Z):
        gains = gains + gslots[i].astype(F32)
    gvec[...] = gains[0:8]

    def norm_one(cb):
        def body(i, carry):
            r = pl.ds(pl.multiple_of(cb * R + i * 64, 64), 64)
            hat, _ = norm_stats(xall[r, :].astype(F32))
            n1[r, :] = (hat * gvec[0:1, :]).astype(BF16)
            return carry

        lax.fori_loop(0, R // 64, body, 0)

    norm_one(c)
    for k in range(3):
        part = wm_h[k * UW : (k + 1) * UW, :].astype(F32).T
        wM[zrow(z), k * UW : (k + 1) * UW] = part.astype(BF16)
    gather_step(L_WA, wA, 1)
    ag_near(AG_X, xall)
    for m in (1, 2):
        ag_peer(AG_COT, cotall, m, cot_h.at[x_half]).start()
    for m in (1, 2):
        ag_sibling_half(AG_X, xall, m)
        norm_one(partner(c, m))
    for h in range(2, Z - 1):
        gather_step(L_WA, wA, h)
    gather_send(L_WM, wM, 1, start)
    ag_far(AG_X, xall)
    ag_sibling_half(AG_X, xall, 3)
    norm_one(partner(c, 3))

    segr[...] = segc_r[...].T[0:8, :]

    ag_near(AG_COT, cotall)
    gather_step(L_WA, wA, Z - 1)

    def project(cb, carry):
        b = block(cb)
        proj = dot(n1[b, :], wA[:, 0 : 3 * PW]).astype(BF16)
        cos, sin = cos_r[b, :], sin_r[b, :]
        qf = proj[:, 0:PW].astype(F32)
        kf = proj[:, PW : 2 * PW].astype(F32)
        q_rot = (qf * cos + swap_halves(qf) * sin).astype(BF16).astype(F32) * (HD**-0.5)
        k_rot = (kf * cos + swap_halves(kf) * sin).astype(BF16)
        val = proj[:, 2 * PW : 3 * PW]
        q_s[b, :] = q_rot.astype(BF16)
        k_s[b, :] = k_rot
        v_s[b, :] = val
        kT[:, b] = k_rot.astype(F32).T.astype(BF16)
        vT[:, b] = val.astype(F32).T.astype(BF16)
        return carry

    lax.fori_loop(0, N, project, 0)

    lane = lax.broadcasted_iota(jnp.int32, (R, PW), 1)

    def only(u, h):
        return jnp.where(lax.div(lane, HD) == h, u, jnp.zeros_like(u))

    def attend(cb):
        b = block(cb)
        same = segc_r[:, 0:1] == segr[0:1, b]
        for h in range(heads):
            s = dot(k_s[...], only(q_s[b, :], h), 1, 1)
            s = jnp.where(same, s, MASK_FILL)
            e = jnp.exp(s - jnp.max(s, axis=0, keepdims=True))
            inv = 1.0 / jnp.sum(e, axis=0, keepdims=True)
            eb = e.astype(BF16)
            eT[h, cb] = eb
            inv_r[h : h + 1, b] = inv
            hr = slice(h * HD, (h + 1) * HD)
            attnT[hr, b] = (dot(vT[hr, :], eb) * inv).astype(BF16)
        attn[b, :] = attnT[:, b].astype(F32).T.astype(BF16)

    def part_attn(cb, half):
        return dot(attn[rows(cb, half), :], wA[:, 3 * PW :], 1, 1)

    def attend_begin(m):
        attend(partner(c, m))
        rs_begin(RS_ATTN, m, part_attn)

    attend_begin(3)
    attend_begin(2)
    rs_far(RS_ATTN)
    attend_begin(1)
    gather_step(L_WM, wM, 1)
    rs_near(RS_ATTN)
    attend_begin(0)
    rs_joined(RS_ATTN)
    rs_own(RS_ATTN)
    ag_far(AG_COT, cotall)
    mixed1[...] = xall[rows(c, t), :].astype(F32) + rs_end(RS_ATTN)

    hat2, inv2 = norm_stats(mixed1[...])
    n2[rows(c, t), :] = (hat2 * gvec[1:2, :]).astype(BF16)
    for m in (1, 2):
        ag_peer(AG_N2, n2, m).start()
    ag_sib(AG_N2, n2, 0).start()
    for h in range(2, Z):
        gather_step(L_WM, wM, h)
    for m in (1, 2, 3):
        ag_sibling_half(AG_COT, cotall, m)

    def mlp(cb):
        b = block(cb)
        pair = dot(n2[b, :], wM[:, 0 : 2 * UW])
        grad_h = dot(cotall[b, :], wM[:, 2 * UW :])
        a, g = pair[:, :UW], pair[:, UW:]
        cdf = 0.5 * (1.0 + lax.erf(a * INV_ROOT_TWO))
        gelu = a * cdf
        hid[b, :] = (gelu * g).astype(BF16)
        slope = cdf + a * jnp.exp(-0.5 * a * a) * INV_ROOT_TWO_PI
        gpair[b, 0:UW] = (grad_h * g * slope).astype(BF16)
        gpair[b, UW:] = (grad_h * gelu).astype(BF16)

    def part_gn2(cb, half):
        return dot(gpair[rows(cb, half), :], wM[:, 0 : 2 * UW], 1, 1)

    def part_out(cb, half):
        return dot(hid[rows(cb, half), :], wM[:, 2 * UW :], 1, 1)

    def mlp_at(m):
        ag_sibling_half(AG_N2, n2, m)
        mlp(partner(c, m))

    mlp_at(0)
    rs_begin(RS_GN2, 0, part_gn2)
    ag_near(AG_N2, n2)
    mlp_at(1)
    rs_begin(RS_GN2, 1, part_gn2)
    rs_own(RS_GN2)
    ag_far(AG_N2, n2)
    mlp_at(3)
    rs_begin(RS_GN2, 3, part_gn2)
    mlp_at(2)
    rs_far(RS_GN2)
    rs_begin(RS_GN2, 2, part_gn2)

    def grads_down(i, carry):
        col = pl.ds(pl.multiple_of(i * CH, CH), CH)
        gDst[col, :] = dot(cotall[:, col], hid[...], 0, 0).astype(BF16)
        return carry

    lax.fori_loop(0, D // CH, grads_down, 0)
    scatter_start(L_GDOWN)
    rs_near(RS_GN2)
    rs_joined(RS_GN2)

    def grads_in(i, carry):
        col = pl.ds(pl.multiple_of(i * CH, CH), CH)
        gIst[col, :] = dot(n2[:, col], gpair[...], 0, 0).astype(BF16)
        return carry

    lax.fori_loop(0, D // CH, grads_in, 0)
    scatter_start(L_GIN)

    hat2, inv2 = norm_stats(mixed1[...])
    back2, gg_mlp = norm_back(rs_end(RS_GN2), hat2, inv2, gvec[1:2, :])
    ggst[0, 1:2, :] = gg_mlp
    gmixed[...] = cotall[rows(c, t), :].astype(F32) + back2
    gm[rows(c, t), :] = gmixed[...].astype(BF16)
    for m in (1, 2):
        ag_peer(AG_GM, gm, m).start()
    ag_sib(AG_GM, gm, 0).start()
    rs_begin(RS_OUT, 3, part_out)
    rs_begin(RS_OUT, 2, part_out)
    rs_begin(RS_OUT, 1, part_out)
    rs_begin(RS_OUT, 0, part_out)

    def fin(kind, m, own, out):
        return rcopy(own, out.at[c], f_s.at[kind, m], f_r.at[kind, m], {"ctx": partner(c, m)})

    def own_copy(kind, own, out):
        return pltpu.make_async_copy(own, out.at[c], loc.at[kind])

    def finish(kind):
        own, out = finals[kind]
        own[...] = scatter_total(kind).astype(BF16)
        for m in (1, 2):
            fin(kind, m, own, out).start()
        own_copy(kind, own, out).start()

    def fin_relay(kind):
        there = finals[kind][1].at[partner(c, via)]
        return rcopy(
            there, there, f_s.at[kind, 3], f_r.at[kind, 3], {"ctx": partner(c, onto)}
        )

    def fin_arrive(kind, m):
        there = finals[kind][1].at[partner(c, m)]
        rcopy(there, there, f_s.at[kind, m], f_r.at[kind, m], {"ctx": partner(c, onto)}).wait_recv()

    def pass_on(kind):
        fin_arrive(kind, via)
        fin_relay(kind).start()

    finals = ((gIf, gi_o), (gDf, gd_o), (gAf, ga_o))

    gk[...] = jnp.zeros_like(gk)
    gv[...] = jnp.zeros_like(gv)

    def rotate_back(g, b):
        return g * cos_r[b, :] + swap_halves(g * sin_r[b, :])

    def attend_back(cb):
        b = block(cb)
        g = dot(gm[b, :], wA[:, 3 * PW :]).astype(BF16)
        gT = g.astype(F32).T
        scaled = []
        grad_q = []
        for h in range(heads):
            hr = slice(h * HD, (h + 1) * HD)
            inv = inv_r[h : h + 1, b]
            delta = jnp.sum(gT[hr, :] * attnT[hr, b].astype(F32), axis=0, keepdims=True)
            gp = dot(v_s[...], only(g, h), 1, 1)
            ds = (eT[h, cb].astype(F32) * ((gp - delta) * inv)).astype(BF16)
            grad_q.append(dot(kT[hr, :], ds))
            gk[...] += dot(ds, only(q_s[b, :], h))
            scaled.append(gT[hr, :] * inv)
        gs = jnp.concatenate(scaled, axis=0).T.astype(BF16)
        for h in range(heads):
            gv[...] += dot(eT[h, cb], only(gs, h))
        gq = jnp.concatenate(grad_q, axis=0).T * (HD**-0.5)
        gproj[b, 0:PW] = rotate_back(gq, b).astype(BF16)

    for m in (0, 1, 2, 3):
        if m == 0:
            ag_near(AG_GM, gm)
        if m == 2:
            ag_far(AG_GM, gm)
        ag_sibling_half(AG_GM, gm, m)
        attend_back(partner(c, m))
        if m == 1:
            rs_far(RS_OUT)
            rs_near(RS_OUT)
    rs_joined(RS_OUT)
    rs_own(RS_OUT)

    def unrotate(cb, carry):
        b = block(cb)
        gproj[b, PW : 2 * PW] = rotate_back(gk[b, :], b).astype(BF16)
        gproj[b, 2 * PW :] = gv[b, :].astype(BF16)
        return carry

    lax.fori_loop(0, N, unrotate, 0)

    def grads_attn(i, carry):
        col = pl.ds(pl.multiple_of(i * CH, CH), CH)
        gAst[col, 0 : 3 * PW] = dot(n1[:, col], gproj[...], 0, 0).astype(BF16)
        gAst[col, 3 * PW :] = dot(gm[:, col], attn[...], 0, 0).astype(BF16)
        return carry

    lax.fori_loop(0, D // CH, grads_attn, 0)
    scatter_start(L_GWA)
    finish(L_GDOWN)

    def part_gn1(cb, half):
        return dot(gproj[rows(cb, half), :], wA[:, 0 : 3 * PW], 1, 1)

    rs_begin(RS_GN1, 3, part_gn1)
    rs_begin(RS_GN1, 2, part_gn1)
    rs_far(RS_GN1)
    pass_on(L_GDOWN)
    rs_begin(RS_GN1, 1, part_gn1)
    rs_near(RS_GN1)
    rs_begin(RS_GN1, 0, part_gn1)
    finish(L_GIN)
    rs_joined(RS_GN1)
    rs_own(RS_GN1)


    hat1, inv1 = norm_stats(xall[rows(c, t), :].astype(F32))
    back1, gg_attn = norm_back(rs_end(RS_GN1), hat1, inv1, gvec[0:1, :])
    ggst[0, 0:1, :] = gg_attn
    gtok_o[x_half, :] = gmixed[...] + back1
    swap_tok = rcopy(
        gtok_o.at[x_half], gtok_o.at[x_half], sw_s.at[0], sw_r.at[0], {"tensor": o}
    )
    swap_tok.start()

    ggst[0, 2:8, :] = jnp.zeros_like(ggst[0, 2:8, :])
    gg0 = rcopy(ggst.at[0], ggrv.at[0], gg_s.at[0], gg_r.at[0], {"tensor": o})
    gg0.start()

    out_o[x_half, :] = (mixed1[...] + rs_end(RS_OUT)).astype(BF16)
    swap_out = rcopy(
        out_o.at[x_half], out_o.at[x_half], sw_s.at[1], sw_r.at[1], {"tensor": o}
    )
    swap_out.start()
    gg0.wait_recv()
    ggst[1] = ggst[0] + ggrv[0]

    def gg_ctx(m):
        return rcopy(ggst.at[1], ggrv.at[m], gg_s.at[m], gg_r.at[m], {"ctx": partner(c, m)})

    for m in (1, 2, 3):
        gg_ctx(m).start()

    for m in (1, 2, 3):
        gg_ctx(m).wait_recv()
    ggst[2] = (ggst[1] + ggrv[1]) + (ggrv[2] + ggrv[3])

    def gg_z(d):
        return z_copy(Z_GG, d, ggst.at[2], ggrv.at[3 + d])

    for d in range(1, Z):
        gg_z(d).start()
    pass_on(L_GIN)
    finish(L_GWA)
    total = ggst[2]
    for d in range(1, Z):
        z_recv(Z_GG, d, ggrv.at[3 + d])
        total = total + ggrv[3 + d]
    gain_o[...] = total
    pass_on(L_GWA)

    other = pl.ds(pl.multiple_of(o * H, H), H)
    rcopy(gtok_o.at[other], gtok_o.at[other], sw_s.at[0], sw_r.at[0], {"tensor": o}).wait_recv()
    rcopy(out_o.at[other], out_o.at[other], sw_s.at[1], sw_r.at[1], {"tensor": o}).wait_recv()
    for kind, (own, out) in enumerate(finals):
        fin_arrive(kind, onto)
        fin_arrive(kind, 3)
        fin_relay(kind).wait_send()
        for m in (1, 2):
            fin(kind, m, own, out).wait_send()
    for m in (1, 2, 3):
        gg_ctx(m).wait_send()
    for kind, (own, out) in enumerate(finals):
        own_copy(kind, own, out).wait()
    gg0.wait_send()
    swap_tok.wait_send()
    swap_out.wait_send()
    for m in (1, 2):
        ag_peer(AG_X, xall, m, x_h.at[x_half]).wait_send()
        ag_peer(AG_COT, cotall, m, cot_h.at[x_half]).wait_send()
        ag_peer(AG_N2, n2, m).wait_send()
        ag_peer(AG_GM, gm, m).wait_send()
    for kind, buf in ((AG_X, xall), (AG_COT, cotall), (AG_N2, n2), (AG_GM, gm)):
        ag_relay(kind, buf).wait_send()
    for m in (1, 2, 3):
        for kind in range(4):
            rs_peer(kind, m, onto).wait_send()
        ag_sib(AG_X, xall, m).wait_send()
        ag_sib(AG_COT, cotall, m).wait_send()
    for m in range(4):
        ag_sib(AG_N2, n2, m).wait_send()
        ag_sib(AG_GM, gm, m).wait_send()
        for kind in range(4):
            rs_sib(kind, m).wait_send()
    for d in range(1, Z):
        z_gain(d).wait_send()
        gg_z(d).wait_send()
        gather_send(L_WA, wA, d, sent)
        gather_send(L_WM, wM, d, sent)
        for kind in (L_GIN, L_GDOWN, L_GWA):
            scatter_copy(kind, d).wait_send()


def spread_kernel(ga, gi, gd, tok_i, gtok_i, qkv_o, out_o, in_o, down_o, tok_o, gtok_o):
    width, units = out_o.shape[0], down_o.shape[0]
    for k in range(3):
        qkv_o[k] = ga[:, k * width : (k + 1) * width].astype(F32)
    out_o[...] = ga[:, 3 * width :].astype(F32).T
    for k in range(2):
        in_o[k] = gi[:, k * units : (k + 1) * units].astype(F32).T
    down_o[...] = gd[...].astype(F32).T
    tok_o[...] = tok_i[...]
    gtok_o[...] = gtok_i[...]


def tables(doc_len, span_len):
    count = doc_len.shape[0]
    upto = jnp.arange(count)[:, None] >= jnp.arange(count)[None, :]
    doc_end = jnp.sum(jnp.where(upto, doc_len[None, :], 0), axis=1)
    doc_start = doc_end - doc_len
    places = jnp.arange(span_len, dtype=jnp.int32)
    begins = jnp.max(
        jnp.where(places[:, None] >= doc_start[None, :], doc_start[None, :], 0), axis=1
    )
    segment = jnp.sum((places[:, None] >= doc_end[None, :]).astype(jnp.int32), axis=1)
    offset = (places - begins).astype(F32)
    half = HD // 2
    place = jnp.arange(LANES, dtype=jnp.int32)
    frequency = ROPE_BASE ** (-((place % half).astype(F32) * (2.0 / HD)))
    turn = jnp.where(place % HD < half, -1.0, 1.0)
    angles = offset[:, None] * frequency[None, :]
    seg = jnp.broadcast_to(segment.astype(F32)[:, None], (span_len, LANES))
    return jnp.cos(angles), jnp.sin(angles) * turn[None, :], seg


def local(ways, tokens, doc_lengths, gain_attn, w_qkv, w_attn_out, gain_mlp, w_in, w_mlp_out, cotangent):
    Z, N = ways
    ci, zi = lax.axis_index("ctx"), lax.axis_index("dp")
    R, D = tokens.shape
    S = R * N
    H = R // 2
    Dz, width = w_qkv.shape[1:]
    units = w_in.shape[2]
    PW = width // N
    UW = -(-units // (N * LANES)) * LANES
    padded = UW * N

    qkv = lax.dynamic_slice_in_dim(w_qkv, ci * PW, PW, 2)
    w_out = lax.dynamic_slice_in_dim(w_attn_out, ci * PW, PW, 0).T
    wa = jnp.concatenate([qkv[0], qkv[1], qkv[2], w_out], axis=1)
    w_up = jnp.pad(w_in.transpose(0, 2, 1), ((0, 0), (0, padded - units), (0, 0)))
    w_up = lax.dynamic_slice_in_dim(w_up, ci * UW, UW, 1)
    w_down = jnp.pad(w_mlp_out, ((0, padded - units), (0, 0)))
    w_down = lax.dynamic_slice_in_dim(w_down, ci * UW, UW, 0)
    wm = jnp.concatenate([w_up[0], w_up[1], w_down], axis=0)
    gains = lax.dynamic_update_slice(
        jnp.zeros((16, D), BF16), jnp.stack([gain_attn, gain_mlp]), (0, zi * Dz)
    )
    cos, sin, seg = tables(doc_lengths[0], S)

    anywhere = pl.BlockSpec(memory_space=pl.ANY)
    vmem = pl.BlockSpec(memory_space=pltpu.VMEM)
    V = pltpu.VMEM
    dma = pltpu.SemaphoreType.DMA
    scratch = [
        V((S, D), BF16), V((S, D), BF16), V((S, D), BF16), V((S, D), BF16), V((S, D), BF16),
        V((Z, 16, D), BF16), V((D, 4 * PW), BF16), V((D, 3 * UW), BF16),
        V((S, PW), BF16), V((S, PW), BF16), V((S, PW), BF16), V((PW, S), BF16), V((PW, S), BF16),
        V((S, PW), BF16), V((PW, S), BF16), V((PW // HD, N, S, R), BF16), V((8, S), F32),
        V((2, N, H, D), F32), V((4, N, H, D), BF16), V((4, N, H, D), BF16), V((4, N - 1, H, D), BF16),
        V((4, N - 1, H, D), BF16), V((S, UW), BF16), V((S, 2 * UW), BF16),
        V((D, 2 * UW), BF16), V((Z, Dz, 2 * UW), BF16), V((D, UW), BF16), V((Z, Dz, UW), BF16),
        V((D, 4 * PW), BF16), V((Z, Dz, 4 * PW), BF16),
        V((Dz, 2 * UW), BF16), V((Dz, UW), BF16), V((Dz, 4 * PW), BF16),
        V((H, D), F32), V((H, D), F32), V((S, 3 * PW), BF16), V((S, PW), F32), V((S, PW), F32),
        V((8, D), F32), V((3, 8, D), F32), V((3 + Z, 8, D), F32), V((8, S), F32),
        dma((4, N)), dma((4, N)), dma((4, N)), dma((4, N)), dma((4, N)), dma((4, N)), dma((4, N)),
        dma((4, N)), dma((2, Z)), dma((2, Z)), dma((5, 2, Z)), dma((5, 2, Z)), dma((3, N)), dma((3, N)), dma((2,)), dma((2,)),
        dma((N,)), dma((N,)), dma((5,)),
    ]
    out, gtok, ga, gi, gd, gg = pl.pallas_call(
        functools.partial(layer_kernel, ways),
        out_shape=[
            jax.ShapeDtypeStruct((R, D), BF16),
            jax.ShapeDtypeStruct((R, D), F32),
            jax.ShapeDtypeStruct((N, Dz, 4 * PW), BF16),
            jax.ShapeDtypeStruct((N, Dz, 2 * UW), BF16),
            jax.ShapeDtypeStruct((N, Dz, UW), BF16),
            jax.ShapeDtypeStruct((8, D), F32),
        ],
        in_specs=[anywhere] * 3 + [vmem, anywhere] + [vmem] * 3,
        out_specs=[vmem, vmem, anywhere, anywhere, anywhere, vmem],
        scratch_shapes=scratch,
        compiler_params=pltpu.CompilerParams(
            collective_id=0, has_side_effects=True, vmem_limit_bytes=60 * 1024 * 1024
        ),
        cost_estimate=pl.CostEstimate(
            flops=12 * 10**9, bytes_accessed=12 * 2**20, transcendentals=4 * 10**6
        ),
        name="layer",
    )(tokens, cotangent, wa, wm, gains, cos, sin, seg)

    gains_own = lax.dynamic_slice_in_dim(gg[0:2], zi * Dz, Dz, 1)
    g_qkv, g_out, g_in, g_down, out, gtok = pl.pallas_call(
        spread_kernel,
        grid=(N,),
        out_shape=[
            jax.ShapeDtypeStruct((3, Dz, N * PW), F32),
            jax.ShapeDtypeStruct((N * PW, Dz), F32),
            jax.ShapeDtypeStruct((2, units, Dz), F32),
            jax.ShapeDtypeStruct((units, Dz), F32),
            jax.ShapeDtypeStruct((R, D), BF16),
            jax.ShapeDtypeStruct((R, D), F32),
        ],
        in_specs=[
            pl.BlockSpec((None, Dz, 4 * PW), lambda i: (i, 0, 0)),
            pl.BlockSpec((None, Dz, 2 * UW), lambda i: (i, 0, 0)),
            pl.BlockSpec((None, Dz, UW), lambda i: (i, 0, 0)),
            pl.BlockSpec((R // N, D), lambda i: (i, 0)),
            pl.BlockSpec((R // N, D), lambda i: (i, 0)),
        ],
        out_specs=[
            pl.BlockSpec((3, Dz, PW), lambda i: (0, 0, i)),
            pl.BlockSpec((PW, Dz), lambda i: (i, 0)),
            pl.BlockSpec((2, UW, Dz), lambda i: (0, i, 0)),
            pl.BlockSpec((UW, Dz), lambda i: (i, 0)),
            pl.BlockSpec((R // N, D), lambda i: (i, 0)),
            pl.BlockSpec((R // N, D), lambda i: (i, 0)),
        ],
        compiler_params=pltpu.CompilerParams(vmem_limit_bytes=60 * 1024 * 1024),
        name="spread",
    )(ga, gi, gd, out, gtok)
    g_in = g_in.transpose(0, 2, 1)
    return (out, gtok, gains_own[0], g_qkv, g_out, gains_own[1], g_in, g_down)


def solution(mesh):
    in_specs = (
        P(("dp", "ctx"), None),
        P("dp", None),
        P("dp"),
        P(None, "dp", "tensor"),
        P("tensor", "dp"),
        P("dp"),
        P(None, "dp", "tensor"),
        P("tensor", "dp"),
        P(("dp", "ctx"), None),
    )
    out_specs = (
        P(("dp", "ctx"), None),
        P(("dp", "ctx"), None),
        P("dp"),
        P(None, "dp", "tensor"),
        P("tensor", "dp"),
        P("dp"),
        P(None, "dp", "tensor"),
        P("tensor", "dp"),
    )
    ways = (mesh.shape["dp"], mesh.shape["ctx"])
    return jax.shard_map(
        functools.partial(local, ways),
        mesh=mesh,
        in_specs=in_specs,
        out_specs=out_specs,
        check_vma=False,
    )
```
